32 devices in a mesh: fsdp: 4 (over z), ctx: 4 (over x, core), tp: 2 (over y).
Axes of the slice: x: 2, y: 2, z: 4, core: 2. Of those that a mesh axis runs over, the one named last changes fastest.
Arguments:
- tokens: bfloat16 [8, 2048, 1024], P('fsdp', 'ctx', 'tp'), may hold values from -6 to 6
- cotangent: bfloat16 [8, 2048, 1024], P('fsdp', 'ctx', 'tp'), may hold values from -6 to 6
- w_query: bfloat16 [1024, 1024], P('fsdp', 'tp'), may hold values from -0.1875 to 0.1875
- w_key: bfloat16 [1024, 1024], P('fsdp', 'tp'), may hold values from -0.1875 to 0.1875
- w_value: bfloat16 [1024, 1024], P('fsdp', 'tp'), may hold values from -0.1875 to 0.1875
- w_out: bfloat16 [1024, 1024], P('tp', 'fsdp'), may hold values from -4 to 4
- w_state_key: bfloat16 [1024, 1024], P('fsdp', 'tp'), may hold values from -0.1875 to 0.1875
- w_state_value: bfloat16 [1024, 1024], P('fsdp', 'tp'), may hold values from -0.1875 to 0.1875
- w_state_query: bfloat16 [1024, 1024], P('fsdp'), may hold values from -0.1875 to 0.1875
- w_state_out: bfloat16 [1024, 1024], P(None, 'fsdp'), may hold values from -4 to 4
- w_up: bfloat16 [1024, 4096], P('fsdp', 'tp'), may hold values from -0.1875 to 0.1875
- w_down: bfloat16 [4096, 1024], P('tp', 'fsdp'), may hold values from -0.09375 to 0.09375
- gain_attn: float32 [1024], P('tp'), may hold values from 0.5 to 1.5
- gain_state: float32 [1024], replicated, may hold values from 0.5 to 1.5
- gain_mlp: float32 [1024], P('tp'), may hold values from 0.5 to 1.5
- forget_logit: float32 [1024], replicated, may hold values from -1 to 3
- state_init: bfloat16 [512, 1024], replicated, may hold values from -6 to 6
Outputs:
- out: bfloat16 [8, 2048, 1024], P('fsdp', 'ctx', 'tp')
- grad_tokens: bfloat16 [8, 2048, 1024], P('fsdp', 'ctx', 'tp')
- grad_w_query: float32 [1024, 1024], P('fsdp', 'tp')
- grad_w_key: float32 [1024, 1024], P('fsdp', 'tp')
- grad_w_value: float32 [1024, 1024], P('fsdp', 'tp')
- grad_w_out: float32 [1024, 1024], P('tp', 'fsdp')
- grad_w_state_key: float32 [1024, 1024], P('fsdp', 'tp')
- grad_w_state_value: float32 [1024, 1024], P('fsdp', 'tp')
- grad_w_state_query: float32 [1024, 1024], P('fsdp')
- grad_w_state_out: float32 [1024, 1024], P(None, 'fsdp')
- grad_w_up: float32 [1024, 4096], P('fsdp', 'tp')
- grad_w_down: float32 [4096, 1024], P('tp', 'fsdp')
- grad_gain_attn: float32 [1024], P('tp')
- grad_gain_state: float32 [1024], replicated
- grad_gain_mlp: float32 [1024], P('tp')
- grad_forget: float32 [1024], replicated
- grad_state_init: float32 [512, 1024], replicated
The draws below stay inside these ranges and needn't reach their ends.
All inputs are finite; a program needn't handle non-finite values.
Results may differ from the reference program's by a relative error of at most 0.025.
Values may be sent and summed in bfloat16 or wider, within the bound.
A program may use at most 384 MiB of HBM per device.

```python
from functools import partial
import jax
import jax.numpy as jnp
from jax import lax

D = 1024
HEADS = 8
HEAD = 128
FF = 4096
NSTATE = 512
BLOCK = 512
SEQS = 8
SEQ_LEN = 2048
N_CTX = 4


def level_of(key, dims, split, least, high):
    def one(axis_at, shards_of):
        draws = jax.random.uniform(jax.random.fold_in(jax.random.fold_in(key, 6), axis_at), (shards_of,), jnp.float32, least / len(split), high / len(split))
        return jnp.repeat(jnp.exp(draws), dims[axis_at] // shards_of).reshape((-1,) + (1,) * (len(dims) - axis_at - 1))

    factor_of = one(*split[0])
    for cut in split[1:]:
        factor_of = factor_of * one(*cut)
    return factor_of


def bell_draw(own_key, dims, spread, limit, cuts=(), kind=jnp.bfloat16):
    drawn = spread * jax.random.normal(own_key, dims, jnp.float32)
    if cuts:
        drawn = drawn * level_of(own_key, dims, cuts, -0.22, 0.18)
    return jnp.clip(drawn, -limit, limit).astype(kind)


def setup_inputs(seed: int = 0) -> dict:
    key_of = jax.random.split(jax.random.key(seed), 18)
    tokens = bell_draw(key_of[0], (SEQS, SEQ_LEN, D), 1.0, 6.0, ((0, 4), (1, 4), (2, 2)))
    cotangent = bell_draw(key_of[1], (SEQS, SEQ_LEN, D), 1.0, 6.0, ((0, 4), (1, 4), (2, 2)))
    w_query = bell_draw(key_of[2], (D, HEADS * HEAD), D ** -0.5, 0.1875, ((0, 4), (1, 2)))
    w_key = bell_draw(key_of[3], (D, HEADS * HEAD), D ** -0.5, 0.1875, ((0, 4), (1, 2)))
    w_value = bell_draw(key_of[4], (D, HEADS * HEAD), D ** -0.5, 0.1875, ((0, 4), (1, 2)))
    w_out = bell_draw(key_of[5], (HEADS * HEAD, D), 2 ** -0.5, 4.0, ((0, 2), (1, 4)))
    w_state_key = bell_draw(key_of[6], (D, HEADS * HEAD), D ** -0.5, 0.1875, ((0, 4), (1, 2)))
    w_state_value = bell_draw(key_of[7], (D, HEADS * HEAD), D ** -0.5, 0.1875, ((0, 4), (1, 2)))
    w_state_query = bell_draw(key_of[8], (D, HEADS * HEAD), D ** -0.5, 0.1875, ((0, 4),))
    w_state_out = bell_draw(key_of[9], (HEADS * HEAD, D), 2 ** -0.5, 4.0, ((1, 4),))
    w_up = bell_draw(key_of[10], (D, FF), D ** -0.5, 0.1875, ((0, 4), (1, 2)))
    w_down = bell_draw(key_of[11], (FF, D), FF ** -0.5, 0.09375, ((0, 2), (1, 4)))
    gain_attn = jnp.clip(1.0 + 0.1 * jax.random.normal(key_of[12], (D,), jnp.float32), 0.5, 1.5)
    gain_state = jnp.clip(1.0 + 0.1 * jax.random.normal(key_of[13], (D,), jnp.float32), 0.5, 1.5)
    gain_mlp = jnp.clip(1.0 + 0.1 * jax.random.normal(key_of[14], (D,), jnp.float32), 0.5, 1.5)
    forget_logit = jnp.clip(jax.random.uniform(key_of[15], (D,), jnp.float32, -1.0, 3.0), -1.0, 3.0)
    state_init = bell_draw(key_of[16], (NSTATE, D), 1.0, 6.0)
    return {"tokens": tokens, "cotangent": cotangent, "w_query": w_query, "w_key": w_key, "w_value": w_value, "w_out": w_out, "w_state_key": w_state_key, "w_state_value": w_state_value, "w_state_query": w_state_query, "w_state_out": w_state_out, "w_up": w_up, "w_down": w_down, "gain_attn": gain_attn, "gain_state": gain_state, "gain_mlp": gain_mlp, "forget_logit": forget_logit, "state_init": state_init}


@jax.custom_vjp
def low(v):
    return lax.optimization_barrier(v.astype(jnp.bfloat16)).astype(jnp.float32)

@jax.custom_vjp
def low_back(v):
    return v

def low_keep(v):
    return (low(v), None)

def low_pass(kept, grad):
    return (grad,)

def back_keep(v):
    return (v, None)

def back_low(kept, grad):
    return (low(grad),)
low.defvjp(low_keep, low_pass)
low_back.defvjp(back_keep, back_low)
epsilon = 1e-06
masked_score = -1e+30
highest = lax.Precision.HIGHEST

def matmul(left, right):
    return jnp.dot(left, right, precision=highest, preferred_element_type=jnp.float32)

def rms_norm(vector, scales):
    return vector * lax.rsqrt(lax.optimization_barrier(jnp.mean(vector * vector, axis=-1, keepdims=True)) + epsilon) * scales

def attend(queries, key_rows, value_rows, allowed):
    row_count = queries.shape[0]
    query_heads = queries.reshape(row_count, HEADS, HEAD)
    key_heads = key_rows.reshape(key_rows.shape[0], HEADS, HEAD)
    value_heads = value_rows.reshape(value_rows.shape[0], HEADS, HEAD)
    scores = jnp.einsum('qhd,khd->hqk', query_heads, key_heads, precision=highest) * HEAD ** (-0.5)
    scores = low_back(scores)
    scores = jnp.where(allowed[None], scores, masked_score)
    weights = low(jax.nn.softmax(scores, axis=-1))
    blended = jnp.einsum('hqk,khd->qhd', weights, value_heads, precision=highest)
    return blended.reshape(row_count, HEADS * HEAD)

def block_forward(params, carry, inputs):
    memory, earlier_keys, earlier_values = carry
    block_tokens, index = inputs
    w_query, w_key, w_value, w_out, w_state_key, w_state_value, w_state_query, w_state_out, w_up, w_down, gain_attn, gain_state, gain_mlp, forget_logit = params
    hidden = low(rms_norm(block_tokens, gain_attn))
    queries = low(low_back(matmul(hidden, w_query)))
    keys_now = low(low_back(matmul(hidden, w_key)))
    values_now = low(low_back(matmul(hidden, w_value)))
    memory_reduced_precision = low(rms_norm(memory, gain_state))
    memory_key_rows = low(low_back(matmul(memory_reduced_precision, w_state_key)))
    memory_values = low(low_back(matmul(memory_reduced_precision, w_state_value)))
    positions = jnp.arange(BLOCK)
    causal = positions[None, :] <= positions[:, None]
    earlier = jnp.broadcast_to(index > 0, (BLOCK, BLOCK))
    allowed = jnp.concatenate([earlier, causal, jnp.ones((BLOCK, NSTATE), jnp.bool_)], axis=1)
    key_rows = jnp.concatenate([earlier_keys, keys_now, memory_key_rows], axis=0)
    value_rows = jnp.concatenate([earlier_values, values_now, memory_values], axis=0)
    attention = low(low_back(attend(queries, key_rows, value_rows, allowed)))
    residual = block_tokens + low_back(matmul(attention, w_out))
    mlp_input = low(rms_norm(residual, gain_mlp))
    pre_act = low_back(matmul(mlp_input, w_up))
    activation = low(jax.nn.gelu(pre_act, approximate=True))
    output = residual + low_back(matmul(activation, w_down))
    memory_queries = low(low_back(matmul(memory_reduced_precision, w_state_query)))
    read_out = low(low_back(attend(memory_queries, keys_now, values_now, jnp.ones((NSTATE, BLOCK), jnp.bool_))))
    update = low_back(matmul(read_out, w_state_out))
    keep_rate = jax.nn.sigmoid(forget_logit)
    next_memory = keep_rate * memory + (1.0 - keep_rate) * update
    return ((next_memory, keys_now, values_now), output)

def sequence_forward(params, memory_start, sequence):
    blocks = sequence.reshape(N_CTX, BLOCK, D)
    empty = jnp.zeros((BLOCK, HEADS * HEAD), jnp.float32)
    stepper = jax.checkpoint(partial(block_forward, params))
    indices = jnp.arange(N_CTX, dtype=jnp.int32)
    final, outputs = lax.scan(stepper, (memory_start, empty, empty), (blocks, indices))
    return outputs.reshape(SEQ_LEN, D)

def whole_layer(tokens32, params, memory_start):

    def per_sequence(carry, sequence):
        return (carry, sequence_forward(params, memory_start, sequence))
    ignored, outputs = lax.scan(jax.checkpoint(per_sequence), jnp.zeros((), jnp.float32), tokens32)
    return outputs

def reference(tokens, cotangent, w_query, w_key, w_value, w_out, w_state_key, w_state_value, w_state_query, w_state_out, w_up, w_down, gain_attn, gain_state, gain_mlp, forget_logit, state_init):
    params = tuple((item.astype(jnp.float32) for item in (w_query, w_key, w_value, w_out, w_state_key, w_state_value, w_state_query, w_state_out, w_up, w_down, gain_attn, gain_state, gain_mlp, forget_logit)))
    tokens32 = tokens.astype(jnp.float32)
    memory_start = state_init.astype(jnp.float32)
    output, pullback = jax.vjp(whole_layer, tokens32, params, memory_start)
    grad_input, grad_params, grad_memory = pullback(cotangent.astype(jnp.float32))
    return (output.astype(jnp.bfloat16), grad_input.astype(jnp.bfloat16), grad_params[0], grad_params[1], grad_params[2], grad_params[3], grad_params[4], grad_params[5], grad_params[6], grad_params[7], grad_params[8], grad_params[9], grad_params[10], grad_params[11], grad_params[12], grad_params[13], grad_memory)
```

```python
import functools

import jax
import jax.numpy as jnp
from jax import lax
from jax.experimental import pallas as pl
from jax.experimental.pallas import tpu as pltpu
from jax.sharding import PartitionSpec as P

MESH = pl.DeviceIdType.MESH
ANY = pl.BlockSpec(memory_space=pl.ANY)
GROUPS=((0,2),(2,2),(4,4),(8,4),(12,4))

def where_am_i():
    f=lax.axis_index("fsdp"); c=lax.axis_index("ctx"); t=lax.axis_index("tp")
    return f, lax.div(c,2), lax.rem(c,2), t

class Gather:
    def __init__(self, L, G, F, zs, zr, ys, yr, xs, xr, ks, kr):
        self.L, self.G, self.F = L, G, F
        self.sems=(zs,zr,ys,yr,xs,xr,ks,kr)
        self.z,self.x,self.k,self.y=where_am_i()
        self.half=L.shape[-1]
    def src_z(self,d): return lax.rem(self.z+d+1,self.F)
    def cols(self,t): return pl.ds(pl.multiple_of(t*self.half,self.half),self.half)
    def zcopy(self,g,d):
        zs,zr=self.sems[0:2]; w,n=GROUPS[g]
        to=lax.rem(self.z-(d+1)+self.F,self.F)
        return pltpu.make_async_remote_copy(
            src_ref=self.L.at[pl.ds(w,n),self.x,self.k],
            dst_ref=self.G.at[pl.ds(w,n),self.z,self.x,self.k,:,self.cols(self.y)],
            send_sem=zs.at[g,d],recv_sem=zr.at[g,d],
            device_id=(to,self.x*2+self.k,self.y),device_id_type=MESH)
    def zland(self,g,d):
        zs,zr=self.sems[0:2]; w,n=GROUPS[g]
        r=self.G.at[pl.ds(w,n),self.src_z(d),self.x,self.k,:,self.cols(self.y)]
        return pltpu.make_async_copy(r,r,zr.at[g,d])
    def ycopy(self,g,d):
        ys,yr=self.sems[2:4]; w,n=GROUPS[g]
        dev=(self.z,self.x*2+self.k,1-self.y)
        if d==self.F-1:
            return pltpu.make_async_remote_copy(
                src_ref=self.L.at[pl.ds(w,n),:,self.k],
                dst_ref=self.G.at[pl.ds(w,n),self.z,:,self.k,:,self.cols(self.y)],
                send_sem=ys.at[g,d],recv_sem=yr.at[g,d],device_id=dev,device_id_type=MESH)
        r=self.G.at[pl.ds(w,n),self.src_z(d),self.x,self.k,:,self.cols(self.y)]
        return pltpu.make_async_remote_copy(src_ref=r,dst_ref=r,send_sem=ys.at[g,d],recv_sem=yr.at[g,d],device_id=dev,device_id_type=MESH)
    def yland(self,g,d):
        yr=self.sems[3]; w,n=GROUPS[g]
        o=self.cols(1-self.y)
        if d==self.F-1: r=self.G.at[pl.ds(w,n),self.z,:,self.k,:,o]
        else: r=self.G.at[pl.ds(w,n),self.src_z(d),self.x,self.k,:,o]
        return pltpu.make_async_copy(r,r,yr.at[g,d])
    def xcopy(self,g,d):
        xs,xr=self.sems[4:6]; w,n=GROUPS[g]
        r=self.G.at[pl.ds(w,n),self.src_z(d),self.x,self.k]
        return pltpu.make_async_remote_copy(src_ref=r,dst_ref=r,send_sem=xs.at[g,d],recv_sem=xr.at[g,d],device_id=(self.z,(1-self.x)*2+self.k,self.y),device_id_type=MESH)
    def xland(self,g,d):
        xr=self.sems[5]; w,n=GROUPS[g]
        r=self.G.at[pl.ds(w,n),self.src_z(d),1-self.x,self.k]
        return pltpu.make_async_copy(r,r,xr.at[g,d])
    def kcopy(self,g,d):
        ks,kr=self.sems[6:8]; w,n=GROUPS[g]
        dev=(self.z,self.x*2+1-self.k,self.y)
        if d==self.F-1: r=self.G.at[pl.ds(w,n),self.z,:,self.k,:,self.cols(1-self.y)]
        else: r=self.G.at[pl.ds(w,n),self.src_z(d),:,self.k]
        return pltpu.make_async_remote_copy(src_ref=r,dst_ref=r,send_sem=ks.at[g,d],recv_sem=kr.at[g,d],device_id=dev,device_id_type=MESH)
    def kland(self,g,d):
        kr=self.sems[7]; w,n=GROUPS[g]
        if d==self.F-1: r=self.G.at[pl.ds(w,n),self.z,:,1-self.k,:,self.cols(1-self.y)]
        else: r=self.G.at[pl.ds(w,n),self.src_z(d),:,1-self.k]
        return pltpu.make_async_copy(r,r,kr.at[g,d])
    def send_z(self,g):
        for d in range(self.F-1): self.zcopy(g,d).start()
        self.ycopy(g,self.F-1).start()
    def stage_y(self,g):
        for d in range(self.F-1):
            self.zland(g,d).wait(); self.ycopy(g,d).start()
    def stage_x(self,g):
        for d in range(self.F-1):
            self.yland(g,d).wait(); self.xcopy(g,d).start()
        self.yland(g,self.F-1).wait(); self.kcopy(g,self.F-1).start()
    def stage_k(self,g):
        for d in range(self.F-1):
            self.xland(g,d).wait(); self.kcopy(g,d).start()
    def stage_done(self,g):
        for d in range(self.F): self.kland(g,d).wait()
    def drain(self,g):
        for d in range(self.F):
            if d<self.F-1: self.zcopy(g,d).wait_send(); self.xcopy(g,d).wait_send()
            self.ycopy(g,d).wait_send(); self.kcopy(g,d).wait_send()

def barrier_with(F):
    z,x,k,y=where_am_i()
    bar=pltpu.get_barrier_semaphore()
    peers=[(lax.rem(z+d+1,F),x*2+k,y) for d in range(F-1)]
    peers+=[(z,x*2+k,1-y),(z,(1-x)*2+k,y),(z,x*2+1-k,y)]
    for p in peers: pl.semaphore_signal(bar,inc=1,device_id=p,device_id_type=MESH)
    pl.semaphore_wait(bar,len(peers))

def gather_kernel(F,L,T,C,N,G,X,Co,Nn,zs,zr,ys,yr,xs,xr,ks,kr,ls,ss,sr):
    z,x,k,y=where_am_i()
    g=Gather(L,G,F,zs,zr,ys,yr,xs,xr,ks,kr)
    own=[pltpu.make_async_copy(L,G.at[:,z,:,:,:,g.cols(y)],ls.at[0]),
         pltpu.make_async_copy(T.at[y],X.at[:,g.cols(y)],ls.at[1]),
         pltpu.make_async_copy(C.at[y],Co.at[:,g.cols(y)],ls.at[2]),
         pltpu.make_async_copy(N,Nn.at[:,g.cols(y)],ls.at[3])]
    for o in own: o.start()
    barrier_with(F)
    dev=(z,x*2+k,1-y)
    swaps=[pltpu.make_async_remote_copy(src_ref=T.at[1-y],dst_ref=X.at[:,g.cols(y)],send_sem=ss.at[0],recv_sem=sr.at[0],device_id=dev,device_id_type=MESH),
      pltpu.make_async_remote_copy(src_ref=N,dst_ref=Nn.at[:,g.cols(y)],send_sem=ss.at[1],recv_sem=sr.at[1],device_id=dev,device_id_type=MESH),
      pltpu.make_async_remote_copy(src_ref=C.at[1-y],dst_ref=Co.at[:,g.cols(y)],send_sem=ss.at[2],recv_sem=sr.at[2],device_id=dev,device_id_type=MESH)]
    swaps[0].start(); swaps[1].start()
    n=len(GROUPS)
    g.send_z(0)
    for i in range(n+3):
        if i+1<n: g.send_z(i+1)
        if i<n: g.stage_y(i)
        if i==n-1: swaps[2].start()
        if 0<=i-1<n: g.stage_x(i-1)
        if 0<=i-2<n: g.stage_k(i-2)
        if 0<=i-3<n: g.stage_done(i-3)
    for i in range(n): g.drain(i)
    for s in swaps: s.wait()
    for o in own: o.wait()

def gather_call(F,L,T,C,N):
    n=len(GROUPS)
    D=pltpu.SemaphoreType.DMA
    W,_,_,rows,half=L.shape
    return pl.pallas_call(functools.partial(gather_kernel,F),
        out_shape=(jax.ShapeDtypeStruct((W,F,2,2,rows,2*half),L.dtype),
                   jax.ShapeDtypeStruct((T.shape[1],2*T.shape[2]),T.dtype),
                   jax.ShapeDtypeStruct((T.shape[1],2*T.shape[2]),T.dtype),
                   jax.ShapeDtypeStruct((N.shape[0],2*N.shape[1]),N.dtype)),
        in_specs=[ANY]*4,out_specs=[ANY]*4,
        scratch_shapes=[D((n,F-1)),D((n,F-1)),D((n,F)),D((n,F)),D((n,F-1)),D((n,F-1)),D((n,F)),D((n,F)),D((4,)),D((3,)),D((3,))],
        compiler_params=pltpu.CompilerParams(collective_id=1,has_side_effects=True),name="gather")(L,T,C,N)


def add_into(dst, src, lead):
    total=1
    for n in lead: total*=n
    def body(i,_):
        idx=[]; r=i
        for n in reversed(lead):
            idx.append(lax.rem(r,n)); r=lax.div(r,n)
        idx=tuple(reversed(idx))
        dst[idx]=(dst[idx].astype(jnp.float32)+src[idx].astype(jnp.float32)).astype(dst.dtype)
        return 0
    lax.fori_loop(0,total,body,0)

def reduce_kernel(F,W,flags,D,R,RX,A,KB,B1,B2,ZB,ld,ks,kr,s1,r1,s2,r2,zs,zr,bs,br,fs,fr,lo):
    z,x,k,y=where_am_i()
    c=x*2+k
    def rc(src,dst,s,r,dev): return pltpu.make_async_remote_copy(src_ref=src,dst_ref=dst,send_sem=s,recv_sem=r,device_id=dev,device_id_type=MESH)
    loads=[pltpu.make_async_copy(D.at[j,k],A.at[j],ld.at[j]) for j in range(W)]
    for l in loads: l.start()
    z_,x_,k_,y_=z,x,k,y
    bar=pltpu.get_barrier_semaphore()
    peers=[(lax.rem(z+d+1,F),c,y) for d in range(F-1)]
    peers+=[(z,c,1-y),(z,(1-x)*2+k,y),(z,x*2+1-k,y),(z,(1-x)*2+1-k,y)]
    peers+=[(z,(1-x)*2+k,1-y),(z,x*2+1-k,1-y),(z,(1-x)*2+1-k,1-y)]
    for p in peers: pl.semaphore_signal(bar,inc=1,device_id=p,device_id_type=MESH)
    pl.semaphore_wait(bar,len(peers))
    xdev=(z,(1-x)*2+k,y); ydev=(z,c,1-y); kdev=(z,x*2+1-k,y); ddev=(z,(1-x)*2+1-k,y)
    kc=[rc(D.at[j,1-k],KB.at[j],ks.at[j],kr.at[j],kdev) for j in range(W)]
    for cp in kc: cp.start()
    def xfirst(j): return j%2==0
    def first(j):
        src=A.at[j,1-x] if xfirst(j) else A.at[j,:,1-y]
        return rc(src,B1.at[j],s1.at[j],r1.at[j],xdev if xfirst(j) else ydev)
    def mine1(j): return A.at[j,x] if xfirst(j) else A.at[j,:,y]
    def second(j):
        src=A.at[j,x,1-y] if xfirst(j) else A.at[j,1-x,y]
        return rc(src,B2.at[j],s2.at[j],r2.at[j],ydev if xfirst(j) else xdev)
    def zcopy(j,d):
        to=lax.rem(z-(d+1)+F,F)
        return rc(A.at[j,x,y,to],ZB.at[j,d],zs.at[j,d],zr.at[j,d],(to,c,y))
    def bcopy(j,i): return rc(R.at[j,c],R.at[j,c],bs.at[j,i],br.at[j,i],(kdev,xdev,ddev)[i])
    def fcopy(fi,j,i):
        cc=i
        return rc(R.at[j,c],RX.at[fi,c],fs.at[fi,i],fr.at[fi,i],(z,lax.rem(c+i,4),1-y))
    for t in range(W+3):
        j=t
        if j<W:
            loads[j].wait(); kc[j].wait_recv()
            add_into(A.at[j],KB.at[j],(2,2,F))
            first(j).start()
        j=t-1
        if 0<=j<W:
            first(j).wait_recv()
            add_into(mine1(j),B1.at[j],(2,F))
            second(j).start()
        j=t-2
        if 0<=j<W:
            second(j).wait_recv()
            add_into(A.at[j,x,y],B2.at[j],(F,))
            for d in range(F-1): zcopy(j,d).start()
        j=t-3
        if 0<=j<W:
            total=A[j,x,y,z].astype(jnp.float32)
            for d in range(F-1):
                zcopy(j,d).wait_recv()
                total=total+ZB[j,d].astype(jnp.float32)
            lo[j]=total.astype(lo.dtype)
            own=pltpu.make_async_copy(lo.at[j],R.at[j,c],ld.at[j]); own.start(); own.wait()
            for i in range(3): bcopy(j,i).start()
            if j in flags:
                for i in range(4): fcopy(flags.index(j),j,i).start()
    for j in range(W):
        kc[j].wait_send(); first(j).wait_send(); second(j).wait_send()
        for d in range(F-1): zcopy(j,d).wait_send()
        for i,(a,b) in enumerate(((0,1),(1,0),(1,1))):
            bcopy(j,i).wait_send()
            r=R.at[j,(x+a-2*a*x)*2+(k+b-2*b*k)]
            pltpu.make_async_copy(r,r,br.at[j,i]).wait()
    for fi,j in enumerate(flags):
        for i in range(4):
            fcopy(fi,j,i).wait_send()
            r=RX.at[fi,lax.rem(c-i+4,4)]
            pltpu.make_async_copy(r,r,fr.at[fi,i]).wait()

def reduce_call(F,Dm,flags,cid,name):
    W,_,_,_,_,rows,half=Dm.shape
    S=pltpu.SemaphoreType.DMA
    nf=max(1,len(flags))
    V=lambda *s: pltpu.VMEM(s,Dm.dtype)
    return pl.pallas_call(functools.partial(reduce_kernel,F,W,flags),
        out_shape=(jax.ShapeDtypeStruct((W,4,rows,half),Dm.dtype),jax.ShapeDtypeStruct((nf,4,rows,half),Dm.dtype)),
        in_specs=[ANY],out_specs=[ANY]*2,
        scratch_shapes=[V(W,2,2,F,rows,half),V(W,2,2,F,rows,half),V(W,2,F,rows,half),V(W,F,rows,half),V(W,F-1,rows,half),
            S((W,)),S((W,)),S((W,)),S((W,)),S((W,)),S((W,)),S((W,)),S((W,F-1)),S((W,F-1)),S((W,3)),S((W,3)),S((nf,4)),S((nf,4)),V(W,rows,half)],
        compiler_params=pltpu.CompilerParams(collective_id=cid,has_side_effects=True,vmem_limit_bytes=50<<20),name=name)(Dm)


D = 1024
HEADS = 8
HEAD = 128
EPS = 1e-06
NEG = -1e30
LOG2E = 1.4426950408889634
QC = 2
F32 = jnp.float32
BF16 = jnp.bfloat16
SCALE = HEAD ** -0.5
CE = SCALE * LOG2E

def nn(a, b): return lax.dot_general(a, b, (((1,), (0,)), ((), ())), preferred_element_type=F32)
def nt(a, b): return lax.dot_general(a, b, (((1,), (1,)), ((), ())), preferred_element_type=F32)
def tn(a, b): return lax.dot_general(a, b, (((0,), (0,)), ((), ())), preferred_element_type=F32)

def rows_loop(total, step, body):
    def run(i, _):
        body(pl.ds(pl.multiple_of(i * step, step), step))
        return 0
    lax.fori_loop(0, total // step, run, 0)

def inverse_of(v):
    return lax.rsqrt(jnp.mean(v * v, axis=-1, keepdims=True) + EPS)

def norm_into(dst, src, gain):
    def body(rs):
        v = src[rs, :].astype(F32)
        dst[rs, :] = (v * inverse_of(v) * gain[...]).astype(dst.dtype)
    rows_loop(src.shape[0], 32, body)

def head_cols(h): return pl.ds(pl.multiple_of(h * HEAD, HEAD), HEAD)

def causal_scores(s, first_key, first_query):
    keys = lax.broadcasted_iota(jnp.int32, s.shape, 0) + first_key
    qs = lax.broadcasted_iota(jnp.int32, s.shape, 1) + first_query
    return jnp.where(keys <= qs, s, NEG)

def attend_heads(parts_of, q, out, lse, rows):
    step = rows // QC
    def body(h, _):
        cs = head_cols(h)
        for qc in range(QC):
            rs = pl.ds(qc * step, step)
            qh = q[rs, cs]
            parts = parts_of(cs, qc)
            scores = [mask(nt(keys(), qh)) for keys, values, mask in parts]
            big = functools.reduce(jnp.maximum, [jnp.max(s, axis=0, keepdims=True) for s in scores])
            es = [jnp.exp2((s - big) * CE) for s in scores]
            total = functools.reduce(jnp.add, [jnp.sum(e, axis=0, keepdims=True) for e in es])
            inv = 1.0 / total
            acc = functools.reduce(jnp.add, [tn((e * inv).astype(BF16), p[1]()) for e, p in zip(es, parts)])
            out[rs, cs] = acc.astype(BF16)
            lse[h, :, pl.ds(qc * step, step)] = big * CE + jnp.log2(total)
        return 0
    lax.fori_loop(0, HEADS, body, 0)

def token_parts(kvp, kv, skv, first, rows):
    def parts_of(cs, qc):
        step = rows // QC
        upto = (qc + 1) * step
        same = lambda s: s
        earlier = lambda s: jnp.where(first, NEG, s)
        causal = lambda s: causal_scores(s, 0, qc * step)
        return [(lambda: kvp[0, :, cs], lambda: kvp[1, :, cs], earlier),
                (lambda: kv[0, pl.ds(0, upto), cs], lambda: kv[1, pl.ds(0, upto), cs], causal),
                (lambda: skv[0, :, cs], lambda: skv[1, :, cs], same)]
    return parts_of

def state_parts(kv):
    def parts_of(cs, qc):
        return [(lambda: kv[0, :, cs], lambda: kv[1, :, cs], lambda s: s)]
    return parts_of

def chain_barrier(r, n, dev):
    bar = pltpu.get_barrier_semaphore()
    @pl.when(r > 0)
    def _(): pl.semaphore_signal(bar, inc=1, device_id=dev(r - 1), device_id_type=MESH)
    @pl.when(r < n - 1)
    def _(): pl.semaphore_signal(bar, inc=1, device_id=dev(r + 1), device_id_type=MESH)
    pl.semaphore_wait(bar, jnp.where(r > 0, 1, 0) + jnp.where(r < n - 1, 1, 0))

FRONT_OUT = ("h", "q", "kv", "kvp", "skv", "n", "s", "sq", "zatt", "z", "lse", "lses", "att", "y1", "m")

def front_kernel(nctx, G, X, S0, gains, keep, *refs):
    outs = dict(zip(FRONT_OUT, refs[:15]))
    (WB, x, h, q, kv, kvp, skv, n, s, ssend, sq, zatt, zb, lse, lses, att, y1, m,
     wsem, osem, ksem, krem, ssem, srem) = refs[15:]
    f = lax.axis_index("fsdp"); r = lax.axis_index("ctx"); t = lax.axis_index("tp")
    dev = lambda c: (f, c, t)
    rows = x.shape[0]
    loads = [pltpu.make_async_copy(G.at[w], WB.at[w], wsem.at[w]) for w in range(8)]
    loads.append(pltpu.make_async_copy(X, x, wsem.at[8]))
    loads[8].start()
    for w in range(8): loads[w].start()
    chain_barrier(r, nctx, dev)
    names = {}
    def put(name, src, i):
        cp = pltpu.make_async_copy(src, outs[name], osem.at[i]); cp.start(); names[name] = cp
    ga, gs, gm = gains.at[pl.ds(0, 1)], gains.at[pl.ds(1, 1)], gains.at[pl.ds(2, 1)]
    loads[8].wait()
    norm_into(h, x, ga)
    put("h", h, 0)
    kcopy = [pltpu.make_async_remote_copy(src_ref=kv.at[i], dst_ref=kvp.at[i], send_sem=ksem.at[i], recv_sem=krem.at[i],
             device_id=dev(r + 1), device_id_type=MESH) for i in range(2)]
    for i in range(2):
        loads[i].wait()
        kv[i] = nn(h[...], WB[i]).astype(BF16)
        @pl.when(r < nctx - 1)
        def _(): kcopy[i].start()
    put("kv", kv, 1)
    half = D // 2
    scopy = [pltpu.make_async_remote_copy(src_ref=ssend.at[:, pl.ds(i * half, half)], dst_ref=s.at[:, pl.ds(i * half, half)],
             send_sem=ssem.at[i], recv_sem=srem.at[i], device_id=dev(r + 1), device_id_type=MESH) for i in range(2)]
    @pl.when(r == 0)
    def _():
        s[...] = S0[...]
        kvp[...] = jnp.zeros_like(kvp)
    @pl.when(r > 0)
    def _():
        loads[4].wait()
        q[...] = nn(h[...], WB[4]).astype(BF16)
        for cp in scopy: cp.wait_recv()
    norm_into(n, s, gs)
    put("s", s, 2)
    put("n", n, 3)
    for w in (2, 3): loads[w].wait()
    @pl.when(r < nctx - 1)
    def _():
        sq[...] = nn(n[...], WB[2]).astype(BF16)
        attend_heads(state_parts(kv), sq, zatt, lses, rows)
        for i in range(2):
            cs = pl.ds(i * half, half)
            z = nt(zatt[...], WB[3, cs, :])
            zb[:, cs] = z.astype(BF16)
            kr = keep[:, cs]
            ssend[:, cs] = (kr * s[:, cs].astype(F32) + (1.0 - kr) * z).astype(BF16)
            scopy[i].start()
    put("sq", sq, 4); put("zatt", zatt, 5); put("z", zb, 6); put("lses", lses, 7)
    @pl.when(r == 0)
    def _():
        loads[4].wait()
        q[...] = nn(h[...], WB[4]).astype(BF16)
    put("q", q, 8)
    for i in range(2):
        loads[5 + i].wait()
        skv[i] = nn(n[...], WB[5 + i]).astype(BF16)
    put("skv", skv, 9)
    @pl.when(r > 0)
    def _():
        for cp in kcopy: cp.wait_recv()
    put("kvp", kvp, 10)
    attend_heads(token_parts(kvp, kv, skv, r == 0, rows), q, att, lse, rows)
    put("att", att, 11); put("lse", lse, 12)
    loads[7].wait()
    y1[...] = x[...].astype(F32) + nt(att[...], WB[7])
    put("y1", y1, 13)
    norm_into(m, y1, gm)
    put("m", m, 14)
    @pl.when(r < nctx - 1)
    def _():
        for cp in kcopy: cp.wait_send()
        for cp in scopy: cp.wait_send()
    for cp in names.values(): cp.wait()

def front_call(nctx, G, X, S0, gains, keep):
    rows = X.shape[0]
    sh = lambda *s: jax.ShapeDtypeStruct(s, BF16)
    fl = lambda *s: jax.ShapeDtypeStruct(s, F32)
    shapes = dict(h=sh(rows, D), q=sh(rows, D), kv=sh(2, rows, D), kvp=sh(2, rows, D), skv=sh(2, rows, D), n=sh(rows, D),
        s=sh(rows, D), sq=sh(rows, D), zatt=sh(rows, D), z=sh(rows, D), lse=fl(HEADS, 1, rows), lses=fl(HEADS, 1, rows),
        att=sh(rows, D), y1=fl(rows, D), m=sh(rows, D))
    V = lambda *s: pltpu.VMEM(s, BF16)
    VF = lambda *s: pltpu.VMEM(s, F32)
    S = pltpu.SemaphoreType.DMA
    vm = pl.BlockSpec(memory_space=pltpu.VMEM)
    outs = pl.pallas_call(functools.partial(front_kernel, nctx),
        out_shape=[shapes[k] for k in FRONT_OUT],
        in_specs=[ANY, ANY, vm, vm, vm], out_specs=[ANY] * 15,
        scratch_shapes=[V(8, D, D), V(rows, D), V(rows, D), V(rows, D), V(2, rows, D), V(2, rows, D), V(2, rows, D), V(rows, D), V(rows, D), V(rows, D),
            V(rows, D), V(rows, D), V(rows, D), VF(HEADS, 1, rows), VF(HEADS, 1, rows), V(rows, D), VF(rows, D), V(rows, D),
            S((9,)), S((15,)), S((2,)), S((2,)), S((2,)), S((2,))],
        compiler_params=pltpu.CompilerParams(collective_id=3, has_side_effects=True, vmem_limit_bytes=58 << 20), name="front")(G, X, S0, gains, keep)
    return dict(zip(FRONT_OUT, outs))

def store_blocks(dst, F, row0, val):
    blk = D // (4 * F)
    half = D // 2
    n = val.shape[0] // blk
    z0 = row0 // (D // F) if isinstance(row0, int) else lax.div(row0, D // F)
    for b in range(n):
        zz, xk = b // 4, b % 4
        for y in range(2):
            dst[xk % 2, xk // 2, y, z0 + zz] = val[b * blk:(b + 1) * blk, y * half:(y + 1) * half].astype(dst.dtype)

def weight_grad(dst, F, left, right):
    step = max(D // F, 256)
    def body(i, _):
        r0 = pl.multiple_of(i * step, step)
        store_blocks(dst, F, r0, tn(left[:, pl.ds(r0, step)], right[...]))
        return 0
    lax.fori_loop(0, D // step, body, 0)

G1 = 0.7978845608028654
G3 = 0.044715

def norm_back_rows(v, gain, e):
    inv = inverse_of(v)
    w = e * gain
    proj = jnp.sum(w * v, axis=-1, keepdims=True) * (1.0 / D)
    return inv * w - v * (inv * inv * inv) * proj, e * v * inv

def fold8(v):
    return functools.reduce(jnp.add, [v[i * 8:(i + 1) * 8] for i in range(v.shape[0] // 8)])

def mlp_kernel(F, up, dn, m, g, y1, gains, Dg, out, gy1, gg, a, du, u, da, oacc, macc):
    j = pl.program_id(0)
    a[...] = nn(m[...], up[0])
    du[...] = nn(g[...], dn[0])
    def body(rs):
        av = a[rs, :]
        sq = av * av
        t = jnp.tanh(G1 * av * (1.0 + G3 * sq))
        u[rs, :] = (0.5 * av * (1.0 + t)).astype(BF16)
        dg = 0.5 * (1.0 + t) + 0.5 * av * (1.0 - t * t) * (G1 * (1.0 + 3.0 * G3 * sq))
        da[rs, :] = (dg * du[rs, :]).astype(BF16)
    rows_loop(m.shape[0], 32, body)
    o = nt(u[...], dn[0])
    d = nt(da[...], up[0])
    @pl.when(j == 0)
    def _():
        oacc[...] = o
        macc[...] = d
    @pl.when(j > 0)
    def _():
        oacc[...] += o
        macc[...] += d
    weight_grad(Dg.at[0, 0], F, m, da)
    weight_grad(Dg.at[1, 0], F, g, u)
    @pl.when(j == pl.num_programs(0) - 1)
    def _():
        gg[...] = jnp.zeros_like(gg)
        gm = gains.at[pl.ds(2, 1)]
        def last(rs):
            y = y1[rs, :]
            out[rs, :] = (y + oacc[rs, :]).astype(BF16)
            dv, dgain = norm_back_rows(y, gm[...], macc[rs, :])
            gy1[rs, :] = g[rs, :].astype(F32) + dv
            gg[...] += fold8(dgain)
        rows_loop(m.shape[0], 32, last)

def mlp_call(F, G, m, g, y1, gains):
    rows = m.shape[0]
    n = 4
    blk = D // (4 * F)
    full = lambda s: pl.BlockSpec(s, lambda j: (0,) * len(s))
    V = lambda *s: pltpu.VMEM(s, BF16)
    VF = lambda *s: pltpu.VMEM(s, F32)
    return pl.pallas_call(functools.partial(mlp_kernel, F), grid=(n,),
        out_shape=[jax.ShapeDtypeStruct((2, n, 2, 2, 2, F, blk, D // 2), BF16), jax.ShapeDtypeStruct((rows, D), BF16),
                   jax.ShapeDtypeStruct((rows, D), F32), jax.ShapeDtypeStruct((8, D), F32)],
        in_specs=[pl.BlockSpec((1, D, D), lambda j: (8 + j, 0, 0)), pl.BlockSpec((1, D, D), lambda j: (12 + j, 0, 0)),
                  full((rows, D)), full((rows, D)), full((rows, D)), full((8, D))],
        out_specs=[pl.BlockSpec((2, 1, 2, 2, 2, F, blk, D // 2), lambda j: (0, j, 0, 0, 0, 0, 0, 0)), full((rows, D)), full((rows, D)), full((8, D))],
        scratch_shapes=[VF(rows, D), VF(rows, D), V(rows, D), V(rows, D), VF(rows, D), VF(rows, D)],
        compiler_params=pltpu.CompilerParams(vmem_limit_bytes=56 << 20), name="mlp")(G, G, m, g, y1, gains)

BACK_IN = ("h", "q", "kv", "kvp", "skv", "n", "s", "sq", "zatt", "z", "lse", "lses", "att", "x", "gy1")

def attend_heads_back(parts_of, q, datt, lse, dq, sink, rows):
    step = rows // QC
    def body(h, _):
        cs = head_cols(h)
        sums = None
        for qc in range(QC):
            rs = pl.ds(qc * step, step)
            qh = q[rs, cs]
            gh = datt[rs, cs]
            ls = lse[h, :, pl.ds(qc * step, step)]
            parts = parts_of(cs, qc)
            ps = [jnp.exp2(p[2](nt(p[0](), qh)) * CE - ls) for p in parts]
            dps = [nt(p[1](), gh) for p in parts]
            delta = functools.reduce(jnp.add, [jnp.sum(a * b, axis=0, keepdims=True) for a, b in zip(ps, dps)])
            dss = [(a * (b - delta)).astype(BF16) for a, b in zip(ps, dps)]
            dq[rs, cs] = (functools.reduce(jnp.add, [tn(d, p[0]()) for d, p in zip(dss, parts)]) * SCALE).astype(dq.dtype)
            new = [(nn(d, qh), nn(a.astype(BF16), gh)) for a, d in zip(ps, dss)]
            if sums is None: sums = new
            else:
                merged = []
                for (k0, v0), (k1, v1) in zip(sums, new):
                    n0 = k0.shape[0]
                    if n0 < k1.shape[0]:
                        k1 = jnp.concatenate([k0 + k1[:n0], k1[n0:]], axis=0)
                        v1 = jnp.concatenate([v0 + v1[:n0], v1[n0:]], axis=0)
                    else:
                        k1, v1 = k0 + k1, v0 + v1
                    merged.append((k1, v1))
                sums = merged
        for i, (dk, dv) in enumerate(sums): sink(i, cs, dk * SCALE, dv)
        return 0
    lax.fori_loop(0, HEADS, body, 0)

def back_kernel(nctx, F, G, gains, keep, *refs):
    ins = dict(zip(BACK_IN, refs[:15]))
    Dg, gx, gg, ds0 = refs[15:19]
    nb = 19
    bufs = dict(zip(BACK_IN, refs[nb:nb + 15]))
    (WB, do, datt, dqb, dkv, dsend, dret, dskv, dntok, dsin, dsout, stage, ggv,
     wsem, isem, dsem, psem, prem, csem, crem, fsem) = refs[nb + 15:]
    f = lax.axis_index("fsdp"); r = lax.axis_index("ctx"); t = lax.axis_index("tp")
    dev = lambda c: (f, c, t)
    B = bufs
    rows = do.shape[0]
    order = ("gy1", "att", "q", "kv", "kvp", "skv", "lse", "n", "s", "sq", "zatt", "z", "lses", "h", "x")
    loads = {k: pltpu.make_async_copy(ins[k], bufs[k], isem.at[i]) for i, k in enumerate(order)}
    slots = ((7, 0), (5, 1), (6, 2), (3, 3), (2, 4), (4, 0), (0, 1), (1, 2))
    wload = {w: pltpu.make_async_copy(G.at[w], WB.at[sl], wsem.at[i]) for i, (w, sl) in enumerate(slots)}
    slot = dict(slots)
    loads["gy1"].start()
    wload[7].start()
    for k in order[1:]: loads[k].start()
    for w in (5, 6, 3, 2): wload[w].start()
    chain_barrier(r, nctx, dev)
    gs, ga = gains.at[pl.ds(1, 1)], gains.at[pl.ds(0, 1)]
    ggv[...] = jnp.zeros_like(ggv)
    loads["gy1"].wait()
    def cast(rs): do[rs, :] = B["gy1"][rs, :].astype(BF16)
    rows_loop(rows, 64, cast)
    wload[7].wait()
    datt[...] = nn(do[...], WB[slot[7]]).astype(BF16)
    wload[4].start()
    for k in order[1:7]: loads[k].wait()
    def sink(i, cs, dk, dv):
        dst = (dsend, dkv, dskv)[i]
        dst[0, :, cs] = dk.astype(dst.dtype)
        dst[1, :, cs] = dv.astype(dst.dtype)
    attend_heads_back(token_parts(B["kvp"], B["kv"], B["skv"], r == 0, rows), B["q"], datt, B["lse"], dqb, sink, rows)
    pcopy = pltpu.make_async_remote_copy(src_ref=dsend, dst_ref=dret, send_sem=psem.at[0], recv_sem=prem.at[0], device_id=dev(r - 1), device_id_type=MESH)
    @pl.when(r > 0)
    def _(): pcopy.start()
    wload[5].wait(); wload[6].wait()
    dntok[...] = nt(dskv[0], WB[slot[5]]) + nt(dskv[1], WB[slot[6]])
    wload[0].start(); wload[1].start()
    for k in order[7:9]: loads[k].wait()
    half = rows // 2
    ccopy = [pltpu.make_async_remote_copy(src_ref=dsout.at[pl.ds(i * half, half)], dst_ref=dsin.at[pl.ds(i * half, half)],
             send_sem=csem.at[i], recv_sem=crem.at[i], device_id=dev(r - 1), device_id_type=MESH) for i in range(2)]
    def finish_state(extra):
        for i in range(2):
            def body(j, _):
                rs = pl.ds(pl.multiple_of(i * half + j * 32, 32), 32)
                dv, dgain = norm_back_rows(B["s"][rs, :].astype(F32), gs[...], dntok[rs, :])
                if extra: dv = dv + keep[...] * dsin[rs, :].astype(F32)
                dsout[rs, :] = dv.astype(BF16)
                ggv[pl.ds(8, 8), :] += fold8(dgain)
                return 0
            lax.fori_loop(0, half // 32, body, 0)
            @pl.when(r > 0)
            def _(): ccopy[i].start()
    @pl.when(r == nctx - 1)
    def _(): finish_state(False)
    dcopies = []
    state = {"n": 0}
    def grad_out(w, left, right, ready=None):
        i = state["n"]; state["n"] += 1
        sl = i % 3
        if i >= 3: dcopies[i - 3].wait()
        weight_grad(stage.at[sl], F, left, right)
        cp = pltpu.make_async_copy(stage.at[sl], Dg.at[w], dsem.at[i])
        cp.start(); dcopies.append(cp)
    loads["h"].wait()
    grad_out(7, do, B["att"])
    grad_out(5, B["n"], dskv.at[0])
    grad_out(6, B["n"], dskv.at[1])
    grad_out(4, B["h"], dqb)
    for k in order[9:13]: loads[k].wait()
    wload[3].wait(); wload[2].wait()
    dzb, dza, dsq = datt, dqb, do
    dh = dntok
    wload[4].wait()
    dhq = B["q"]
    @pl.when(r < nctx - 1)
    def _():
        for cp in ccopy: cp.wait_recv()
        def body(rs):
            d = dsin[rs, :].astype(F32)
            kr = keep[...]
            dzb[rs, :] = ((1.0 - kr) * d).astype(BF16)
            ggv[pl.ds(16, 8), :] += fold8(d * (B["s"][rs, :].astype(F32) - B["z"][rs, :].astype(F32)) * kr * (1.0 - kr))
        rows_loop(rows, 32, body)
        do[...] = nn(dzb[...], WB[slot[3]]).astype(BF16)
        def sink2(i, cs, dk, dv):
            dkv[0, :, cs] += dk
            dkv[1, :, cs] += dv
        attend_heads_back(state_parts(B["kv"]), B["sq"], do, B["lses"], B["q"], sink2, rows)
        dntok[...] += nt(B["q"][...], WB[slot[2]])
        finish_state(True)
    @pl.when(r == nctx - 1)
    def _():
        B["q"][...] = jnp.zeros_like(B["q"])
        dzb[...] = jnp.zeros_like(dzb)
        B["zatt"][...] = jnp.zeros_like(B["zatt"])
    @pl.when(r == 0)
    def _():
        cp = pltpu.make_async_copy(dsout, ds0, fsem.at[0]); cp.start(); cp.wait()
    @pl.when(r > 0)
    def _():
        dsin[...] = jnp.zeros_like(dsin)
        cp = pltpu.make_async_copy(dsin, ds0, fsem.at[0]); cp.start(); cp.wait()
    grad_out(2, B["n"], B["q"])
    grad_out(3, dzb, B["zatt"])
    @pl.when(r < nctx - 1)
    def _(): pcopy.wait_recv()
    @pl.when(r == nctx - 1)
    def _(): dret[...] = jnp.zeros_like(dret)
    dkvb = B["kvp"]
    for i in range(2):
        def add(rs): dkvb[i, rs, :] = (dkv[i, rs, :] + dret[i, rs, :].astype(F32)).astype(BF16)
        rows_loop(rows, 32, add)
    grad_out(0, B["h"], dkvb.at[0])
    grad_out(1, B["h"], dkvb.at[1])
    wload[0].wait(); wload[1].wait()
    loads["x"].wait()
    dntok[...] = nt(dqb[...], WB[slot[4]]) + nt(dkvb[0], WB[slot[0]]) + nt(dkvb[1], WB[slot[1]])
    gxb = B["att"]
    def last(rs):
        dv, dgain = norm_back_rows(B["x"][rs, :].astype(F32), ga[...], dntok[rs, :])
        gxb[rs, :] = (B["gy1"][rs, :] + dv).astype(BF16)
        ggv[pl.ds(0, 8), :] += fold8(dgain)
    rows_loop(rows, 32, last)
    cps = [pltpu.make_async_copy(gxb, gx, fsem.at[1]), pltpu.make_async_copy(ggv, gg, fsem.at[2])]
    for cp in cps: cp.start()
    for cp in dcopies[-3:]: cp.wait()
    for cp in cps: cp.wait()
    @pl.when(r > 0)
    def _():
        pcopy.wait_send()
        for cp in ccopy: cp.wait_send()

def back_call(nctx, F, G, gains, keep, vals):
    rows = vals["h"].shape[0]
    blk = D // (4 * F)
    V = lambda *s: pltpu.VMEM(s, BF16)
    VF = lambda *s: pltpu.VMEM(s, F32)
    S = pltpu.SemaphoreType.DMA
    vm = pl.BlockSpec(memory_space=pltpu.VMEM)
    args = [vals[k] for k in BACK_IN]
    return pl.pallas_call(functools.partial(back_kernel, nctx, F),
        out_shape=[jax.ShapeDtypeStruct((8, 2, 2, 2, F, blk, D // 2), BF16), jax.ShapeDtypeStruct((rows, D), BF16),
                   jax.ShapeDtypeStruct((24, D), F32), jax.ShapeDtypeStruct((rows, D), BF16)],
        in_specs=[ANY, vm, vm] + [ANY] * 15, out_specs=[ANY] * 4,
        scratch_shapes=[pltpu.VMEM(a.shape, a.dtype) for a in args] + [
            V(5, D, D), V(rows, D), V(rows, D), V(rows, D), VF(2, rows, D), V(2, rows, D), V(2, rows, D), V(2, rows, D), VF(rows, D), V(rows, D), V(rows, D),
            V(3, 2, 2, 2, F, blk, D // 2), VF(24, D),
            S((8,)), S((15,)), S((8,)), S((1,)), S((1,)), S((2,)), S((2,)), S((3,))],
        compiler_params=pltpu.CompilerParams(collective_id=4, has_side_effects=True, vmem_limit_bytes=62 << 20), name="back")(G, gains, keep, *args)


def pack_local(w, tp_rank):
    (w_query, w_key, w_value, w_out, w_skey, w_svalue, w_squery, w_sout, w_up, w_down) = w
    half = D // 2
    rows = w_query.shape[0]
    squery = lax.dynamic_slice_in_dim(w_squery, tp_rank * half, half, 1)
    sout = lax.dynamic_slice_in_dim(w_sout, tp_rank * half, half, 0)
    up = w_up.reshape(rows, -1, half).swapaxes(0, 1)
    down = w_down.reshape(-1, half, rows).swapaxes(1, 2)
    one = [w_key, w_value, squery, sout.T, w_query, w_skey, w_svalue, w_out.T]
    packed = jnp.concatenate([jnp.stack(one), up, down], axis=0)
    return packed.reshape(packed.shape[0], 2, 2, rows // 4, half)


def local(
    tokens,
    cotangent,
    w_query,
    w_key,
    w_value,
    w_out,
    w_state_key,
    w_state_value,
    w_state_query,
    w_state_out,
    w_up,
    w_down,
    gain_attn,
    gain_state,
    gain_mlp,
    forget_logit,
    state_init,
):
    fsdp = lax.axis_size("fsdp")
    tp_rank = lax.axis_index("tp")
    ctx_count = lax.axis_size("ctx")
    half = D // 2
    shards = (w_query, w_key, w_value, w_out, w_state_key, w_state_value, w_state_query, w_state_out, w_up, w_down)
    packed = pack_local(shards, tp_rank)
    tp_gains = jnp.pad(jnp.stack([gain_attn, gain_mlp]), ((0, 6), (0, 0)))
    full, x, g, both_gains = gather_call(fsdp, packed, tokens, cotangent, tp_gains)
    full = full.reshape(full.shape[0], D, D)
    gains = jnp.pad(jnp.stack([both_gains[0], gain_state, both_gains[1]]), ((0, 5), (0, 0)))
    keep = jax.nn.sigmoid(forget_logit)[None]
    vals = front_call(ctx_count, full, x, state_init, gains, keep)
    grads_mlp, out, gy1, sum_mlp = mlp_call(fsdp, full, vals["m"], g, vals["y1"], gains)
    vals["x"] = x
    vals["gy1"] = gy1
    grads, gx, sums, ds0 = back_call(ctx_count, fsdp, full, gains, keep, vals)
    grads_mlp = grads_mlp.reshape((8,) + grads.shape[1:])
    r, rx = reduce_call(fsdp, grads, (2, 3), 2, "reduce_attn")
    rm, _ = reduce_call(fsdp, grads_mlp, (), 5, "reduce_mlp")
    rows = D // fsdp
    r = r.reshape(8, rows, half).astype(F32)
    rx = rx.reshape(2, rows, half).astype(F32)
    rm = rm.reshape(8, rows, half).astype(F32)

    def both(mine, other):
        first = jnp.where(tp_rank == 0, mine, other)
        second = jnp.where(tp_rank == 0, other, mine)
        return jnp.concatenate([first, second], axis=1)

    def swapped(value):
        parts = value.reshape(value.shape[0], 2, half).swapaxes(0, 1)
        mine = lax.dynamic_index_in_dim(parts, tp_rank, 0, False)
        sent = lax.dynamic_index_in_dim(parts, 1 - tp_rank, 0, False)
        got = lax.ppermute(sent, "tp", [(0, 1), (1, 0)])
        return jnp.where(tp_rank == 0, jnp.stack([mine, got]), jnp.stack([got, mine]))

    small = jnp.concatenate([sums, sum_mlp], axis=0).reshape(4, 8, D).sum(axis=1)
    small = lax.psum(small, ("fsdp", "ctx", "tp"))
    start = lax.psum(ds0, ("fsdp", "ctx", "tp")).astype(F32)
    at = lambda i: lax.dynamic_slice_in_dim(small[i], tp_rank * half, half, 0)
    return (
        swapped(out),
        swapped(gx),
        r[4],
        r[0],
        r[1],
        r[7].T,
        r[5],
        r[6],
        both(r[2], rx[0]),
        both(r[3], rx[1]).T,
        rm[:4].swapaxes(0, 1).reshape(rows, -1),
        rm[4:].swapaxes(1, 2).reshape(-1, rows),
        at(0),
        small[1],
        at(3),
        small[2],
        start,
    )


def solution(mesh):
    placed = (
        P("fsdp", "ctx", "tp"),
        P("fsdp", "ctx", "tp"),
        P("fsdp", "tp"),
        P("fsdp", "tp"),
        P("fsdp", "tp"),
        P("tp", "fsdp"),
        P("fsdp", "tp"),
        P("fsdp", "tp"),
        P("fsdp", None),
        P(None, "fsdp"),
        P("fsdp", "tp"),
        P("tp", "fsdp"),
        P("tp"),
        P(),
        P("tp"),
        P(),
        P(),
    )
    return jax.shard_map(
        local,
        mesh=mesh,
        in_specs=placed,
        out_specs=(
            P("fsdp", "ctx", "tp"),
            P("fsdp", "ctx", "tp"),
            P("fsdp", "tp"),
            P("fsdp", "tp"),
            P("fsdp", "tp"),
            P("tp", "fsdp"),
            P("fsdp", "tp"),
            P("fsdp", "tp"),
            P("fsdp", None),
            P(None, "fsdp"),
            P("fsdp", "tp"),
            P("tp", "fsdp"),
            P("tp"),
            P(),
            P("tp"),
            P(),
            P(),
        ),
        check_vma=False,
    )
```

```python
import functools

import jax
import jax.numpy as jnp
from jax import lax
from jax.experimental import pallas as pl
from jax.experimental.pallas import tpu as pltpu
from jax.sharding import PartitionSpec as P

MESH = pl.DeviceIdType.MESH
ANY = pl.BlockSpec(memory_space=pl.ANY)
D = 1024
HEADS = 8
HEAD = 128
EPS = 1e-06
NEG = -1e30
LOG2E = 1.4426950408889634
F32 = jnp.float32
BF16 = jnp.bfloat16
SCALE = HEAD ** -0.5
CE = SCALE * LOG2E

def nn(a, b): return lax.dot_general(a, b, (((1,), (0,)), ((), ())), preferred_element_type=F32)
def nt(a, b): return lax.dot_general(a, b, (((1,), (1,)), ((), ())), preferred_element_type=F32)
def tn(a, b): return lax.dot_general(a, b, (((0,), (0,)), ((), ())), preferred_element_type=F32)

def rows_loop(total, step, body):
    def run(i, _):
        body(pl.ds(pl.multiple_of(i * step, step), step))
        return 0
    lax.fori_loop(0, total // step, run, 0)

def inverse_of(v):
    return lax.rsqrt(jnp.mean(v * v, axis=-1, keepdims=True) + EPS)

def norm_into(dst, src, gain):
    def body(rs):
        v = src[rs, :].astype(F32)
        dst[rs, :] = (v * inverse_of(v) * gain[...]).astype(dst.dtype)
    rows_loop(src.shape[0], 32, body)

def head_cols(h): return pl.ds(pl.multiple_of(h * HEAD, HEAD), HEAD)

def causal_scores(s, first_key, first_query):
    keys = lax.broadcasted_iota(jnp.int32, s.shape, 0) + first_key
    qs = lax.broadcasted_iota(jnp.int32, s.shape, 1) + first_query
    return jnp.where(keys <= qs, s, NEG)

def over_heads(one, unroll):
    def body(i, _):
        for u in range(unroll):
            one(i * unroll + u)
        return 0
    lax.fori_loop(0, HEADS // unroll, body, 0)

def attend_heads(parts_of, q, out, lse, rows, chunks, unroll):
    step = rows // chunks
    def one(h):
        cs = head_cols(h)
        for qc in range(chunks):
            rs = pl.ds(qc * step, step)
            qh = q[rs, cs]
            parts = parts_of(cs, qc)
            scores = [mask(nt(keys(), qh)) for keys, values, mask in parts]
            big = functools.reduce(jnp.maximum, [jnp.max(s, axis=0, keepdims=True) for s in scores])
            es = [jnp.exp2((s - big) * CE) for s in scores]
            total = functools.reduce(jnp.add, [jnp.sum(e, axis=0, keepdims=True) for e in es])
            inv = 1.0 / total
            acc = functools.reduce(jnp.add, [tn((e * inv).astype(BF16), p[1]()) for e, p in zip(es, parts)])
            out[rs, cs] = acc.astype(BF16)
            lse[h, :, pl.ds(qc * step, step)] = big * CE + jnp.log2(total)
    over_heads(one, unroll)

def token_parts(kvp, kv, skv, first, rows, chunks):
    def parts_of(cs, qc):
        step = rows // chunks
        upto = (qc + 1) * step
        same = lambda s: s
        earlier = lambda s: jnp.where(first, NEG, s)
        causal = lambda s: causal_scores(s, 0, qc * step)
        return [(lambda: kvp[0, :, cs], lambda: kvp[1, :, cs], earlier),
                (lambda: kv[0, pl.ds(0, upto), cs], lambda: kv[1, pl.ds(0, upto), cs], causal),
                (lambda: skv[0, :, cs], lambda: skv[1, :, cs], same)]
    return parts_of

def state_parts(kv):
    def parts_of(cs, qc):
        return [(lambda: kv[0, :, cs], lambda: kv[1, :, cs], lambda s: s)]
    return parts_of

def chain_barrier(r, n, dev):
    bar = pltpu.get_barrier_semaphore()
    @pl.when(r > 0)
    def _(): pl.semaphore_signal(bar, inc=1, device_id=dev(r - 1), device_id_type=MESH)
    @pl.when(r < n - 1)
    def _(): pl.semaphore_signal(bar, inc=1, device_id=dev(r + 1), device_id_type=MESH)
    pl.semaphore_wait(bar, jnp.where(r > 0, 1, 0) + jnp.where(r < n - 1, 1, 0))

def where_am_i():
    f = lax.axis_index("fsdp")
    c = lax.axis_index("ctx")
    return f, lax.div(c, 2), lax.rem(c, 2), lax.axis_index("tp")

def cols_of(t):
    return pl.ds(pl.multiple_of(t * (D // 2), D // 2), D // 2)

G1 = 0.7978845608028654
G3 = 0.044715

def norm_back_rows(v, gain, e):
    inv = inverse_of(v)
    w = e * gain
    proj = jnp.sum(w * v, axis=-1, keepdims=True) * (1.0 / D)
    return inv * w - v * (inv * inv * inv) * proj, e * v * inv

def fold8(v):
    return functools.reduce(jnp.add, [v[i * 8:(i + 1) * 8] for i in range(v.shape[0] // 8)])


class Gather:
    def __init__(self, G, F, sems):
        self.G, self.F, self.sems = G, F, sems
        self.z, self.x, self.k, self.y = where_am_i()

    def src_z(self, d):
        return lax.rem(self.z + d + 1, self.F)

    def region(self, g, z, x, k, cols=None):
        w = pl.ds(2 * g, 2)
        if cols is None:
            return self.G.at[w, z, x, k]
        return self.G.at[w, z, x, k, :, cols]

    def both_x(self, g, z, k, cols=None):
        w = pl.ds(2 * g, 2)
        if cols is None:
            return self.G.at[w, z, :, k]
        return self.G.at[w, z, :, k, :, cols]

    def remote(self, ref, i, g, d, dev):
        return pltpu.make_async_remote_copy(
            src_ref=ref, dst_ref=ref, send_sem=self.sems[i].at[g, d], recv_sem=self.sems[i + 1].at[g, d],
            device_id=dev, device_id_type=MESH)

    def landed(self, ref, i, g, d):
        pltpu.make_async_copy(ref, ref, self.sems[i + 1].at[g, d]).wait()

    def zcopy(self, g, d):
        to = lax.rem(self.z - (d + 1) + self.F, self.F)
        return self.remote(self.region(g, self.z, self.x, self.k, cols_of(self.y)), 0, g, d, (to, self.x * 2 + self.k, self.y))

    def ycopy(self, g, d):
        dev = (self.z, self.x * 2 + self.k, 1 - self.y)
        if d == self.F - 1:
            return self.remote(self.both_x(g, self.z, self.k, cols_of(self.y)), 2, g, d, dev)
        return self.remote(self.region(g, self.src_z(d), self.x, self.k, cols_of(self.y)), 2, g, d, dev)

    def xcopy(self, g, d):
        return self.remote(self.region(g, self.src_z(d), self.x, self.k), 4, g, d, (self.z, (1 - self.x) * 2 + self.k, self.y))

    def kcopy(self, g, d):
        dev = (self.z, self.x * 2 + 1 - self.k, self.y)
        if d == self.F - 1:
            return self.remote(self.both_x(g, self.z, self.k, cols_of(1 - self.y)), 6, g, d, dev)
        return self.remote(self.both_x(g, self.src_z(d), self.k), 6, g, d, dev)

    def send_z(self, g):
        for d in range(self.F - 1):
            self.zcopy(g, d).start()
        self.ycopy(g, self.F - 1).start()

    def stage_y(self, g):
        for d in range(self.F - 1):
            self.landed(self.region(g, self.src_z(d), self.x, self.k, cols_of(self.y)), 0, g, d)
            self.ycopy(g, d).start()

    def stage_x(self, g):
        o = cols_of(1 - self.y)
        for d in range(self.F - 1):
            self.landed(self.region(g, self.src_z(d), self.x, self.k, o), 2, g, d)
            self.xcopy(g, d).start()
        self.landed(self.both_x(g, self.z, self.k, o), 2, g, self.F - 1)
        self.kcopy(g, self.F - 1).start()

    def stage_k(self, g):
        for d in range(self.F - 1):
            self.landed(self.region(g, self.src_z(d), 1 - self.x, self.k), 4, g, d)
            self.kcopy(g, d).start()

    def done(self, g):
        for d in range(self.F - 1):
            self.landed(self.both_x(g, self.src_z(d), 1 - self.k), 6, g, d)
        self.landed(self.both_x(g, self.z, 1 - self.k, cols_of(1 - self.y)), 6, g, self.F - 1)

    def drain(self, g):
        for d in range(self.F):
            if d < self.F - 1:
                self.zcopy(g, d).wait_send()
                self.xcopy(g, d).wait_send()
            self.ycopy(g, d).wait_send()
            self.kcopy(g, d).wait_send()

def barrier_with(F, count):
    z, x, k, y = where_am_i()
    bar = pltpu.get_barrier_semaphore()
    peers = [(lax.rem(z + d + 1, F), x * 2 + k, y) for d in range(F - 1)]
    for dx, dk, dy in ((0, 0, 1), (1, 0, 0), (0, 1, 0), (1, 1, 0), (1, 0, 1), (0, 1, 1), (1, 1, 1))[:count]:
        peers.append((z, lax.rem(x + dx, 2) * 2 + lax.rem(k + dk, 2), lax.rem(y + dy, 2)))
    for p in peers:
        pl.semaphore_signal(bar, inc=1, device_id=p, device_id_type=MESH)
    pl.semaphore_wait(bar, len(peers))

A_IN = ("tokens", "cotangent", "gtp", "gstate", "keep", "s0", "key", "value", "squery", "sout", "query", "skey", "svalue", "out", "up", "down")
A_OUT = ("G", "Dc", "out", "gg", "h", "q", "kv", "kvp", "skv", "n", "s", "sq", "zatt", "z", "lse", "lses", "att", "x", "gy1", "gains")
A_BUF = ("x", "g", "h", "q", "kv", "kvp", "skv", "n", "s", "ssend", "sq", "zatt", "z", "att", "m", "u", "da", "y1", "a", "du", "oacc", "macc", "lse", "lses", "gains", "gs", "gg", "keep", "tin", "tout", "WB")

def forward_kernel(F, nctx, *refs):
    I = dict(zip(A_IN, refs)); at = len(A_IN)
    O = dict(zip(A_OUT, refs[at:])); at += len(A_OUT)
    B = dict(zip(A_BUF, refs[at:])); at += len(A_BUF)
    gsems = refs[at:at + 8]
    own, ins, osem, wsem, ksem, krem, ssem, srem, ysem, yrem, dsem = refs[at + 8:]
    z_, x_, k_, y_ = where_am_i()
    r = x_ * 2 + k_
    rows = B["x"].shape[0]
    half = D // 2
    dev = lambda c: (z_, c, y_)
    gat = Gather(O["G"], F, gsems)
    G = O["G"]
    mine = cols_of(y_)
    WB = B["WB"]
    W = lambda i: WB[i].reshape(D, D)
    def place(w, ref): return pltpu.make_async_copy(ref, G.at[w, z_, :, :, :, mine], own.at[w])
    owns = {0: place(0, I["key"]), 1: place(1, I["value"]), 2: place(2, I["squery"].at[:, :, :, mine]), 4: place(4, I["query"]),
            5: place(5, I["skey"]), 6: place(6, I["svalue"])}
    for j in range(4):
        owns[8 + 2 * j] = place(8 + 2 * j, I["up"].at[:, :, :, pl.ds(j * half, half)])
    tcopies = []
    tsrc = [(3, I["sout"].at[mine]), (7, I["out"])] + [(9 + 2 * j, I["down"].at[pl.ds(j * half, half)]) for j in range(4)]
    for i, (w, ref) in enumerate(tsrc):
        tcopies.append(pltpu.make_async_copy(ref, B["tin"].at[i], ins.at[i]))
        owns[w] = place(w, B["tout"].at[i])
    for w in (0, 1, 2): owns[w].start()
    for c in tcopies: c.start()
    loc = [pltpu.make_async_copy(I["tokens"].at[y_], B["x"].at[:, mine], ins.at[6]),
           pltpu.make_async_copy(I["gtp"], B["gains"].at[:, mine], ins.at[7]),
           pltpu.make_async_copy(I["keep"], B["keep"], ins.at[8]),
           pltpu.make_async_copy(I["gstate"], B["gs"], ins.at[9]),
           pltpu.make_async_copy(I["cotangent"].at[y_], B["g"].at[:, mine], ins.at[10])]
    s0copy = pltpu.make_async_copy(I["s0"], B["s"], ins.at[11])
    for c in loc: c.start()
    for w in (4, 5, 6, 8, 10, 12, 14): owns[w].start()
    barrier_with(F, 4)
    pdev = (z_, r, 1 - y_)
    swap = lambda i, s, d: pltpu.make_async_remote_copy(src_ref=s, dst_ref=d, send_sem=ysem.at[i], recv_sem=yrem.at[i], device_id=pdev, device_id_type=MESH)
    swaps = [swap(0, I["tokens"].at[1 - y_], B["x"].at[:, mine]), swap(1, I["gtp"], B["gains"].at[:, mine]), swap(2, I["cotangent"].at[1 - y_], B["g"].at[:, mine])]
    swaps[0].start(); swaps[1].start()
    owns[0].wait(); owns[1].wait()
    gat.send_z(0)
    def flip(i):
        tcopies[i].wait()
        B["tout"][i] = B["tin"][i].T.reshape(B["tout"].shape[1:])
        owns[tsrc[i][0]].start()
    flip(0)
    owns[2].wait(); owns[3].wait()
    gat.send_z(1)
    for i in range(1, 6): flip(i)
    for w in (4, 5, 6, 7): owns[w].wait()
    gat.send_z(2)
    for i in range(5): loc[i].wait()
    swaps[0].wait_recv(); swaps[1].wait_recv()
    ga, gm, gs = B["gains"].at[pl.ds(0, 1)], B["gains"].at[pl.ds(1, 1)], B["gs"]
    norm_into(B["h"], B["x"], ga)
    puts = []
    def put(name, src=None):
        cp = pltpu.make_async_copy(B[name] if src is None else src, O[name], osem.at[len(puts)])
        cp.start(); puts.append(cp)
    put("x"); put("h"); put("gains")
    gat.stage_y(0)
    gat.send_z(3)
    gat.stage_x(0); gat.stage_y(1)
    for w in range(8, 16): owns[w].wait()
    gat.send_z(4)
    gat.stage_y(2); gat.stage_x(1)
    gat.stage_k(0)
    gat.send_z(5)
    gat.stage_y(3); gat.stage_x(2)
    gat.done(0)
    loads = [pltpu.make_async_copy(G.at[w], WB.at[w], wsem.at[w]) for w in range(8)]
    loads[0].start(); loads[1].start()
    kv, kvp, s = B["kv"], B["kvp"], B["s"]
    kcopy = [pltpu.make_async_remote_copy(src_ref=kv.at[i], dst_ref=kvp.at[i], send_sem=ksem.at[i], recv_sem=krem.at[i],
             device_id=dev(r + 1), device_id_type=MESH) for i in range(2)]
    for i in range(2):
        loads[i].wait()
        kv[i] = nn(B["h"][...], W(i)).astype(BF16)
    gat.send_z(6)
    put("kv")
    gat.stage_k(1)
    gat.stage_y(4); gat.stage_x(3)
    gat.send_z(7)
    swaps[2].start()
    gat.done(1)
    loads[2].start(); loads[3].start()
    @pl.when(r == 0)
    def _():
        s0copy.start()
        kvp[...] = jnp.zeros_like(kvp)
        s0copy.wait()
    loads[2].wait(); loads[3].wait()
    scopy = [pltpu.make_async_remote_copy(src_ref=B["ssend"].at[:, pl.ds(i * half, half)], dst_ref=s.at[:, pl.ds(i * half, half)],
             send_sem=ssem.at[i], recv_sem=srem.at[i], device_id=dev(r + 1), device_id_type=MESH) for i in range(2)]
    def state_in():
        @pl.when(r > 0)
        def _():
            for cp in scopy: cp.wait_recv()
        norm_into(B["n"], s, gs)
    def turn(t, _):
        @pl.when(r == t)
        def _():
            state_in()
            B["sq"][...] = nn(B["n"][...], W(2)).astype(BF16)
            attend_heads(state_parts(kv), B["sq"], B["zatt"], B["lses"], rows, 1, 8)
            for i in range(2):
                cs = pl.ds(i * half, half)
                zz = nt(B["zatt"][...], WB[3].reshape(D, D)[i * half:(i + 1) * half])
                B["z"][:, cs] = zz.astype(BF16)
                kr = B["keep"][:, cs]
                B["ssend"][:, cs] = (kr * s[:, cs].astype(F32) + (1.0 - kr) * zz).astype(BF16)
                scopy[i].start()
            for i in range(2): kcopy[i].start()
        @pl.when(t < 3)
        def _(): gat.stage_y(5 + t)
        gat.stage_x(4 + t)
        gat.stage_k(2 + t)
        return 0
    lax.fori_loop(0, nctx - 1, turn, 0)
    gat.done(2); gat.done(3)
    for w in range(4, 8): loads[w].start()
    gat.stage_x(7)
    loads[4].wait()
    B["q"][...] = nn(B["h"][...], W(4)).astype(BF16)
    gat.stage_k(5)
    @pl.when(r == nctx - 1)
    def _(): state_in()
    for name in ("s", "n", "sq", "zatt", "z", "lses", "q"): put(name)
    for i in range(2):
        loads[5 + i].wait()
        B["skv"][i] = nn(B["n"][...], W(5 + i)).astype(BF16)
    put("skv")
    @pl.when(r > 0)
    def _():
        for cp in kcopy: cp.wait_recv()
    put("kvp")
    attend_heads(token_parts(kvp, kv, B["skv"], r == 0, rows, 2), B["q"], B["att"], B["lse"], rows, 2, 4)
    put("att"); put("lse")
    gat.stage_k(6)
    loads[7].wait()
    B["y1"][...] = B["x"][...].astype(F32) + nt(B["att"][...], W(7))
    norm_into(B["m"], B["y1"], gm)
    gat.stage_k(7)
    swaps[2].wait_recv()
    m, g, a, du, u, da = B["m"], B["g"], B["a"], B["du"], B["u"], B["da"]
    def wl(j, i): return pltpu.make_async_copy(G.at[8 + 2 * j + i], WB.at[2 * lax.rem(j, 2) + i], wsem.at[2 * lax.rem(j, 2) + i])
    def dcopy(j, i): return pltpu.make_async_copy(WB.at[4 + 2 * lax.rem(j, 2) + i], O["Dc"].at[2 * j + i], dsem.at[2 * lax.rem(j, 2) + i])
    gat.done(4)
    wl(0, 0).start(); wl(0, 1).start()
    B["oacc"][...] = jnp.zeros_like(B["oacc"])
    B["macc"][...] = jnp.zeros_like(B["macc"])
    def slice_step(j, _):
        b = 2 * lax.rem(j, 2)
        wl(j, 0).wait(); wl(j, 1).wait()
        a[...] = nn(m[...], W(b))
        du[...] = nn(g[...], W(b + 1))
        def body(rs):
            av = a[rs, :]
            sq = av * av
            t = jnp.tanh(G1 * av * (1.0 + G3 * sq))
            u[rs, :] = (0.5 * av * (1.0 + t)).astype(BF16)
            dg = 0.5 * (1.0 + t) + 0.5 * av * (1.0 - t * t) * (G1 * (1.0 + 3.0 * G3 * sq))
            da[rs, :] = (dg * du[rs, :]).astype(BF16)
        rows_loop(rows, 32, body)
        @pl.when(j < 3)
        def _():
            gat.done(5 + j)
            wl(j + 1, 0).start(); wl(j + 1, 1).start()
        B["oacc"][...] += nt(u[...], W(b + 1))
        B["macc"][...] += nt(da[...], W(b))
        @pl.when(j >= 2)
        def _():
            dcopy(j - 2, 0).wait(); dcopy(j - 2, 1).wait()
        WB[4 + b] = tn(m[...], da[...]).astype(BF16).reshape(WB.shape[1:])
        dcopy(j, 0).start()
        WB[5 + b] = tn(g[...], u[...]).astype(BF16).reshape(WB.shape[1:])
        dcopy(j, 1).start()
        return 0
    lax.fori_loop(0, 4, slice_step, 0)
    B["gg"][...] = jnp.zeros_like(B["gg"])
    def last(rs):
        yv = B["y1"][rs, :]
        u[rs, :] = (yv + B["oacc"][rs, :]).astype(BF16)
        dv, dgain = norm_back_rows(yv, gm[...], B["macc"][rs, :])
        a[rs, :] = g[rs, :].astype(F32) + dv
        B["gg"][...] += fold8(dgain)
    rows_loop(rows, 32, last)
    put("out", u); put("gy1", a); put("gg")
    for j in (2, 3):
        for i in range(2): dcopy(j, i).wait()
    @pl.when(r < nctx - 1)
    def _():
        for cp in kcopy: cp.wait_send()
        for cp in scopy: cp.wait_send()
    def drains(g_, _):
        gat.drain(g_)
        return 0
    lax.fori_loop(0, 8, drains, 0)
    for sw in swaps: sw.wait_send()
    for cp in puts: cp.wait()

def forward_call(F, nctx, args):
    rows = args["tokens"].shape[1]
    blk = D // (4 * F)
    sh = lambda *s: jax.ShapeDtypeStruct(s, BF16)
    fl = lambda *s: jax.ShapeDtypeStruct(s, F32)
    R = sh(rows, D)
    R2 = sh(2, rows, D)
    L = fl(HEADS, 1, rows)
    mats = lambda n: sh(n, F, 2, 2, blk, D)
    shapes = dict(G=mats(16), Dc=mats(8), out=R, gg=fl(8, D), h=R, q=R, kv=R2, kvp=R2, skv=R2, n=R, s=R, sq=R, zatt=R, z=R, lse=L, lses=L, att=R, x=R, gy1=fl(rows, D), gains=fl(8, D))
    bufs = dict(x=R, g=R, h=R, q=R, kv=R2, kvp=R2, skv=R2, n=R, s=R, ssend=R, sq=R, zatt=R, z=R, att=R, m=R, u=R, da=R,
        y1=fl(rows, D), a=fl(rows, D), du=fl(rows, D), oacc=fl(rows, D), macc=fl(rows, D), lse=L, lses=L, gains=fl(8, D), gs=fl(1, D), gg=fl(8, D), keep=fl(1, D),
        tin=sh(6, D // 2, D // F), tout=sh(6, 2, 2, blk, D // 2), WB=mats(8))
    S = pltpu.SemaphoreType.DMA
    n = 8
    outs = pl.pallas_call(functools.partial(forward_kernel, F, nctx),
        out_shape=[shapes[k] for k in A_OUT],
        in_specs=[ANY] * len(A_IN), out_specs=[ANY] * len(A_OUT),
        scratch_shapes=[pltpu.VMEM(bufs[k].shape, bufs[k].dtype) for k in A_BUF]
            + [S((n, F - 1)), S((n, F - 1)), S((n, F)), S((n, F)), S((n, F - 1)), S((n, F - 1)), S((n, F)), S((n, F))]
            + [S((16,)), S((12,)), S((len(A_OUT),)), S((8,)), S((2,)), S((2,)), S((2,)), S((2,)), S((3,)), S((3,)), S((4,))],
        compiler_params=pltpu.CompilerParams(collective_id=1, has_side_effects=True, vmem_limit_bytes=62 << 20), name="forward")(*[args[k] for k in A_IN])
    return dict(zip(A_OUT, outs))


BACK_IN = ("h", "q", "kv", "kvp", "skv", "n", "s", "sq", "zatt", "z", "lse", "lses", "att", "x", "gy1")

def attend_heads_back(parts_of, q, datt, lse, dq, sink, rows, chunks, unroll):
    step = rows // chunks
    def one(h):
        cs = head_cols(h)
        sums = None
        for qc in range(chunks):
            rs = pl.ds(qc * step, step)
            qh = q[rs, cs]
            gh = datt[rs, cs]
            ls = lse[h, :, pl.ds(qc * step, step)]
            parts = parts_of(cs, qc)
            ps = [jnp.exp2(p[2](nt(p[0](), qh)) * CE - ls) for p in parts]
            dps = [nt(p[1](), gh) for p in parts]
            delta = functools.reduce(jnp.add, [jnp.sum(a * b, axis=0, keepdims=True) for a, b in zip(ps, dps)])
            dss = [(a * (b - delta)).astype(BF16) for a, b in zip(ps, dps)]
            dq[rs, cs] = (functools.reduce(jnp.add, [tn(d, p[0]()) for d, p in zip(dss, parts)]) * SCALE).astype(dq.dtype)
            new = [(nn(d, qh), nn(a.astype(BF16), gh)) for a, d in zip(ps, dss)]
            if sums is None: sums = new
            else:
                merged = []
                for (k0, v0), (k1, v1) in zip(sums, new):
                    n0 = k0.shape[0]
                    if n0 < k1.shape[0]:
                        k1 = jnp.concatenate([k0 + k1[:n0], k1[n0:]], axis=0)
                        v1 = jnp.concatenate([v0 + v1[:n0], v1[n0:]], axis=0)
                    else:
                        k1, v1 = k0 + k1, v0 + v1
                    merged.append((k1, v1))
                sums = merged
        for i, (dk, dv) in enumerate(sums): sink(i, cs, dk * SCALE, dv)
    over_heads(one, unroll)

def back_kernel(nctx, F, G, gains, gs, keep, *refs):
    ins = dict(zip(BACK_IN, refs[:15]))
    Dg, gx, gg, ds0 = refs[15:19]
    nb = 19
    bufs = dict(zip(BACK_IN, refs[nb:nb + 15]))
    (WB, do, datt, dqb, dkv, dsend, dret, dskv, dntok, dsin, dsout, stage, ggv,
     wsem, isem, dsem, psem, prem, csem, crem, fsem) = refs[nb + 15:]
    f = lax.axis_index("fsdp"); r = lax.axis_index("ctx"); t = lax.axis_index("tp")
    dev = lambda c: (f, c, t)
    B = bufs
    rows = do.shape[0]
    order = ("gy1", "att", "q", "kv", "kvp", "skv", "lse", "n", "s", "sq", "zatt", "z", "lses", "h", "x")
    loads = {k: pltpu.make_async_copy(ins[k], bufs[k], isem.at[i]) for i, k in enumerate(order)}
    slots = ((7, 0), (5, 1), (6, 2), (3, 3), (2, 4), (4, 0), (0, 1), (1, 2))
    wload = {w: pltpu.make_async_copy(G.at[w], WB.at[sl], wsem.at[i]) for i, (w, sl) in enumerate(slots)}
    slot = dict(slots)
    W = lambda w: WB[slot[w]].reshape(D, D)
    loads["gy1"].start()
    wload[7].start()
    for k in order[1:]: loads[k].start()
    for w in (5, 6, 3, 2): wload[w].start()
    chain_barrier(r, nctx, dev)
    ga = gains.at[pl.ds(0, 1)]
    ggv[...] = jnp.zeros_like(ggv)
    loads["gy1"].wait()
    def cast(rs): do[rs, :] = B["gy1"][rs, :].astype(BF16)
    rows_loop(rows, 64, cast)
    wload[7].wait()
    datt[...] = nn(do[...], W(7)).astype(BF16)
    wload[4].start()
    for k in order[1:7]: loads[k].wait()
    def sink(i, cs, dk, dv):
        dst = (dsend, dkv, dskv)[i]
        dst[0, :, cs] = dk.astype(dst.dtype)
        dst[1, :, cs] = dv.astype(dst.dtype)
    attend_heads_back(token_parts(B["kvp"], B["kv"], B["skv"], r == 0, rows, 2), B["q"], datt, B["lse"], dqb, sink, rows, 2, 2)
    pcopy = pltpu.make_async_remote_copy(src_ref=dsend, dst_ref=dret, send_sem=psem.at[0], recv_sem=prem.at[0], device_id=dev(r - 1), device_id_type=MESH)
    @pl.when(r > 0)
    def _(): pcopy.start()
    wload[5].wait(); wload[6].wait()
    dntok[...] = nt(dskv[0], W(5)) + nt(dskv[1], W(6))
    wload[0].start(); wload[1].start()
    for k in order[7:9]: loads[k].wait()
    half = rows // 2
    ccopy = [pltpu.make_async_remote_copy(src_ref=dsout.at[pl.ds(i * half, half)], dst_ref=dsin.at[pl.ds(i * half, half)],
             send_sem=csem.at[i], recv_sem=crem.at[i], device_id=dev(r - 1), device_id_type=MESH) for i in range(2)]
    def finish_state(extra):
        for i in range(2):
            def body(j, _):
                rs = pl.ds(pl.multiple_of(i * half + j * 32, 32), 32)
                dv, dgain = norm_back_rows(B["s"][rs, :].astype(F32), gs[...], dntok[rs, :])
                if extra: dv = dv + keep[...] * dsin[rs, :].astype(F32)
                dsout[rs, :] = dv.astype(BF16)
                ggv[pl.ds(8, 8), :] += fold8(dgain)
                return 0
            lax.fori_loop(0, half // 32, body, 0)
            @pl.when(r > 0)
            def _(): ccopy[i].start()
    @pl.when(r == nctx - 1)
    def _(): finish_state(False)
    dcopies = []
    state = {"n": 0}
    def grad_out(w, left, right, ready=None):
        i = state["n"]; state["n"] += 1
        sl = i % 3
        if i >= 3: dcopies[i - 3].wait()
        stage[sl] = tn(left[...], right[...]).astype(BF16).reshape(stage.shape[1:])
        cp = pltpu.make_async_copy(stage.at[sl], Dg.at[w], dsem.at[i])
        cp.start(); dcopies.append(cp)
    loads["h"].wait()
    grad_out(7, do, B["att"])
    grad_out(5, B["n"], dskv.at[0])
    grad_out(6, B["n"], dskv.at[1])
    grad_out(4, B["h"], dqb)
    for k in order[9:13]: loads[k].wait()
    wload[3].wait(); wload[2].wait()
    dzb, dza, dsq = datt, dqb, do
    dh = dntok
    wload[4].wait()
    dhq = B["q"]
    @pl.when(r < nctx - 1)
    def _():
        for cp in ccopy: cp.wait_recv()
        def body(rs):
            d = dsin[rs, :].astype(F32)
            kr = keep[...]
            dzb[rs, :] = ((1.0 - kr) * d).astype(BF16)
            ggv[pl.ds(16, 8), :] += fold8(d * (B["s"][rs, :].astype(F32) - B["z"][rs, :].astype(F32)) * kr * (1.0 - kr))
        rows_loop(rows, 32, body)
        do[...] = nn(dzb[...], W(3)).astype(BF16)
        def sink2(i, cs, dk, dv):
            dkv[0, :, cs] += dk
            dkv[1, :, cs] += dv
        attend_heads_back(state_parts(B["kv"]), B["sq"], do, B["lses"], B["q"], sink2, rows, 1, 4)
        dntok[...] += nt(B["q"][...], W(2))
        finish_state(True)
    @pl.when(r == nctx - 1)
    def _():
        B["q"][...] = jnp.zeros_like(B["q"])
        dzb[...] = jnp.zeros_like(dzb)
        B["zatt"][...] = jnp.zeros_like(B["zatt"])
    @pl.when(r == 0)
    def _():
        cp = pltpu.make_async_copy(dsout, ds0, fsem.at[0]); cp.start(); cp.wait()
    @pl.when(r > 0)
    def _():
        dsin[...] = jnp.zeros_like(dsin)
        cp = pltpu.make_async_copy(dsin, ds0, fsem.at[0]); cp.start(); cp.wait()
    grad_out(2, B["n"], B["q"])
    grad_out(3, dzb, B["zatt"])
    @pl.when(r < nctx - 1)
    def _(): pcopy.wait_recv()
    @pl.when(r == nctx - 1)
    def _(): dret[...] = jnp.zeros_like(dret)
    dkvb = B["kvp"]
    for i in range(2):
        def add(rs): dkvb[i, rs, :] = (dkv[i, rs, :] + dret[i, rs, :].astype(F32)).astype(BF16)
        rows_loop(rows, 32, add)
    grad_out(0, B["h"], dkvb.at[0])
    grad_out(1, B["h"], dkvb.at[1])
    wload[0].wait(); wload[1].wait()
    loads["x"].wait()
    dntok[...] = nt(dqb[...], W(4)) + nt(dkvb[0], W(0)) + nt(dkvb[1], W(1))
    gxb = B["att"]
    def last(rs):
        dv, dgain = norm_back_rows(B["x"][rs, :].astype(F32), ga[...], dntok[rs, :])
        gxb[rs, :] = (B["gy1"][rs, :] + dv).astype(BF16)
        ggv[pl.ds(0, 8), :] += fold8(dgain)
    rows_loop(rows, 32, last)
    cps = [pltpu.make_async_copy(gxb, gx, fsem.at[1]), pltpu.make_async_copy(ggv, gg, fsem.at[2])]
    for cp in cps: cp.start()
    for cp in dcopies[-3:]: cp.wait()
    for cp in cps: cp.wait()
    @pl.when(r > 0)
    def _():
        pcopy.wait_send()
        for cp in ccopy: cp.wait_send()

def back_call(nctx, F, gs, keep, vals):
    rows = vals["h"].shape[0]
    blk = D // (4 * F)
    V = lambda *s: pltpu.VMEM(s, BF16)
    VF = lambda *s: pltpu.VMEM(s, F32)
    S = pltpu.SemaphoreType.DMA
    vm = pl.BlockSpec(memory_space=pltpu.VMEM)
    args = [vals[k] for k in BACK_IN]
    return pl.pallas_call(functools.partial(back_kernel, nctx, F),
        out_shape=[jax.ShapeDtypeStruct((8, F, 2, 2, blk, D), BF16), jax.ShapeDtypeStruct((rows, D), BF16),
                   jax.ShapeDtypeStruct((24, D), F32), jax.ShapeDtypeStruct((rows, D), BF16)],
        in_specs=[ANY, vm, vm, vm] + [ANY] * 15, out_specs=[ANY] * 4,
        scratch_shapes=[pltpu.VMEM(a.shape, a.dtype) for a in args] + [
            V(5, F, 2, 2, blk, D), V(rows, D), V(rows, D), V(rows, D), VF(2, rows, D), V(2, rows, D), V(2, rows, D), V(2, rows, D), VF(rows, D), V(rows, D), V(rows, D),
            V(3, F, 2, 2, blk, D), VF(24, D),
            S((8,)), S((15,)), S((8,)), S((1,)), S((1,)), S((2,)), S((2,)), S((3,))],
        compiler_params=pltpu.CompilerParams(collective_id=4, has_side_effects=True, vmem_limit_bytes=62 << 20),
        cost_estimate=pl.CostEstimate(flops=120 << 30, bytes_accessed=60 << 20, transcendentals=8 << 20), name="back")(vals["G"], vals["gains"], gs, keep, *args)


def add_into(dst, src, lead, rows, cols=None):
    total = 1
    for n in lead: total *= n
    def body(i, _):
        idx = []
        r = i
        for n in reversed(lead):
            idx.append(lax.rem(r, n))
            r = lax.div(r, n)
        idx = tuple(reversed(idx))
        dst[idx] = (dst[idx].astype(F32) + src[idx].astype(F32)).astype(dst.dtype)
        return 0
    lax.fori_loop(0, total, body, 0)

def reduce_kernel(F, W, flags, D_, R, RX, A, KB, B1, B2, ZB, lo, ld, ks, kr, s1, r1, s2, r2, zs, zr, bs, br, fs, fr):
    z, x, k, y = where_am_i()
    c = x * 2 + k
    def rc(src, dst, s, r, dev):
        return pltpu.make_async_remote_copy(src_ref=src, dst_ref=dst, send_sem=s, recv_sem=r, device_id=dev, device_id_type=MESH)
    loads = [pltpu.make_async_copy(D_.at[j, :, :, k], A.at[j], ld.at[j]) for j in range(W)]
    for l in loads: l.start()
    barrier_with(F, 7)
    xdev = (z, (1 - x) * 2 + k, y)
    ydev = (z, c, 1 - y)
    kdev = (z, x * 2 + 1 - k, y)
    ddev = (z, (1 - x) * 2 + 1 - k, y)
    mine, other = cols_of(y), cols_of(1 - y)
    kc = [rc(D_.at[j, :, :, 1 - k], KB.at[j], ks.at[j], kr.at[j], kdev) for j in range(W)]
    for cp in kc: cp.start()
    nx = W // 2
    def first(j):
        if j % 2 == 0: return rc(A.at[j, :, 1 - x], B1[0].at[j // 2], s1.at[j], r1.at[j], xdev)
        return rc(A.at[j, :, :, :, other], B1[1].at[j // 2], s1.at[j], r1.at[j], ydev)
    def second(j):
        if j % 2 == 0: return rc(A.at[j, :, x, :, other], B2.at[j], s2.at[j], r2.at[j], ydev)
        return rc(A.at[j, :, 1 - x, :, mine], B2.at[j], s2.at[j], r2.at[j], xdev)
    def zcopy(j, d):
        to = lax.rem(z - (d + 1) + F, F)
        return rc(A.at[j, to, x, :, mine], ZB.at[j, d], zs.at[j, d], zr.at[j, d], (to, c, y))
    def bcopy(j, i): return rc(R.at[j, c], R.at[j, c], bs.at[j, i], br.at[j, i], (kdev, xdev, ddev)[i])
    def fcopy(fi, j, i): return rc(R.at[j, c], RX.at[fi, c], fs.at[fi, i], fr.at[fi, i], (z, lax.rem(c + i, 4), 1 - y))
    def plus(a, b): return (a.astype(F32) + b.astype(F32)).astype(BF16)
    for t in range(W + 3):
        j = t
        if j < W:
            loads[j].wait()
            kc[j].wait_recv()
            add_into(A.at[j], KB.at[j], (F, 2), None)
            first(j).start()
        j = t - 1
        if 0 <= j < W:
            first(j).wait_recv()
            if j % 2 == 0:
                def body(i, _):
                    A[j, i, x] = plus(A[j, i, x], B1[0][j // 2, i])
                    return 0
                lax.fori_loop(0, F, body, 0)
            else:
                def body(i, _):
                    for xx in range(2):
                        A[j, i, xx, :, mine] = plus(A[j, i, xx, :, mine], B1[1][j // 2, i, xx])
                    return 0
                lax.fori_loop(0, F, body, 0)
            second(j).start()
        j = t - 2
        if 0 <= j < W:
            second(j).wait_recv()
            def body2(i, _):
                A[j, i, x, :, mine] = plus(A[j, i, x, :, mine], B2[j, i])
                return 0
            lax.fori_loop(0, F, body2, 0)
            for d in range(F - 1): zcopy(j, d).start()
        j = t - 3
        if 0 <= j < W:
            total = A[j, z, x, :, mine].astype(F32)
            for d in range(F - 1):
                zcopy(j, d).wait_recv()
                total = total + ZB[j, d].astype(F32)
            lo[j] = total.astype(lo.dtype)
            own = pltpu.make_async_copy(lo.at[j], R.at[j, c], ld.at[j])
            own.start()
            own.wait()
            for i in range(3): bcopy(j, i).start()
            if j in flags:
                for i in range(4): fcopy(flags.index(j), j, i).start()
    for j in range(W):
        kc[j].wait_send()
        first(j).wait_send()
        second(j).wait_send()
        for d in range(F - 1): zcopy(j, d).wait_send()
        for i, (a, b) in enumerate(((0, 1), (1, 0), (1, 1))):
            bcopy(j, i).wait_send()
            rr = R.at[j, lax.rem(x + a, 2) * 2 + lax.rem(k + b, 2)]
            pltpu.make_async_copy(rr, rr, br.at[j, i]).wait()
    for fi, j in enumerate(flags):
        for i in range(4):
            fcopy(fi, j, i).wait_send()
            rr = RX.at[fi, lax.rem(c - i + 4, 4)]
            pltpu.make_async_copy(rr, rr, fr.at[fi, i]).wait()

def reduce_entry(F, W, flags, D_, R, RX, A, KB, B1x, B1y, *rest):
    reduce_kernel(F, W, flags, D_, R, RX, A, KB, (B1x, B1y), *rest)

def reduce_call(F, Dm, flags, cid, name):
    W, _, _, _, rows, _ = Dm.shape
    half = D // 2
    S = pltpu.SemaphoreType.DMA
    nf = max(1, len(flags))
    V = lambda *s: pltpu.VMEM(s, Dm.dtype)
    return pl.pallas_call(functools.partial(reduce_entry, F, W, flags),
        out_shape=(jax.ShapeDtypeStruct((W, 4, rows, half), Dm.dtype), jax.ShapeDtypeStruct((nf, 4, rows, half), Dm.dtype)),
        in_specs=[ANY], out_specs=[ANY] * 2,
        scratch_shapes=[V(W, F, 2, rows, D), V(W, F, 2, rows, D), V(W // 2, F, rows, D), V(W // 2, F, 2, rows, half), V(W, F, rows, half), V(W, F - 1, rows, half), V(W, rows, half),
            S((W,)), S((W,)), S((W,)), S((W,)), S((W,)), S((W,)), S((W,)), S((W, F - 1)), S((W, F - 1)), S((W, 3)), S((W, 3)), S((nf, 4)), S((nf, 4))],
        compiler_params=pltpu.CompilerParams(collective_id=cid, has_side_effects=True, vmem_limit_bytes=60 << 20), name=name)(Dm)


def local(
    tokens,
    cotangent,
    w_query,
    w_key,
    w_value,
    w_out,
    w_state_key,
    w_state_value,
    w_state_query,
    w_state_out,
    w_up,
    w_down,
    gain_attn,
    gain_state,
    gain_mlp,
    forget_logit,
    state_init,
):
    fsdp = lax.axis_size("fsdp")
    tp_rank = lax.axis_index("tp")
    ctx_count = lax.axis_size("ctx")
    half = D // 2
    rows = D // fsdp
    blk = rows // 4
    tiles = lambda w: w.reshape(2, 2, blk, w.shape[1])
    args = dict(
        tokens=tokens, cotangent=cotangent, gtp=jnp.pad(jnp.stack([gain_attn, gain_mlp]), ((0, 6), (0, 0))),
        gstate=gain_state[None], keep=jax.nn.sigmoid(forget_logit)[None], s0=state_init,
        key=tiles(w_key), value=tiles(w_value), squery=tiles(w_state_query), sout=w_state_out, query=tiles(w_query),
        skey=tiles(w_state_key), svalue=tiles(w_state_value), out=w_out, up=tiles(w_up), down=w_down)
    vals = forward_call(fsdp, ctx_count, args)
    out = vals["out"]
    grads, gx, sums, ds0 = back_call(ctx_count, fsdp, args["gstate"], args["keep"], vals)
    r, rx = reduce_call(fsdp, grads, (2, 3), 2, "reduce_attn")
    rm, _ = reduce_call(fsdp, vals["Dc"], (), 5, "reduce_mlp")
    r = r.reshape(8, rows, half).astype(F32)
    rx = rx.reshape(2, rows, half).astype(F32)
    rm = rm.reshape(8, rows, half).astype(F32)

    def both(mine, other):
        first = jnp.where(tp_rank == 0, mine, other)
        second = jnp.where(tp_rank == 0, other, mine)
        return jnp.concatenate([first, second], axis=1)

    def swapped(value):
        parts = value.reshape(value.shape[0], 2, half).swapaxes(0, 1)
        mine = lax.dynamic_index_in_dim(parts, tp_rank, 0, False)
        sent = lax.dynamic_index_in_dim(parts, 1 - tp_rank, 0, False)
        got = lax.ppermute(sent, "tp", [(0, 1), (1, 0)])
        return jnp.where(tp_rank == 0, jnp.stack([mine, got]), jnp.stack([got, mine]))

    small = jnp.concatenate([sums, vals["gg"]], axis=0).reshape(4, 8, D).sum(axis=1)
    small = lax.psum(small, ("fsdp", "ctx", "tp"))
    start = lax.psum(ds0, ("fsdp", "ctx", "tp")).astype(F32)
    at = lambda i: lax.dynamic_slice_in_dim(small[i], tp_rank * half, half, 0)
    return (
        swapped(out),
        swapped(gx),
        r[4],
        r[0],
        r[1],
        r[7].T,
        r[5],
        r[6],
        both(r[2], rx[0]),
        both(r[3], rx[1]).T,
        rm[0::2].swapaxes(0, 1).reshape(rows, -1),
        rm[1::2].swapaxes(1, 2).reshape(-1, rows),
        at(0),
        small[1],
        at(3),
        small[2],
        start,
    )


def solution(mesh):
    placed = (
        P("fsdp", "ctx", "tp"),
        P("fsdp", "ctx", "tp"),
        P("fsdp", "tp"),
        P("fsdp", "tp"),
        P("fsdp", "tp"),
        P("tp", "fsdp"),
        P("fsdp", "tp"),
        P("fsdp", "tp"),
        P("fsdp", None),
        P(None, "fsdp"),
        P("fsdp", "tp"),
        P("tp", "fsdp"),
        P("tp"),
        P(),
        P("tp"),
        P(),
        P(),
    )
    return jax.shard_map(
        local,
        mesh=mesh,
        in_specs=placed,
        out_specs=(
            P("fsdp", "ctx", "tp"),
            P("fsdp", "ctx", "tp"),
            P("fsdp", "tp"),
            P("fsdp", "tp"),
            P("fsdp", "tp"),
            P("tp", "fsdp"),
            P("fsdp", "tp"),
            P("fsdp", "tp"),
            P("fsdp", None),
            P(None, "fsdp"),
            P("fsdp", "tp"),
            P("tp", "fsdp"),
            P("tp"),
            P(),
            P("tp"),
            P(),
            P(),
        ),
        check_vma=False,
    )
```

```python
import functools

import jax
import jax.numpy as jnp
from jax import lax
from jax.experimental import pallas as pl
from jax.experimental.pallas import tpu as pltpu
from jax.sharding import PartitionSpec as P

MESH = pl.DeviceIdType.MESH
ANY = pl.BlockSpec(memory_space=pl.ANY)
D = 1024
HEADS = 8
HEAD = 128
EPS = 1e-06
NEG = -1e30
LOG2E = 1.4426950408889634
F32 = jnp.float32
BF16 = jnp.bfloat16
SCALE = HEAD ** -0.5
CE = SCALE * LOG2E

def nn(a, b): return lax.dot_general(a, b, (((1,), (0,)), ((), ())), preferred_element_type=F32)
def nt(a, b): return lax.dot_general(a, b, (((1,), (1,)), ((), ())), preferred_element_type=F32)
def tn(a, b): return lax.dot_general(a, b, (((0,), (0,)), ((), ())), preferred_element_type=F32)

def rows_loop(total, step, body):
    def run(i, _):
        body(pl.ds(pl.multiple_of(i * step, step), step))
        return 0
    lax.fori_loop(0, total // step, run, 0)

def inverse_of(v):
    return lax.rsqrt(jnp.mean(v * v, axis=-1, keepdims=True) + EPS)

def norm_into(dst, src, gain):
    def body(rs):
        v = src[rs, :].astype(F32)
        dst[rs, :] = (v * inverse_of(v) * gain[...]).astype(dst.dtype)
    rows_loop(src.shape[0], 32, body)

def head_cols(h): return pl.ds(pl.multiple_of(h * HEAD, HEAD), HEAD)

def causal_scores(s, first_key, first_query):
    keys = lax.broadcasted_iota(jnp.int32, s.shape, 0) + first_key
    qs = lax.broadcasted_iota(jnp.int32, s.shape, 1) + first_query
    return jnp.where(keys <= qs, s, NEG)

def over_heads(one, unroll, h0, count):
    def body(i, _):
        for u in range(unroll):
            one(h0 + i * unroll + u)
        return 0
    lax.fori_loop(0, count // unroll, body, 0)

def attend_heads(parts_of, q, out, lse, rows, chunks, unroll):
    step = rows // chunks
    def one(h):
        cs = head_cols(h)
        for qc in range(chunks):
            rs = pl.ds(qc * step, step)
            qh = q[rs, cs]
            parts = parts_of(cs, qc)
            scores = [mask(nt(keys(), qh)) for keys, values, mask in parts]
            big = functools.reduce(jnp.maximum, [jnp.max(s, axis=0, keepdims=True) for s in scores])
            es = [jnp.exp2((s - big) * CE) for s in scores]
            total = functools.reduce(jnp.add, [jnp.sum(e, axis=0, keepdims=True) for e in es])
            inv = 1.0 / total
            acc = functools.reduce(jnp.add, [tn((e * inv).astype(BF16), p[1]()) for e, p in zip(es, parts)])
            out[rs, cs] = acc.astype(BF16)
            lse[h, :, pl.ds(qc * step, step)] = big * CE + jnp.log2(total)
    over_heads(one, unroll, 0, HEADS)

def token_parts(kvp, kv, skv, first, rows, chunks):
    def parts_of(cs, qc):
        step = rows // chunks
        upto = (qc + 1) * step
        same = lambda s: s
        earlier = lambda s: jnp.where(first, NEG, s)
        causal = lambda s: causal_scores(s, 0, qc * step)
        return [(lambda: kvp[0, :, cs], lambda: kvp[1, :, cs], earlier),
                (lambda: kv[0, pl.ds(0, upto), cs], lambda: kv[1, pl.ds(0, upto), cs], causal),
                (lambda: skv[0, :, cs], lambda: skv[1, :, cs], same)]
    return parts_of

def state_parts(kv):
    def parts_of(cs, qc):
        return [(lambda: kv[0, :, cs], lambda: kv[1, :, cs], lambda s: s)]
    return parts_of

def chain_barrier(r, n, dev):
    bar = pltpu.get_barrier_semaphore()
    @pl.when(r > 0)
    def _(): pl.semaphore_signal(bar, inc=1, device_id=dev(r - 1), device_id_type=MESH)
    @pl.when(r < n - 1)
    def _(): pl.semaphore_signal(bar, inc=1, device_id=dev(r + 1), device_id_type=MESH)
    pl.semaphore_wait(bar, jnp.where(r > 0, 1, 0) + jnp.where(r < n - 1, 1, 0))

def where_am_i():
    f = lax.axis_index("fsdp")
    c = lax.axis_index("ctx")
    return f, lax.div(c, 2), lax.rem(c, 2), lax.axis_index("tp")

def cols_of(t):
    return pl.ds(pl.multiple_of(t * (D // 2), D // 2), D // 2)

G1 = 0.7978845608028654
G3 = 0.044715

def norm_back_rows(v, gain, e):
    inv = inverse_of(v)
    w = e * gain
    proj = jnp.sum(w * v, axis=-1, keepdims=True) * (1.0 / D)
    return inv * w - v * (inv * inv * inv) * proj, e * v * inv

def fold8(v):
    return functools.reduce(jnp.add, [v[i * 8:(i + 1) * 8] for i in range(v.shape[0] // 8)])

def attend_heads_back(parts_of, q, datt, lse, dq, sink, rows, chunks, unroll, h0, count):
    step = rows // chunks
    def one(h):
        cs = head_cols(h)
        sums = None
        for qc in range(chunks):
            rs = pl.ds(qc * step, step)
            qh = q[rs, cs]
            gh = datt[rs, cs]
            ls = lse[h, :, pl.ds(qc * step, step)]
            parts = parts_of(cs, qc)
            ps = [jnp.exp2(p[2](nt(p[0](), qh)) * CE - ls) for p in parts]
            dps = [nt(p[1](), gh) for p in parts]
            delta = functools.reduce(jnp.add, [jnp.sum(a * b, axis=0, keepdims=True) for a, b in zip(ps, dps)])
            dss = [(a * (b - delta)).astype(BF16) for a, b in zip(ps, dps)]
            dq[rs, cs] = (functools.reduce(jnp.add, [tn(d, p[0]()) for d, p in zip(dss, parts)]) * SCALE).astype(dq.dtype)
            new = [(nn(d, qh), nn(a.astype(BF16), gh)) for a, d in zip(ps, dss)]
            if sums is None: sums = new
            else:
                merged = []
                for (k0, v0), (k1, v1) in zip(sums, new):
                    n0 = k0.shape[0]
                    if n0 < k1.shape[0]:
                        k1 = jnp.concatenate([k0 + k1[:n0], k1[n0:]], axis=0)
                        v1 = jnp.concatenate([v0 + v1[:n0], v1[n0:]], axis=0)
                    else:
                        k1, v1 = k0 + k1, v0 + v1
                    merged.append((k1, v1))
                sums = merged
        for i, (dk, dv) in enumerate(sums): sink(i, cs, dk * SCALE, dv)
    over_heads(one, unroll, h0, count)


class Gather:
    def __init__(self, G, F, sems):
        self.G, self.F, self.sems = G, F, sems
        self.z, self.x, self.k, self.y = where_am_i()

    def src_z(self, d):
        return lax.rem(self.z + d + 1, self.F)

    def region(self, g, z, x, k, cols=None):
        w = pl.ds(2 * g, 2)
        if cols is None:
            return self.G.at[w, z, x, k]
        return self.G.at[w, z, x, k, :, cols]

    def both_x(self, g, z, k, cols=None):
        w = pl.ds(2 * g, 2)
        if cols is None:
            return self.G.at[w, z, :, k]
        return self.G.at[w, z, :, k, :, cols]

    def remote(self, ref, i, g, d, dev):
        return pltpu.make_async_remote_copy(
            src_ref=ref, dst_ref=ref, send_sem=self.sems[i].at[g, d], recv_sem=self.sems[i + 1].at[g, d],
            device_id=dev, device_id_type=MESH)

    def landed(self, ref, i, g, d):
        pltpu.make_async_copy(ref, ref, self.sems[i + 1].at[g, d]).wait()

    def zcopy(self, g, d):
        to = lax.rem(self.z - (d + 1) + self.F, self.F)
        return self.remote(self.region(g, self.z, self.x, self.k, cols_of(self.y)), 0, g, d, (to, self.x * 2 + self.k, self.y))

    def ycopy(self, g, d):
        dev = (self.z, self.x * 2 + self.k, 1 - self.y)
        if d == self.F - 1:
            return self.remote(self.both_x(g, self.z, self.k, cols_of(self.y)), 2, g, d, dev)
        return self.remote(self.region(g, self.src_z(d), self.x, self.k, cols_of(self.y)), 2, g, d, dev)

    def xcopy(self, g, d):
        return self.remote(self.region(g, self.src_z(d), self.x, self.k), 4, g, d, (self.z, (1 - self.x) * 2 + self.k, self.y))

    def kcopy(self, g, d):
        dev = (self.z, self.x * 2 + 1 - self.k, self.y)
        if d == self.F - 1:
            return self.remote(self.both_x(g, self.z, self.k, cols_of(1 - self.y)), 6, g, d, dev)
        return self.remote(self.both_x(g, self.src_z(d), self.k), 6, g, d, dev)

    def send_z(self, g):
        for d in range(self.F - 1):
            self.zcopy(g, d).start()
        self.ycopy(g, self.F - 1).start()

    def stage_y(self, g):
        for d in range(self.F - 1):
            self.landed(self.region(g, self.src_z(d), self.x, self.k, cols_of(self.y)), 0, g, d)
            self.ycopy(g, d).start()

    def stage_x(self, g):
        o = cols_of(1 - self.y)
        for d in range(self.F - 1):
            self.landed(self.region(g, self.src_z(d), self.x, self.k, o), 2, g, d)
            self.xcopy(g, d).start()
        self.landed(self.both_x(g, self.z, self.k, o), 2, g, self.F - 1)
        self.kcopy(g, self.F - 1).start()

    def stage_k(self, g):
        for d in range(self.F - 1):
            self.landed(self.region(g, self.src_z(d), 1 - self.x, self.k), 4, g, d)
            self.kcopy(g, d).start()

    def done(self, g):
        for d in range(self.F - 1):
            self.landed(self.both_x(g, self.src_z(d), 1 - self.k), 6, g, d)
        self.landed(self.both_x(g, self.z, 1 - self.k, cols_of(1 - self.y)), 6, g, self.F - 1)

    def drain(self, g):
        for d in range(self.F):
            if d < self.F - 1:
                self.zcopy(g, d).wait_send()
                self.xcopy(g, d).wait_send()
            self.ycopy(g, d).wait_send()
            self.kcopy(g, d).wait_send()

def barrier_with(F, count, across=False):
    z, x, k, y = where_am_i()
    bar = pltpu.get_barrier_semaphore()
    peers = [(lax.rem(z + d + 1, F), x * 2 + k, y) for d in range(F - 1)]
    for dx, dk, dy in ((0, 0, 1), (1, 0, 0), (0, 1, 0), (1, 1, 0), (1, 0, 1), (0, 1, 1), (1, 1, 1))[:count]:
        peers.append((z, lax.rem(x + dx, 2) * 2 + lax.rem(k + dk, 2), lax.rem(y + dy, 2)))
    if across:
        peers += [(lax.rem(z + d + 1, F), x * 2 + k, 1 - y) for d in range(F - 1)]
    for p in peers:
        pl.semaphore_signal(bar, inc=1, device_id=p, device_id_type=MESH)
    pl.semaphore_wait(bar, len(peers))

A_IN = ("tokens", "cotangent", "gtp", "gstate", "keep", "s0", "key", "value", "squery", "sout", "query", "skey", "svalue", "out", "up", "down")
A_OUT = ("G", "Dc", "out", "gg", "h", "q", "kv", "kvp", "skv", "n", "s", "sq", "zatt", "z", "lse", "lses", "att", "x", "gy1", "gains")
A_BUF = ("x", "g", "h", "q", "kv", "kvp", "skv", "n", "s", "ssend", "sq", "zatt", "z", "att", "m", "u", "da", "y1", "a", "du", "oacc", "macc", "lse", "lses", "gains", "gs", "gg", "keep", "tin", "tout", "WB")

def forward_kernel(F, nctx, *refs):
    I = dict(zip(A_IN, refs)); at = len(A_IN)
    O = dict(zip(A_OUT, refs[at:])); at += len(A_OUT)
    B = dict(zip(A_BUF, refs[at:])); at += len(A_BUF)
    gsems = refs[at:at + 8]
    own, ins, osem, wsem, ksem, krem, ssem, srem, ysem, yrem, dsem = refs[at + 8:]
    z_, x_, k_, y_ = where_am_i()
    r = x_ * 2 + k_
    rows = B["x"].shape[0]
    half = D // 2
    dev = lambda c: (z_, c, y_)
    gat = Gather(O["G"], F, gsems)
    G = O["G"]
    mine = cols_of(y_)
    WB = B["WB"]
    W = lambda i: WB[i].reshape(D, D)
    def place(w, ref): return pltpu.make_async_copy(ref, G.at[w, z_, :, :, :, mine], own.at[w])
    owns = {0: place(0, I["key"]), 1: place(1, I["value"]), 2: place(2, I["squery"].at[:, :, :, mine]), 4: place(4, I["query"]),
            5: place(5, I["skey"]), 6: place(6, I["svalue"])}
    for j in range(4):
        owns[8 + 2 * j] = place(8 + 2 * j, I["up"].at[:, :, :, pl.ds(j * half, half)])
    tcopies = []
    tsrc = [(3, I["sout"].at[mine]), (7, I["out"])] + [(9 + 2 * j, I["down"].at[pl.ds(j * half, half)]) for j in range(4)]
    for i, (w, ref) in enumerate(tsrc):
        tcopies.append(pltpu.make_async_copy(ref, B["tin"].at[i], ins.at[i]))
        owns[w] = place(w, B["tout"].at[i])
    for w in (0, 1, 2): owns[w].start()
    for c in tcopies: c.start()
    loc = [pltpu.make_async_copy(I["tokens"].at[y_], B["x"].at[:, mine], ins.at[6]),
           pltpu.make_async_copy(I["gtp"], B["gains"].at[:, mine], ins.at[7]),
           pltpu.make_async_copy(I["keep"], B["keep"], ins.at[8]),
           pltpu.make_async_copy(I["gstate"], B["gs"], ins.at[9]),
           pltpu.make_async_copy(I["cotangent"].at[y_], B["g"].at[:, mine], ins.at[10])]
    s0copy = pltpu.make_async_copy(I["s0"], B["s"], ins.at[11])
    for c in loc: c.start()
    for w in (4, 5, 6, 8, 10, 12, 14): owns[w].start()
    barrier_with(F, 4)
    pdev = (z_, r, 1 - y_)
    swap = lambda i, s, d: pltpu.make_async_remote_copy(src_ref=s, dst_ref=d, send_sem=ysem.at[i], recv_sem=yrem.at[i], device_id=pdev, device_id_type=MESH)
    swaps = [swap(0, I["tokens"].at[1 - y_], B["x"].at[:, mine]), swap(1, I["gtp"], B["gains"].at[:, mine]), swap(2, I["cotangent"].at[1 - y_], B["g"].at[:, mine])]
    swaps[0].start(); swaps[1].start()
    owns[0].wait(); owns[1].wait()
    gat.send_z(0)
    def flip(i):
        tcopies[i].wait()
        B["tout"][i] = B["tin"][i].T.reshape(B["tout"].shape[1:])
        owns[tsrc[i][0]].start()
    flip(0)
    owns[2].wait(); owns[3].wait()
    gat.send_z(1)
    for i in range(1, 6): flip(i)
    for w in (4, 5, 6, 7): owns[w].wait()
    gat.send_z(2)
    for i in range(5): loc[i].wait()
    swaps[0].wait_recv(); swaps[1].wait_recv()
    ga, gm, gs = B["gains"].at[pl.ds(0, 1)], B["gains"].at[pl.ds(1, 1)], B["gs"]
    norm_into(B["h"], B["x"], ga)
    puts = []
    def put(name, src=None):
        cp = pltpu.make_async_copy(B[name] if src is None else src, O[name], osem.at[len(puts)])
        cp.start(); puts.append(cp)
    put("x"); put("h"); put("gains")
    gat.stage_y(0)
    gat.send_z(3)
    gat.stage_x(0); gat.stage_y(1)
    for w in range(8, 16): owns[w].wait()
    gat.send_z(4)
    gat.stage_y(2); gat.stage_x(1)
    gat.stage_k(0)
    gat.send_z(5)
    gat.stage_y(3); gat.stage_x(2)
    gat.done(0)
    loads = [pltpu.make_async_copy(G.at[w], WB.at[w], wsem.at[w]) for w in range(8)]
    loads[0].start(); loads[1].start()
    kv, kvp, s = B["kv"], B["kvp"], B["s"]
    kcopy = [pltpu.make_async_remote_copy(src_ref=kv.at[i], dst_ref=kvp.at[i], send_sem=ksem.at[i], recv_sem=krem.at[i],
             device_id=dev(r + 1), device_id_type=MESH) for i in range(2)]
    for i in range(2):
        loads[i].wait()
        kv[i] = nn(B["h"][...], W(i)).astype(BF16)
    gat.send_z(6)
    put("kv")
    gat.stage_k(1)
    gat.stage_y(4); gat.stage_x(3)
    gat.send_z(7)
    swaps[2].start()
    gat.done(1)
    loads[2].start(); loads[3].start()
    @pl.when(r == 0)
    def _():
        s0copy.start()
        kvp[...] = jnp.zeros_like(kvp)
        s0copy.wait()
    loads[2].wait(); loads[3].wait()
    scopy = [pltpu.make_async_remote_copy(src_ref=B["ssend"].at[:, pl.ds(i * half, half)], dst_ref=s.at[:, pl.ds(i * half, half)],
             send_sem=ssem.at[i], recv_sem=srem.at[i], device_id=dev(r + 1), device_id_type=MESH) for i in range(2)]
    def state_in():
        @pl.when(r > 0)
        def _():
            for cp in scopy: cp.wait_recv()
        norm_into(B["n"], s, gs)
    def turn(t, _):
        @pl.when(r == t)
        def _():
            state_in()
            B["sq"][...] = nn(B["n"][...], W(2)).astype(BF16)
            attend_heads(state_parts(kv), B["sq"], B["zatt"], B["lses"], rows, 1, 8)
            for i in range(2):
                cs = pl.ds(i * half, half)
                zz = nt(B["zatt"][...], WB[3].reshape(D, D)[i * half:(i + 1) * half])
                B["z"][:, cs] = zz.astype(BF16)
                kr = B["keep"][:, cs]
                B["ssend"][:, cs] = (kr * s[:, cs].astype(F32) + (1.0 - kr) * zz).astype(BF16)
                scopy[i].start()
            for i in range(2): kcopy[i].start()
        @pl.when(t < 3)
        def _(): gat.stage_y(5 + t)
        gat.stage_x(4 + t)
        gat.stage_k(2 + t)
        return 0
    lax.fori_loop(0, nctx - 1, turn, 0)
    gat.done(2); gat.done(3)
    for w in range(4, 8): loads[w].start()
    gat.stage_x(7)
    loads[4].wait()
    B["q"][...] = nn(B["h"][...], W(4)).astype(BF16)
    gat.stage_k(5)
    @pl.when(r == nctx - 1)
    def _(): state_in()
    for name in ("s", "n", "sq", "zatt", "z", "lses", "q"): put(name)
    for i in range(2):
        loads[5 + i].wait()
        B["skv"][i] = nn(B["n"][...], W(5 + i)).astype(BF16)
    put("skv")
    @pl.when(r > 0)
    def _():
        for cp in kcopy: cp.wait_recv()
    put("kvp")
    attend_heads(token_parts(kvp, kv, B["skv"], r == 0, rows, 2), B["q"], B["att"], B["lse"], rows, 2, 4)
    put("att"); put("lse")
    gat.stage_k(6)
    loads[7].wait()
    B["y1"][...] = B["x"][...].astype(F32) + nt(B["att"][...], W(7))
    norm_into(B["m"], B["y1"], gm)
    gat.stage_k(7)
    swaps[2].wait_recv()
    m, g, a, du, u, da = B["m"], B["g"], B["a"], B["du"], B["u"], B["da"]
    def wl(j, i): return pltpu.make_async_copy(G.at[8 + 2 * j + i], WB.at[2 * lax.rem(j, 2) + i], wsem.at[2 * lax.rem(j, 2) + i])
    def dcopy(j, i): return pltpu.make_async_copy(WB.at[4 + 2 * lax.rem(j, 2) + i], O["Dc"].at[2 * j + i], dsem.at[2 * lax.rem(j, 2) + i])
    gat.done(4)
    wl(0, 0).start(); wl(0, 1).start()
    B["oacc"][...] = jnp.zeros_like(B["oacc"])
    B["macc"][...] = jnp.zeros_like(B["macc"])
    def slice_step(j, _):
        b = 2 * lax.rem(j, 2)
        wl(j, 0).wait(); wl(j, 1).wait()
        a[...] = nn(m[...], W(b))
        du[...] = nn(g[...], W(b + 1))
        def body(rs):
            av = a[rs, :]
            sq = av * av
            t = jnp.tanh(G1 * av * (1.0 + G3 * sq))
            u[rs, :] = (0.5 * av * (1.0 + t)).astype(BF16)
            dg = 0.5 * (1.0 + t) + 0.5 * av * (1.0 - t * t) * (G1 * (1.0 + 3.0 * G3 * sq))
            da[rs, :] = (dg * du[rs, :]).astype(BF16)
        rows_loop(rows, 32, body)
        @pl.when(j < 3)
        def _():
            gat.done(5 + j)
            wl(j + 1, 0).start(); wl(j + 1, 1).start()
        B["oacc"][...] += nt(u[...], W(b + 1))
        B["macc"][...] += nt(da[...], W(b))
        @pl.when(j >= 2)
        def _():
            dcopy(j - 2, 0).wait(); dcopy(j - 2, 1).wait()
        WB[4 + b] = tn(m[...], da[...]).astype(BF16).reshape(WB.shape[1:])
        dcopy(j, 0).start()
        WB[5 + b] = tn(g[...], u[...]).astype(BF16).reshape(WB.shape[1:])
        dcopy(j, 1).start()
        return 0
    lax.fori_loop(0, 4, slice_step, 0)
    B["gg"][...] = jnp.zeros_like(B["gg"])
    def last(rs):
        yv = B["y1"][rs, :]
        u[rs, :] = (yv + B["oacc"][rs, :]).astype(BF16)
        dv, dgain = norm_back_rows(yv, gm[...], B["macc"][rs, :])
        a[rs, :] = g[rs, :].astype(F32) + dv
        B["gg"][...] += fold8(dgain)
    rows_loop(rows, 32, last)
    put("out", u); put("gy1", a); put("gg")
    for j in (2, 3):
        for i in range(2): dcopy(j, i).wait()
    @pl.when(r < nctx - 1)
    def _():
        for cp in kcopy: cp.wait_send()
        for cp in scopy: cp.wait_send()
    def drains(g_, _):
        gat.drain(g_)
        return 0
    lax.fori_loop(0, 8, drains, 0)
    for sw in swaps: sw.wait_send()
    for cp in puts: cp.wait()

def forward_call(F, nctx, args):
    rows = args["tokens"].shape[1]
    blk = D // (4 * F)
    sh = lambda *s: jax.ShapeDtypeStruct(s, BF16)
    fl = lambda *s: jax.ShapeDtypeStruct(s, F32)
    R = sh(rows, D)
    R2 = sh(2, rows, D)
    L = fl(HEADS, 1, rows)
    mats = lambda n: sh(n, F, 2, 2, blk, D)
    shapes = dict(G=mats(16), Dc=mats(8), out=R, gg=fl(8, D), h=R, q=R, kv=R2, kvp=R2, skv=R2, n=R, s=R, sq=R, zatt=R, z=R, lse=L, lses=L, att=R, x=R, gy1=fl(rows, D), gains=fl(8, D))
    bufs = dict(x=R, g=R, h=R, q=R, kv=R2, kvp=R2, skv=R2, n=R, s=R, ssend=R, sq=R, zatt=R, z=R, att=R, m=R, u=R, da=R,
        y1=fl(rows, D), a=fl(rows, D), du=fl(rows, D), oacc=fl(rows, D), macc=fl(rows, D), lse=L, lses=L, gains=fl(8, D), gs=fl(1, D), gg=fl(8, D), keep=fl(1, D),
        tin=sh(6, D // 2, D // F), tout=sh(6, 2, 2, blk, D // 2), WB=mats(8))
    S = pltpu.SemaphoreType.DMA
    n = 8
    outs = pl.pallas_call(functools.partial(forward_kernel, F, nctx),
        out_shape=[shapes[k] for k in A_OUT],
        in_specs=[ANY] * len(A_IN), out_specs=[ANY] * len(A_OUT),
        scratch_shapes=[pltpu.VMEM(bufs[k].shape, bufs[k].dtype) for k in A_BUF]
            + [S((n, F - 1)), S((n, F - 1)), S((n, F)), S((n, F)), S((n, F - 1)), S((n, F - 1)), S((n, F)), S((n, F))]
            + [S((16,)), S((12,)), S((len(A_OUT),)), S((8,)), S((2,)), S((2,)), S((2,)), S((2,)), S((3,)), S((3,)), S((4,))],
        compiler_params=pltpu.CompilerParams(collective_id=1, has_side_effects=True, vmem_limit_bytes=62 << 20), name="forward")(*[args[k] for k in A_IN])
    return dict(zip(A_OUT, outs))


B_IN = ("G", "Dc", "out", "gg", "gains", "gs", "keep", "h", "q", "kv", "kvp", "skv", "n", "s", "sq", "zatt", "z", "lse", "lses", "att", "x", "gy1")
B_OUT = ("R", "RX", "OUTF", "GXF", "S0", "SUMS", "DD", "KBH", "B1X", "B1Y", "B2H", "ZBH")
B_BUF = ("h", "q", "kv", "kvp", "skv", "n", "s", "sq", "zatt", "z", "lse", "lses", "att", "gy1", "gg", "gains", "gs", "keep",
         "WB", "do", "datt", "dqb", "dkv", "dsend", "dret", "dskv", "dntok", "dsin", "dsout", "ggv",
         "A", "TK", "T1X", "T1Y", "T2", "TZ", "lo", "DS1", "dsp", "gin", "g1", "g2")
B_SEM = ("isem", "wsem", "dsem", "psem", "prem", "csem", "crem", "osem", "orem",
         "ks", "kr", "s1", "r1", "s2", "r2", "zs", "zr", "bs", "br", "fs", "fr", "xs", "xr", "lsem", "dss", "dsr", "d2s", "d2r", "d3s", "d3r", "g1s", "g1r", "g2s", "g2r", "rsem")

def back_kernel(F, nctx, *refs):
    I = dict(zip(B_IN, refs)); at = len(B_IN)
    O = dict(zip(B_OUT, refs[at:])); at += len(B_OUT)
    B = dict(zip(B_BUF, refs[at:])); at += len(B_BUF)
    S = dict(zip(B_SEM, refs[at:]))
    z, x, k, y = where_am_i()
    c = x * 2 + k
    r = c
    rows = B["do"].shape[0]
    blk = D // (4 * F)
    half = D // 2
    mine, other = cols_of(y), cols_of(1 - y)
    xdev, ydev, kdev = (z, (1 - x) * 2 + k, y), (z, c, 1 - y), (z, x * 2 + 1 - k, y)
    dev = lambda cc: (z, cc, y)
    def local(src, dst, sem): return pltpu.make_async_copy(src, dst, sem)
    def remote(src, dst, s, rr, d):
        return pltpu.make_async_remote_copy(src_ref=src, dst_ref=dst, send_sem=s, recv_sem=rr, device_id=d, device_id_type=MESH)
    def to_z(d): return lax.rem(z - (d + 1) + F, F)
    def from_z(d): return lax.rem(z + d + 1, F)
    W4 = (0, 1, 2, 3)
    slots = {7: (0, 0), 5: (1, 1), 6: (2, 2), 3: (3, 3), 2: (4, 0), 4: (5, 1), 0: (6, 2), 1: (7, 3)}
    wload = {w: local(I["G"].at[w], B["WB"].at[sl], S["wsem"].at[i]) for w, (i, sl) in slots.items()}
    W = lambda w: B["WB"][slots[w][1]].reshape(D, D)
    order = ("gy1", "att", "q", "kv", "kvp", "skv", "lse", "gs", "n", "s", "h", "keep", "sq", "zatt", "z", "lses", "gains", "gg")
    loads = {}
    for i, name in enumerate(order):
        loads[name] = local(I[name], B[name], S["isem"].at[i])
    loads["gy1"].start()
    wload[7].start()
    for name in order[1:]: loads[name].start()
    for w in (5, 6, 3): wload[w].start()
    barrier_with(F, 7, True)
    def ksend_from(ref, p, first_row): return remote(ref.at[pl.ds(first_row, 2), :, :, 1 - k], O["KBH"].at[pl.ds(2 * p, 2)], S["ks"].at[p], S["kr"].at[p], kdev)
    for p in range(4): ksend_from(I["Dc"], p, 2 * p).start()
    oswap = remote(I["out"].at[:, other], O["OUTF"].at[y], S["osem"].at[0], S["orem"].at[0], ydev)
    oown = local(I["out"].at[:, mine], O["OUTF"].at[y], S["rsem"].at[0])
    oswap.start(); oown.start()
    A = B["A"]
    def sl(p): return lax.rem(p, 4)
    def first(p, e):
        a = A.at[sl(p), e]
        if e == 0: return remote(a.at[:, 1 - x], O["B1X"].at[p], S["s1"].at[p, 0], S["r1"].at[p, 0], xdev)
        return remote(a.at[:, :, :, other], O["B1Y"].at[p], S["s1"].at[p, 1], S["r1"].at[p, 1], ydev)
    def second(p, e):
        a = A.at[sl(p), e]
        if e == 0: return remote(a.at[:, x, :, other], O["B2H"].at[2 * p], S["s2"].at[p, 0], S["r2"].at[p, 0], ydev)
        return remote(a.at[:, 1 - x, :, mine], O["B2H"].at[2 * p + 1], S["s2"].at[p, 1], S["r2"].at[p, 1], xdev)
    def zsend(p, d):
        return remote(A.at[sl(p), :, to_z(d), x, :, mine], O["ZBH"].at[pl.ds(2 * p, 2), d], S["zs"].at[p, d], S["zr"].at[p, d], (to_z(d), c, y))
    def bcast(p, i):
        return remote(B["lo"].at[lax.rem(p, 2)], O["R"].at[pl.ds(2 * p, 2), c], S["bs"].at[p, i], S["br"].at[p, i], (kdev, xdev)[i])
    cx = (1 - x) * 2 + k
    def fwd(p):
        rr = O["R"].at[pl.ds(2 * p, 2), cx]
        return remote(rr, rr, S["fs"].at[p], S["fr"].at[p], kdev)
    def extra(i): return remote(B["lo"].at[0], O["RX"].at[:, c], S["xs"].at[i], S["xr"].at[i], (z, lax.rem(c + i, 4), 1 - y))
    def rown(p): return local(B["lo"].at[lax.rem(p, 2)], O["R"].at[pl.ds(2 * p, 2), c], S["lsem"].at[5])
    def landed(ref, sem): local(ref, ref, sem).wait()
    def plus(a, b): return (a.astype(F32) + b.astype(F32)).astype(BF16)
    def own_load(p, do):
        @pl.when(p < 4)
        def _(): do(local(I["Dc"].at[pl.ds(2 * p, 2), :, :, k], A.at[sl(p)], S["lsem"].at[0]))
        @pl.when(p >= 4)
        def _(): do(local(O["DD"].at[pl.ds(jnp.maximum(2 * p - 8, 0), 2), :, :, k], A.at[sl(p)], S["lsem"].at[0]))
    def guard(p, body):
        if isinstance(p, int):
            if 0 <= p < 8: body()
        else:
            pl.when((p >= 0) & (p < 8))(body)
    def pair_step(s):
        def k_in():
            if not isinstance(s, int) or s >= 4:
                def free():
                    for e in range(2):
                        first(s - 4, e).wait_send()
                        second(s - 4, e).wait_send()
                    for d in range(F - 1): zsend(s - 4, d).wait_send()
                if isinstance(s, int): free()
                else: pl.when(s >= 4)(free)
            landed(O["KBH"].at[pl.ds(2 * s, 2)], S["kr"].at[s])
            own_load(s, lambda cp: cp.start())
            local(O["KBH"].at[pl.ds(2 * s, 2)], B["TK"], S["lsem"].at[1]).start()
        def s1_in():
            p = s - 1
            first(p, 0).wait_recv()
            local(O["B1X"].at[p], B["T1X"], S["lsem"].at[2]).start()
            first(p, 1).wait_recv()
            local(O["B1Y"].at[p], B["T1Y"], S["lsem"].at[6]).start()
        def s2_in():
            p = s - 2
            second(p, 0).wait_recv()
            second(p, 1).wait_recv()
            local(O["B2H"].at[pl.ds(2 * p, 2)], B["T2"], S["lsem"].at[3]).start()
        def z_in():
            p = s - 3
            for d in range(F - 1): zsend(p, d).wait_recv()
            local(O["ZBH"].at[pl.ds(2 * p, 2)], B["TZ"], S["lsem"].at[4]).start()
        def k_do():
            own_load(s, lambda cp: cp.wait())
            local(O["KBH"].at[pl.ds(2 * s, 2)], B["TK"], S["lsem"].at[1]).wait()
            a, t = A.at[sl(s)], B["TK"]
            for e in range(2):
                def add(i, _):
                    zz, xx = lax.div(i, 2), lax.rem(i, 2)
                    a[e, zz, xx] = plus(a[e, zz, xx], t[e, zz, xx])
                    return 0
                lax.fori_loop(0, 2 * F, add, 0)
                first(s, e).start()
        def s1_do():
            p = s - 1
            a = A.at[sl(p)]
            local(O["B1X"].at[p], B["T1X"], S["lsem"].at[2]).wait()
            def add0(i, _):
                a[0, i, x] = plus(a[0, i, x], B["T1X"][i])
                return 0
            lax.fori_loop(0, F, add0, 0)
            second(p, 0).start()
            local(O["B1Y"].at[p], B["T1Y"], S["lsem"].at[6]).wait()
            def add1(i, _):
                for xx in range(2): a[1, i, xx, :, mine] = plus(a[1, i, xx, :, mine], B["T1Y"][i, xx])
                return 0
            lax.fori_loop(0, F, add1, 0)
            second(p, 1).start()
        def s2_do():
            p = s - 2
            a = A.at[sl(p)]
            local(O["B2H"].at[pl.ds(2 * p, 2)], B["T2"], S["lsem"].at[3]).wait()
            def add(i, _):
                for e in range(2): a[e, i, x, :, mine] = plus(a[e, i, x, :, mine], B["T2"][e, i])
                return 0
            lax.fori_loop(0, F, add, 0)
            for d in range(F - 1): zsend(p, d).start()
        def z_do():
            p = s - 3
            local(O["ZBH"].at[pl.ds(2 * p, 2)], B["TZ"], S["lsem"].at[4]).wait()
            def free():
                bcast(p - 2, 0).wait_send()
                bcast(p - 2, 1).wait_send()
                @pl.when(p == 8)
                def _(): pass
            if isinstance(p, int):
                if p >= 2: free()
            else: pl.when(p >= 2)(free)
            for e in range(2):
                total = A[sl(p), e, z, x, :, mine].astype(F32)
                for d in range(F - 1): total = total + B["TZ"][e, d].astype(F32)
                B["lo"][lax.rem(p, 2), e] = total.astype(BF16)
            for i in range(2): bcast(p, i).start()
            cp = rown(p)
            cp.start()
            cp.wait()
            def special():
                for i in range(4): extra(i).start()
                for i in range(4): extra(i).wait_send()
            if isinstance(p, int):
                if p == 6: special()
            else: pl.when(p == 6)(special)
        def f_do():
            p = s - 4
            landed(O["R"].at[pl.ds(2 * p, 2), cx], S["br"].at[p, 1])
            fwd(p).start()
        guard(s, k_in)
        guard(s - 1, s1_in)
        guard(s - 2, s2_in)
        guard(s - 3, z_in)
        guard(s, k_do)
        guard(s - 1, s1_do)
        guard(s - 2, s2_do)
        guard(s - 3, z_do)
        guard(s - 4, f_do)
    ggv = B["ggv"]
    ggv[...] = jnp.zeros_like(ggv)
    loads["gy1"].wait()
    do, datt, dqb, dkv, dskv, dntok, dsin, dsout = (B[i] for i in ("do", "datt", "dqb", "dkv", "dskv", "dntok", "dsin", "dsout"))
    def cast(rs): do[rs, :] = B["gy1"][rs, :].astype(BF16)
    rows_loop(rows, 64, cast)
    wload[7].wait()
    datt[...] = nn(do[...], W(7)).astype(BF16)
    wload[2].start()
    for name in order[1:7]: loads[name].wait()
    hz = F // 2
    def pair_view(ref):
        return lambda i, cs: ref[i * hz:(i + 1) * hz, :, :, :, cs].reshape(rows, HEAD)
    kvp_at, skv_at = pair_view(B["kvp"]), pair_view(B["skv"])
    def parts_of(cs, qc):
        upto = (qc + 1) * (rows // 2)
        return [(lambda: kvp_at(0, cs), lambda: kvp_at(1, cs), lambda s: jnp.where(r == 0, NEG, s)),
                (lambda: B["kv"][0, pl.ds(0, upto), cs], lambda: B["kv"][1, pl.ds(0, upto), cs], lambda s: causal_scores(s, 0, qc * (rows // 2))),
                (lambda: skv_at(0, cs), lambda: skv_at(1, cs), lambda s: s)]
    def sink(i, cs, dk, dv):
        dst = (B["dsend"], dkv, dskv)[i]
        dst[0, :, cs] = dk.astype(dst.dtype)
        dst[1, :, cs] = dv.astype(dst.dtype)
    def halves(i, _):
        pair_step(i)
        attend_heads_back(parts_of, B["q"], datt, B["lse"], dqb, sink, rows, 2, 1, i * (HEADS // 2), HEADS // 2)
        return 0
    lax.fori_loop(0, 2, halves, 0)
    pcopy = remote(B["dsend"], B["dret"], S["psem"].at[0], S["prem"].at[0], dev(r - 1))
    @pl.when(r > 0)
    def _(): pcopy.start()
    wload[5].wait(); wload[6].wait()
    dntok[...] = nt(dskv[0], W(5)) + nt(dskv[1], W(6))
    wload[4].start(); wload[0].start()
    for name in order[7:11]: loads[name].wait()
    hr = rows // 2
    ccopy = [remote(dsout.at[pl.ds(i * hr, hr)], dsin.at[pl.ds(i * hr, hr)], S["csem"].at[i], S["crem"].at[i], dev(r - 1)) for i in range(2)]
    def finish_state(more):
        for i in range(2):
            def body(j, _):
                rs = pl.ds(pl.multiple_of(i * hr + j * 32, 32), 32)
                dv, dgain = norm_back_rows(B["s"][rs, :].astype(F32), B["gs"][...], dntok[rs, :])
                if more: dv = dv + B["keep"][...] * dsin[rs, :].astype(F32)
                dsout[rs, :] = dv.astype(BF16)
                ggv[pl.ds(8, 8), :] += fold8(dgain)
                return 0
            lax.fori_loop(0, hr // 32, body, 0)
            @pl.when(r > 0)
            def _(): ccopy[i].start()
    @pl.when(r == nctx - 1)
    def _(): finish_state(False)
    stages = (B["kvp"], B["skv"])
    def grad_out(i, left, right):
        if i >= 2: pass
        st = stages[i % 2]
        st[...] = tn(left[...], right[...]).astype(BF16).reshape(st.shape)
        local(st, O["DD"].at[i], S["dsem"].at[i]).start()
        if i % 2 == 1:
            for q in (i - 1, i): local(stages[q % 2], O["DD"].at[q], S["dsem"].at[q]).wait()
            ksend_from(O["DD"], 4 + i // 2, i - 1).start()
    grad_out(0, do, B["att"])
    xload = local(I["x"], B["att"], S["rsem"].at[2])
    xload.start()
    grad_out(1, B["n"], dskv.at[0])
    pair_step(2)
    grad_out(2, B["n"], dskv.at[1])
    grad_out(3, B["h"], dqb)
    for name in order[11:]: loads[name].wait()
    wload[3].wait(); wload[2].wait()
    dzb = datt
    def turn(t, _):
        @pl.when(r == nctx - 2 - t)
        def _():
            for cp in ccopy: cp.wait_recv()
            def body(rs):
                d = dsin[rs, :].astype(F32)
                kr = B["keep"][...]
                dzb[rs, :] = ((1.0 - kr) * d).astype(BF16)
                ggv[pl.ds(16, 8), :] += fold8(d * (B["s"][rs, :].astype(F32) - B["z"][rs, :].astype(F32)) * kr * (1.0 - kr))
            rows_loop(rows, 32, body)
            do[...] = nn(dzb[...], W(3)).astype(BF16)
            def sink2(i, cs, dk, dv):
                dkv[0, :, cs] += dk
                dkv[1, :, cs] += dv
            attend_heads_back(state_parts(B["kv"]), B["sq"], do, B["lses"], B["q"], sink2, rows, 1, 4, 0, HEADS)
            dntok[...] += nt(B["q"][...], W(2))
            finish_state(True)
        @pl.when(t < nctx - 2)
        def _(): pair_step(3 + t)
        return 0
    lax.fori_loop(0, nctx - 1, turn, 0)
    n2 = 2 * F
    prow = rows // n2
    me = z * 2 + y
    def zy(i):
        q = lax.rem(me + i + 1, n2)
        return q, (lax.div(q, 2), 0, lax.rem(q, 2))
    def back_of(i): return lax.rem(me - (i + 1) + n2, n2)
    def d1(i):
        q, d = zy(i)
        return remote(dsout.at[pl.ds(pl.multiple_of(q * prow, prow), prow)], B["DS1"].at[me], S["dss"].at[i], S["dsr"].at[i], d)
    def d2(i):
        q, d = zy(i)
        return remote(B["dsp"], O["S0"].at[me], S["d2s"].at[i], S["d2r"].at[i], d)
    def d3(i, d): return remote(O["S0"], O["S0"], S["d3s"].at[i], S["d3r"].at[0], d)
    dsown = local(B["dsp"], O["S0"].at[me], S["rsem"].at[3])
    @pl.when(r == 0)
    def _():
        for i in range(n2 - 1): d1(i).start()
    @pl.when(r == nctx - 1)
    def _():
        B["q"][...] = jnp.zeros_like(B["q"])
        dzb[...] = jnp.zeros_like(dzb)
        B["zatt"][...] = jnp.zeros_like(B["zatt"])
    grad_out(4, B["n"], B["q"])
    grad_out(5, dzb, B["zatt"])
    @pl.when(r < nctx - 1)
    def _(): pcopy.wait_recv()
    @pl.when(r == nctx - 1)
    def _(): B["dret"][...] = jnp.zeros_like(B["dret"])
    wload[1].start()
    for i in range(2):
        def add(rs): dskv[i, rs, :] = (dkv[i, rs, :] + B["dret"][i, rs, :].astype(F32)).astype(BF16)
        rows_loop(rows, 32, add)
    grad_out(6, B["h"], dskv.at[0])
    grad_out(7, B["h"], dskv.at[1])
    pair_step(5)
    wload[4].wait(); wload[0].wait(); wload[1].wait()
    xload.wait()
    dntok[...] = nt(dqb[...], W(4)) + nt(dskv[0], W(0)) + nt(dskv[1], W(1))
    gxb = B["att"]
    def last(rs):
        dv, dgain = norm_back_rows(gxb[rs, :].astype(F32), B["gains"][pl.ds(0, 1), :], dntok[rs, :])
        ggv[pl.ds(0, 8), :] += fold8(dgain)
        gxb[rs, :] = (B["gy1"][rs, :] + dv).astype(BF16)
    rows_loop(rows, 32, last)
    gswap = remote(gxb.at[:, other], O["GXF"].at[y], S["osem"].at[1], S["orem"].at[1], ydev)
    gown = local(gxb.at[:, mine], O["GXF"].at[y], S["rsem"].at[1])
    gswap.start(); gown.start()
    gin = B["gin"]
    gin[...] = jnp.zeros_like(gin)
    for i in range(3): gin[pl.ds(i, 1), :] = jnp.sum(ggv[pl.ds(8 * i, 8), :], axis=0, keepdims=True)
    gin[pl.ds(3, 1), :] = jnp.sum(B["gg"][...], axis=0, keepdims=True)
    around = ((0, 0, 1), (0, 1, 0), (0, 1, 1), (1, 0, 0), (1, 0, 1), (1, 1, 0), (1, 1, 1))
    def plane(i):
        dx, dk, dy = around[i]
        return lax.rem(x + dx, 2), lax.rem(k + dk, 2), lax.rem(y + dy, 2)
    spot = c * 2 + y
    def g1copy(i):
        px, pk, py = plane(i)
        return remote(gin, B["g1"].at[spot], S["g1s"].at[i], S["g1r"].at[i], (z, px * 2 + pk, py))
    def g2copy(d): return remote(gin, B["g2"].at[z], S["g2s"].at[d], S["g2r"].at[d], (to_z(d), c, y))
    B["g1"][spot] = gin[...]
    for i in range(7): g1copy(i).start()
    def tail(i, _):
        s = 6 + i
        @pl.when(i == 1)
        def _():
            for j in range(7):
                g1copy(j).wait_send()
                px, pk, py = plane(j)
                landed(B["g1"].at[(px * 2 + pk) * 2 + py], S["g1r"].at[j])
            total = B["g1"][0]
            for j in range(1, 8): total = total + B["g1"][j]
            gin[...] = total
            B["g2"][z] = total
            for d in range(F - 1): g2copy(d).start()
        @pl.when((i == 1) & (r == 0))
        def _():
            B["DS1"][me] = dsout[pl.ds(pl.multiple_of(me * prow, prow), prow), :]
            for j in range(n2 - 1): landed(B["DS1"].at[back_of(j)], S["dsr"].at[j])
            total = B["DS1"][0].astype(F32)
            for j in range(1, n2): total = total + B["DS1"][j].astype(F32)
            B["dsp"][...] = total.astype(BF16)
            dsown.start()
            for j in range(n2 - 1): d2(j).start()
        @pl.when((i == 2) & (r == 0))
        def _():
            for j in range(n2 - 1): landed(O["S0"].at[back_of(j)], S["d2r"].at[j])
            dsown.wait()
            d3(0, dev(1)).start()
            d3(1, dev(2)).start()
        @pl.when((i == 3) & (r == 2))
        def _():
            landed(O["S0"], S["d3r"].at[0])
            d3(0, dev(3)).start()
        @pl.when(i == 3)
        def _():
            for d in range(F - 1):
                g2copy(d).wait_send()
                landed(B["g2"].at[from_z(d)], S["g2r"].at[d])
            total = B["g2"][0]
            for d in range(1, F): total = total + B["g2"][d]
            gin[...] = total
            local(gin, O["SUMS"], S["rsem"].at[4]).start()
        pair_step(s)
        return 0
    lax.fori_loop(0, 6, tail, 0)
    local(gin, O["SUMS"], S["rsem"].at[4]).wait()
    for p in range(4, 8):
        for e in range(2):
            first(p, e).wait_send()
            second(p, e).wait_send()
        for d in range(F - 1): zsend(p, d).wait_send()
    for p in (6, 7):
        for i in range(2): bcast(p, i).wait_send()
    sib = x * 2 + 1 - k
    def ends(p, _):
        ksend_from(O["DD"], p, 0).wait_send()
        fwd(p).wait_send()
        landed(O["R"].at[pl.ds(2 * p, 2), sib], S["br"].at[p, 0])
        landed(O["R"].at[pl.ds(2 * p, 2), (1 - x) * 2 + 1 - k], S["fr"].at[p])
        return 0
    lax.fori_loop(0, 8, ends, 0)
    for i in range(4): landed(O["RX"].at[:, lax.rem(c - i + 4, 4)], S["xr"].at[i])
    @pl.when(r == 0)
    def _():
        for j in range(n2 - 1):
            d1(j).wait_send()
            d2(j).wait_send()
        d3(0, dev(1)).wait_send()
        d3(1, dev(2)).wait_send()
    @pl.when(r == 2)
    def _(): d3(0, dev(3)).wait_send()
    @pl.when((r == 1) | (r == 3))
    def _(): landed(O["S0"], S["d3r"].at[0])
    @pl.when(r > 0)
    def _():
        pcopy.wait_send()
        for cp in ccopy: cp.wait_send()
    oswap.wait(); oown.wait(); gswap.wait(); gown.wait()

def back_call(F, nctx, vals, gs, keep):
    rows = vals["h"].shape[0]
    blk = D // (4 * F)
    half = D // 2
    sh = lambda *s: jax.ShapeDtypeStruct(s, BF16)
    fl = lambda *s: jax.ShapeDtypeStruct(s, F32)
    mats = lambda n: sh(n, F, 2, 2, blk, D)
    R, R2, L = sh(rows, D), sh(2, rows, D), fl(HEADS, 1, rows)
    prow = rows // (2 * F)
    shapes = dict(R=sh(16, 4, blk, half), RX=sh(2, 4, blk, half), OUTF=sh(2, rows, half), GXF=sh(2, rows, half), S0=sh(2 * F, prow, D), SUMS=fl(8, D),
        DD=mats(8), KBH=sh(16, F, 2, blk, D), B1X=sh(8, F, blk, D), B1Y=sh(8, F, 2, blk, half), B2H=sh(16, F, blk, half), ZBH=sh(16, F - 1, blk, half))
    one = sh(F, 2, 2, blk, D)
    bufs = dict(h=R, q=R, kv=R2, kvp=one, skv=one, n=R, s=R, sq=R, zatt=R, z=R, lse=L, lses=L, att=R, gy1=fl(rows, D), gg=fl(8, D), gains=fl(8, D), gs=fl(1, D), keep=fl(1, D),
        WB=mats(4), do=R, datt=R, dqb=R, dkv=fl(2, rows, D), dsend=R2, dret=R2, dskv=R2, dntok=fl(rows, D), dsin=R, dsout=R, ggv=fl(24, D),
        A=sh(4, 2, F, 2, blk, D), TK=sh(2, F, 2, blk, D), T1X=sh(F, blk, D), T1Y=sh(F, 2, blk, half), T2=sh(2, F, blk, half), TZ=sh(2, F - 1, blk, half),
        lo=sh(2, 2, blk, half), DS1=sh(2 * F, prow, D), dsp=sh(prow, D), gin=fl(8, D), g1=fl(8, 8, D), g2=fl(F, 8, D))
    X = pltpu.SemaphoreType.DMA
    sems = dict(isem=(18,), wsem=(8,), dsem=(8,), psem=(1,), prem=(1,), csem=(2,), crem=(2,), osem=(2,), orem=(2,),
        ks=(8,), kr=(8,), s1=(8, 2), r1=(8, 2), s2=(8, 2), r2=(8, 2), zs=(8, F - 1), zr=(8, F - 1), bs=(8, 2), br=(8, 2), fs=(8,), fr=(8,), xs=(4,), xr=(4,), lsem=(7,),
        dss=(2 * F,), dsr=(2 * F,), d2s=(2 * F,), d2r=(2 * F,), d3s=(2,), d3r=(1,), g1s=(7,), g1r=(7,), g2s=(F - 1,), g2r=(F - 1,), rsem=(5,))
    args = dict(vals)
    args["gs"], args["keep"] = gs, keep
    args["kvp"], args["skv"] = (args[i].reshape(one.shape) for i in ("kvp", "skv"))
    outs = pl.pallas_call(functools.partial(back_kernel, F, nctx),
        out_shape=[shapes[i] for i in B_OUT], in_specs=[ANY] * len(B_IN), out_specs=[ANY] * len(B_OUT),
        scratch_shapes=[pltpu.VMEM(bufs[i].shape, bufs[i].dtype) for i in B_BUF] + [X(sems[i]) for i in B_SEM],
        compiler_params=pltpu.CompilerParams(collective_id=2, has_side_effects=True, vmem_limit_bytes=63 << 20), name="backward")(*[args[i] for i in B_IN])
    return dict(zip(B_OUT, outs))


def local(
    tokens,
    cotangent,
    w_query,
    w_key,
    w_value,
    w_out,
    w_state_key,
    w_state_value,
    w_state_query,
    w_state_out,
    w_up,
    w_down,
    gain_attn,
    gain_state,
    gain_mlp,
    forget_logit,
    state_init,
):
    fsdp = lax.axis_size("fsdp")
    tp_rank = lax.axis_index("tp")
    ctx_count = lax.axis_size("ctx")
    half = D // 2
    rows = D // fsdp
    blk = rows // 4
    tiles = lambda w: w.reshape(2, 2, blk, w.shape[1])
    args = dict(
        tokens=tokens, cotangent=cotangent, gtp=jnp.pad(jnp.stack([gain_attn, gain_mlp]), ((0, 6), (0, 0))),
        gstate=gain_state[None], keep=jax.nn.sigmoid(forget_logit)[None], s0=state_init,
        key=tiles(w_key), value=tiles(w_value), squery=tiles(w_state_query), sout=w_state_out, query=tiles(w_query),
        skey=tiles(w_state_key), svalue=tiles(w_state_value), out=w_out, up=tiles(w_up), down=w_down)
    vals = forward_call(fsdp, ctx_count, args)
    got = back_call(fsdp, ctx_count, vals, args["gstate"], args["keep"])
    full = got["R"].reshape(16, rows, half).astype(F32)
    r = {w: full[8 + i] for i, w in enumerate((7, 5, 6, 4, 2, 3, 0, 1))}
    rx = got["RX"].reshape(2, rows, half).astype(F32)
    small = got["SUMS"]

    def both(mine, other):
        first = jnp.where(tp_rank == 0, mine, other)
        second = jnp.where(tp_rank == 0, other, mine)
        return jnp.concatenate([first, second], axis=1)

    at = lambda i: lax.dynamic_slice_in_dim(small[i], tp_rank * half, half, 0)
    return (
        got["OUTF"],
        got["GXF"],
        r[4],
        r[0],
        r[1],
        r[7].T,
        r[5],
        r[6],
        both(r[2], rx[0]),
        both(r[3], rx[1]).T,
        full[0:8:2].swapaxes(0, 1).reshape(rows, -1),
        full[1:8:2].swapaxes(1, 2).reshape(-1, rows),
        at(0),
        small[1],
        at(3),
        small[2],
        got["S0"].reshape(state_init.shape).astype(F32),
    )


def solution(mesh):
    placed = (
        P("fsdp", "ctx", "tp"),
        P("fsdp", "ctx", "tp"),
        P("fsdp", "tp"),
        P("fsdp", "tp"),
        P("fsdp", "tp"),
        P("tp", "fsdp"),
        P("fsdp", "tp"),
        P("fsdp", "tp"),
        P("fsdp", None),
        P(None, "fsdp"),
        P("fsdp", "tp"),
        P("tp", "fsdp"),
        P("tp"),
        P(),
        P("tp"),
        P(),
        P(),
    )
    return jax.shard_map(
        local,
        mesh=mesh,
        in_specs=placed,
        out_specs=(
            P("fsdp", "ctx", "tp"),
            P("fsdp", "ctx", "tp"),
            P("fsdp", "tp"),
            P("fsdp", "tp"),
            P("fsdp", "tp"),
            P("tp", "fsdp"),
            P("fsdp", "tp"),
            P("fsdp", "tp"),
            P("fsdp", None),
            P(None, "fsdp"),
            P("fsdp", "tp"),
            P("tp", "fsdp"),
            P("tp"),
            P(),
            P("tp"),
            P(),
            P(),
        ),
        check_vma=False,
    )
```

```python
import functools

import jax
import jax.numpy as jnp
from jax import lax
from jax.experimental import pallas as pl
from jax.experimental.pallas import tpu as pltpu
from jax.sharding import PartitionSpec as P

MESH = pl.DeviceIdType.MESH
ANY = pl.BlockSpec(memory_space=pl.ANY)
D = 1024
HEADS = 8
HEAD = 128
EPS = 1e-06
NEG = -1e30
LOG2E = 1.4426950408889634
F32 = jnp.float32
BF16 = jnp.bfloat16
SCALE = HEAD ** -0.5
CE = SCALE * LOG2E

def nn(a, b): return lax.dot_general(a, b, (((1,), (0,)), ((), ())), preferred_element_type=F32)
def nt(a, b): return lax.dot_general(a, b, (((1,), (1,)), ((), ())), preferred_element_type=F32)
def tn(a, b): return lax.dot_general(a, b, (((0,), (0,)), ((), ())), preferred_element_type=F32)

def rows_loop(total, step, body):
    def run(i, _):
        body(pl.ds(pl.multiple_of(i * step, step), step))
        return 0
    lax.fori_loop(0, total // step, run, 0)

def inverse_of(v):
    return lax.rsqrt(jnp.mean(v * v, axis=-1, keepdims=True) + EPS)

def norm_into(dst, src, gain):
    def body(rs):
        v = src[rs, :].astype(F32)
        dst[rs, :] = (v * inverse_of(v) * gain[...]).astype(dst.dtype)
    rows_loop(src.shape[0], 32, body)

def head_cols(h): return pl.ds(pl.multiple_of(h * HEAD, HEAD), HEAD)

def causal_scores(s, first_key, first_query):
    keys = lax.broadcasted_iota(jnp.int32, s.shape, 0) + first_key
    qs = lax.broadcasted_iota(jnp.int32, s.shape, 1) + first_query
    return jnp.where(keys <= qs, s, NEG)

def over_heads(one, unroll, h0, count):
    def body(i, _):
        for u in range(unroll):
            one(h0 + i * unroll + u)
        return 0
    lax.fori_loop(0, count // unroll, body, 0)

def attend_heads(parts_of, q, out, lse, rows, chunks, unroll):
    step = rows // chunks
    def one(h):
        cs = head_cols(h)
        for qc in range(chunks):
            rs = pl.ds(qc * step, step)
            qh = q[rs, cs]
            parts = parts_of(cs, qc)
            scores = [mask(nt(keys(), qh)) for keys, values, mask in parts]
            big = functools.reduce(jnp.maximum, [jnp.max(s, axis=0, keepdims=True) for s in scores])
            es = [jnp.exp2((s - big) * CE) for s in scores]
            total = functools.reduce(jnp.add, [jnp.sum(e, axis=0, keepdims=True) for e in es])
            inv = 1.0 / total
            acc = functools.reduce(jnp.add, [tn((e * inv).astype(BF16), p[1]()) for e, p in zip(es, parts)])
            out[rs, cs] = acc.astype(BF16)
            lse[h, :, pl.ds(qc * step, step)] = big * CE + jnp.log2(total)
    over_heads(one, unroll, 0, HEADS)

def token_parts(kvp, kv, skv, first, rows, chunks):
    def parts_of(cs, qc):
        step = rows // chunks
        upto = (qc + 1) * step
        same = lambda s: s
        earlier = lambda s: jnp.where(first, NEG, s)
        causal = lambda s: causal_scores(s, 0, qc * step)
        return [(lambda: kvp[0, :, cs], lambda: kvp[1, :, cs], earlier),
                (lambda: kv[0, pl.ds(0, upto), cs], lambda: kv[1, pl.ds(0, upto), cs], causal),
                (lambda: skv[0, :, cs], lambda: skv[1, :, cs], same)]
    return parts_of

def state_parts(kv):
    def parts_of(cs, qc):
        return [(lambda: kv[0, :, cs], lambda: kv[1, :, cs], lambda s: s)]
    return parts_of

def chain_barrier(r, n, dev):
    bar = pltpu.get_barrier_semaphore()
    @pl.when(r > 0)
    def _(): pl.semaphore_signal(bar, inc=1, device_id=dev(r - 1), device_id_type=MESH)
    @pl.when(r < n - 1)
    def _(): pl.semaphore_signal(bar, inc=1, device_id=dev(r + 1), device_id_type=MESH)
    pl.semaphore_wait(bar, jnp.where(r > 0, 1, 0) + jnp.where(r < n - 1, 1, 0))

def where_am_i():
    f = lax.axis_index("fsdp")
    c = lax.axis_index("ctx")
    return f, lax.div(c, 2), lax.rem(c, 2), lax.axis_index("tp")

def cols_of(t):
    return pl.ds(pl.multiple_of(t * (D // 2), D // 2), D // 2)

G1 = 0.7978845608028654
G3 = 0.044715

def norm_back_rows(v, gain, e):
    inv = inverse_of(v)
    w = e * gain
    proj = jnp.sum(w * v, axis=-1, keepdims=True) * (1.0 / D)
    return inv * w - v * (inv * inv * inv) * proj, e * v * inv

def fold8(v):
    return functools.reduce(jnp.add, [v[i * 8:(i + 1) * 8] for i in range(v.shape[0] // 8)])

def attend_heads_back(parts_of, q, datt, lse, dq, sink, rows, chunks, unroll, h0, count):
    step = rows // chunks
    def one(h):
        cs = head_cols(h)
        sums = None
        for qc in range(chunks):
            rs = pl.ds(qc * step, step)
            qh = q[rs, cs]
            gh = datt[rs, cs]
            ls = lse[h, :, pl.ds(qc * step, step)]
            parts = parts_of(cs, qc)
            ps = [jnp.exp2(p[2](nt(p[0](), qh)) * CE - ls) for p in parts]
            dps = [nt(p[1](), gh) for p in parts]
            delta = functools.reduce(jnp.add, [jnp.sum(a * b, axis=0, keepdims=True) for a, b in zip(ps, dps)])
            dss = [(a * (b - delta)).astype(BF16) for a, b in zip(ps, dps)]
            dq[rs, cs] = (functools.reduce(jnp.add, [tn(d, p[0]()) for d, p in zip(dss, parts)]) * SCALE).astype(dq.dtype)
            new = [(nn(d, qh), nn(a.astype(BF16), gh)) for a, d in zip(ps, dss)]
            if sums is None: sums = new
            else:
                merged = []
                for (k0, v0), (k1, v1) in zip(sums, new):
                    n0 = k0.shape[0]
                    if n0 < k1.shape[0]:
                        k1 = jnp.concatenate([k0 + k1[:n0], k1[n0:]], axis=0)
                        v1 = jnp.concatenate([v0 + v1[:n0], v1[n0:]], axis=0)
                    else:
                        k1, v1 = k0 + k1, v0 + v1
                    merged.append((k1, v1))
                sums = merged
        for i, (dk, dv) in enumerate(sums): sink(i, cs, dk * SCALE, dv)
    over_heads(one, unroll, h0, count)


class Gather:
    def __init__(self, G, F, sems):
        self.G, self.F, self.sems = G, F, sems
        self.z, self.x, self.k, self.y = where_am_i()

    def src_z(self, d):
        return lax.rem(self.z + d + 1, self.F)

    def region(self, g, z, x, k, cols=None):
        w = pl.ds(2 * g, 2)
        if cols is None:
            return self.G.at[w, z, x, k]
        return self.G.at[w, z, x, k, :, cols]

    def both_x(self, g, z, k, cols=None):
        w = pl.ds(2 * g, 2)
        if cols is None:
            return self.G.at[w, z, :, k]
        return self.G.at[w, z, :, k, :, cols]

    def remote(self, ref, i, g, d, dev):
        return pltpu.make_async_remote_copy(
            src_ref=ref, dst_ref=ref, send_sem=self.sems[i].at[g, d], recv_sem=self.sems[i + 1].at[g, d],
            device_id=dev, device_id_type=MESH)

    def landed(self, ref, i, g, d):
        pltpu.make_async_copy(ref, ref, self.sems[i + 1].at[g, d]).wait()

    def zcopy(self, g, d):
        to = lax.rem(self.z - (d + 1) + self.F, self.F)
        return self.remote(self.region(g, self.z, self.x, self.k, cols_of(self.y)), 0, g, d, (to, self.x * 2 + self.k, self.y))

    def ycopy(self, g, d):
        dev = (self.z, self.x * 2 + self.k, 1 - self.y)
        if d == self.F - 1:
            return self.remote(self.both_x(g, self.z, self.k, cols_of(self.y)), 2, g, d, dev)
        return self.remote(self.region(g, self.src_z(d), self.x, self.k, cols_of(self.y)), 2, g, d, dev)

    def xcopy(self, g, d):
        return self.remote(self.region(g, self.src_z(d), self.x, self.k), 4, g, d, (self.z, (1 - self.x) * 2 + self.k, self.y))

    def kcopy(self, g, d):
        dev = (self.z, self.x * 2 + 1 - self.k, self.y)
        if d == self.F - 1:
            return self.remote(self.both_x(g, self.z, self.k, cols_of(1 - self.y)), 6, g, d, dev)
        return self.remote(self.both_x(g, self.src_z(d), self.k), 6, g, d, dev)

    def send_z(self, g):
        for d in range(self.F - 1):
            self.zcopy(g, d).start()
        self.ycopy(g, self.F - 1).start()

    def stage_y(self, g):
        for d in range(self.F - 1):
            self.landed(self.region(g, self.src_z(d), self.x, self.k, cols_of(self.y)), 0, g, d)
            self.ycopy(g, d).start()

    def stage_x(self, g):
        o = cols_of(1 - self.y)
        for d in range(self.F - 1):
            self.landed(self.region(g, self.src_z(d), self.x, self.k, o), 2, g, d)
            self.xcopy(g, d).start()
        self.landed(self.both_x(g, self.z, self.k, o), 2, g, self.F - 1)
        self.kcopy(g, self.F - 1).start()

    def stage_k(self, g):
        for d in range(self.F - 1):
            self.landed(self.region(g, self.src_z(d), 1 - self.x, self.k), 4, g, d)
            self.kcopy(g, d).start()

    def done(self, g):
        for d in range(self.F - 1):
            self.landed(self.both_x(g, self.src_z(d), 1 - self.k), 6, g, d)
        self.landed(self.both_x(g, self.z, 1 - self.k, cols_of(1 - self.y)), 6, g, self.F - 1)

    def zwide(self, g, d):
        to = lax.rem(self.z - (d + 1) + self.F, self.F)
        return self.remote(self.both_x(g, self.z, self.k, cols_of(self.y)), 0, g, d, (to, self.x * 2 + self.k, self.y))

    def ywide(self, g, d):
        return self.remote(self.both_x(g, self.src_z(d), self.k, cols_of(self.y)), 2, g, d, (self.z, self.x * 2 + self.k, 1 - self.y))

    def send_z_wide(self, g):
        for d in range(self.F - 1):
            self.zwide(g, d).start()
        self.ycopy(g, self.F - 1).start()

    def stage_y_wide(self, g):
        for d in range(self.F - 1):
            self.landed(self.both_x(g, self.src_z(d), self.k, cols_of(self.y)), 0, g, d)
            self.ywide(g, d).start()

    def stage_x_wide(self, g):
        for d in range(self.F - 1):
            self.landed(self.both_x(g, self.src_z(d), self.k, cols_of(1 - self.y)), 2, g, d)
            self.kcopy(g, d).start()
        self.landed(self.both_x(g, self.z, self.k, cols_of(1 - self.y)), 2, g, self.F - 1)
        self.kcopy(g, self.F - 1).start()

    def drain_wide(self, g):
        for d in range(self.F):
            if d < self.F - 1:
                self.zwide(g, d).wait_send()
                self.ywide(g, d).wait_send()
            self.kcopy(g, d).wait_send()
        self.ycopy(g, self.F - 1).wait_send()

    def drain(self, g):
        for d in range(self.F):
            if d < self.F - 1:
                self.zcopy(g, d).wait_send()
                self.xcopy(g, d).wait_send()
            self.ycopy(g, d).wait_send()
            self.kcopy(g, d).wait_send()

def barrier_with(F, count, across=False):
    z, x, k, y = where_am_i()
    bar = pltpu.get_barrier_semaphore()
    peers = [(lax.rem(z + d + 1, F), x * 2 + k, y) for d in range(F - 1)]
    for dx, dk, dy in ((0, 0, 1), (1, 0, 0), (0, 1, 0), (1, 1, 0), (1, 0, 1), (0, 1, 1), (1, 1, 1))[:count]:
        peers.append((z, lax.rem(x + dx, 2) * 2 + lax.rem(k + dk, 2), lax.rem(y + dy, 2)))
    if across:
        peers += [(lax.rem(z + d + 1, F), x * 2 + k, 1 - y) for d in range(F - 1)]
    for p in peers:
        pl.semaphore_signal(bar, inc=1, device_id=p, device_id_type=MESH)
    pl.semaphore_wait(bar, len(peers))

A_IN = ("tokens", "cotangent", "gtp", "gstate", "keep", "s0", "key", "value", "squery", "sout", "query", "skey", "svalue", "out", "up", "down")
A_OUT = ("G", "Dc", "out", "gg", "h", "q", "kv", "kvp", "skv", "n", "s", "sq", "zatt", "z", "lse", "lses", "att", "x", "gy1", "gains")
A_BUF = ("x", "g", "h", "q", "kv", "kvp", "skv", "n", "s", "ssend", "sq", "zatt", "z", "att", "m", "u", "da", "y1", "a", "du", "oacc", "macc", "lse", "lses", "gains", "gs", "gg", "keep", "tin", "tout", "WB")

def forward_kernel(F, nctx, *refs):
    I = dict(zip(A_IN, refs)); at = len(A_IN)
    O = dict(zip(A_OUT, refs[at:])); at += len(A_OUT)
    B = dict(zip(A_BUF, refs[at:])); at += len(A_BUF)
    gsems = refs[at:at + 8]
    own, ins, osem, wsem, ksem, krem, ssem, srem, ysem, yrem, dsem = refs[at + 8:]
    z_, x_, k_, y_ = where_am_i()
    r = x_ * 2 + k_
    rows = B["x"].shape[0]
    half = D // 2
    dev = lambda c: (z_, c, y_)
    gat = Gather(O["G"], F, gsems)
    G = O["G"]
    mine = cols_of(y_)
    WB = B["WB"]
    W = lambda i: WB[i].reshape(D, D)
    def place(w, ref): return pltpu.make_async_copy(ref, G.at[w, z_, :, :, :, mine], own.at[w])
    owns = {0: place(0, I["key"]), 1: place(1, I["value"]), 2: place(2, I["squery"].at[:, :, :, mine]), 4: place(4, I["query"]),
            5: place(5, I["skey"]), 6: place(6, I["svalue"])}
    for j in range(4):
        owns[8 + 2 * j] = place(8 + 2 * j, I["up"].at[:, :, :, pl.ds(j * half, half)])
    tcopies = []
    tsrc = [(3, I["sout"].at[mine]), (7, I["out"])] + [(9 + 2 * j, I["down"].at[pl.ds(j * half, half)]) for j in range(4)]
    for i, (w, ref) in enumerate(tsrc):
        tcopies.append(pltpu.make_async_copy(ref, B["tin"].at[i], ins.at[i]))
        owns[w] = place(w, B["tout"].at[i])
    for w in (0, 1, 2): owns[w].start()
    for c in tcopies: c.start()
    loc = [pltpu.make_async_copy(I["tokens"].at[y_], B["x"].at[:, mine], ins.at[6]),
           pltpu.make_async_copy(I["gtp"], B["gains"].at[:, mine], ins.at[7]),
           pltpu.make_async_copy(I["keep"], B["keep"], ins.at[8]),
           pltpu.make_async_copy(I["gstate"], B["gs"], ins.at[9]),
           pltpu.make_async_copy(I["cotangent"].at[y_], B["g"].at[:, mine], ins.at[10])]
    s0copy = pltpu.make_async_copy(I["s0"], B["s"], ins.at[11])
    for c in loc: c.start()
    for w in (4, 5, 6, 8, 10, 12, 14): owns[w].start()
    barrier_with(F, 4)
    pdev = (z_, r, 1 - y_)
    swap = lambda i, s, d: pltpu.make_async_remote_copy(src_ref=s, dst_ref=d, send_sem=ysem.at[i], recv_sem=yrem.at[i], device_id=pdev, device_id_type=MESH)
    swaps = [swap(0, I["tokens"].at[1 - y_], B["x"].at[:, mine]), swap(1, I["gtp"], B["gains"].at[:, mine]), swap(2, I["cotangent"].at[1 - y_], B["g"].at[:, mine])]
    swaps[0].start(); swaps[1].start()
    owns[0].wait(); owns[1].wait()
    gat.send_z(0)
    def flip(i):
        tcopies[i].wait()
        B["tout"][i] = B["tin"][i].T.reshape(B["tout"].shape[1:])
        owns[tsrc[i][0]].start()
    flip(0)
    owns[2].wait(); owns[3].wait()
    gat.send_z(1)
    for i in range(1, 6): flip(i)
    for w in (4, 5, 6, 7): owns[w].wait()
    gat.send_z(2)
    for i in range(5): loc[i].wait()
    swaps[0].wait_recv(); swaps[1].wait_recv()
    ga, gm, gs = B["gains"].at[pl.ds(0, 1)], B["gains"].at[pl.ds(1, 1)], B["gs"]
    norm_into(B["h"], B["x"], ga)
    puts = []
    def put(name, src=None):
        cp = pltpu.make_async_copy(B[name] if src is None else src, O[name], osem.at[len(puts)])
        cp.start(); puts.append(cp)
    put("x"); put("h"); put("gains")
    gat.stage_y(0)
    gat.send_z(3)
    gat.stage_x(0); gat.stage_y(1)
    for w in range(8, 16): owns[w].wait()
    gat.send_z(4)
    gat.stage_y(2); gat.stage_x(1)
    gat.stage_k(0)
    gat.send_z(5)
    gat.stage_y(3); gat.stage_x(2)
    gat.done(0)
    loads = [pltpu.make_async_copy(G.at[w], WB.at[w], wsem.at[w]) for w in range(8)]
    loads[0].start(); loads[1].start()
    kv, kvp, s = B["kv"], B["kvp"], B["s"]
    kcopy = [pltpu.make_async_remote_copy(src_ref=kv.at[i], dst_ref=kvp.at[i], send_sem=ksem.at[i], recv_sem=krem.at[i],
             device_id=dev(r + 1), device_id_type=MESH) for i in range(2)]
    for i in range(2):
        loads[i].wait()
        kv[i] = nn(B["h"][...], W(i)).astype(BF16)
    gat.send_z(6)
    put("kv")
    gat.stage_k(1)
    gat.stage_y(4); gat.stage_x(3)
    gat.send_z_wide(7)
    swaps[2].start()
    gat.done(1)
    loads[2].start(); loads[3].start()
    @pl.when(r == 0)
    def _():
        s0copy.start()
        kvp[...] = jnp.zeros_like(kvp)
        s0copy.wait()
    loads[2].wait(); loads[3].wait()
    scopy = [pltpu.make_async_remote_copy(src_ref=B["ssend"].at[:, pl.ds(i * half, half)], dst_ref=s.at[:, pl.ds(i * half, half)],
             send_sem=ssem.at[i], recv_sem=srem.at[i], device_id=dev(r + 1), device_id_type=MESH) for i in range(2)]
    def state_in():
        @pl.when(r > 0)
        def _():
            for cp in scopy: cp.wait_recv()
        norm_into(B["n"], s, gs)
    def turn(t, _):
        @pl.when(r == t)
        def _():
            state_in()
            B["sq"][...] = nn(B["n"][...], W(2)).astype(BF16)
            attend_heads(state_parts(kv), B["sq"], B["zatt"], B["lses"], rows, 1, 8)
            for i in range(2):
                cs = pl.ds(i * half, half)
                zz = nt(B["zatt"][...], WB[3].reshape(D, D)[i * half:(i + 1) * half])
                B["z"][:, cs] = zz.astype(BF16)
                kr = B["keep"][:, cs]
                B["ssend"][:, cs] = (kr * s[:, cs].astype(F32) + (1.0 - kr) * zz).astype(BF16)
                scopy[i].start()
            for i in range(2): kcopy[i].start()
        @pl.when(t < 2)
        def _(): gat.stage_y(5 + t)
        @pl.when(t == 2)
        def _(): gat.stage_y_wide(7)
        gat.stage_x(4 + t)
        gat.stage_k(2 + t)
        return 0
    lax.fori_loop(0, nctx - 1, turn, 0)
    gat.done(2); gat.done(3)
    for w in range(4, 8): loads[w].start()
    gat.stage_x_wide(7)
    loads[4].wait()
    B["q"][...] = nn(B["h"][...], W(4)).astype(BF16)
    gat.stage_k(5)
    @pl.when(r == nctx - 1)
    def _(): state_in()
    for name in ("s", "n", "sq", "zatt", "z", "lses", "q"): put(name)
    for i in range(2):
        loads[5 + i].wait()
        B["skv"][i] = nn(B["n"][...], W(5 + i)).astype(BF16)
    put("skv")
    @pl.when(r > 0)
    def _():
        for cp in kcopy: cp.wait_recv()
    put("kvp")
    attend_heads(token_parts(kvp, kv, B["skv"], r == 0, rows, 2), B["q"], B["att"], B["lse"], rows, 2, 4)
    put("att"); put("lse")
    loads[7].wait()
    B["y1"][...] = B["x"][...].astype(F32) + nt(B["att"][...], W(7))
    norm_into(B["m"], B["y1"], gm)
    swaps[2].wait_recv()
    m, g, a, du, u, da = B["m"], B["g"], B["a"], B["du"], B["u"], B["da"]
    def wl(j, i): return pltpu.make_async_copy(G.at[8 + 2 * j + i], WB.at[2 * lax.rem(j, 2) + i], wsem.at[2 * lax.rem(j, 2) + i])
    def dcopy(j, i): return pltpu.make_async_copy(WB.at[4 + 2 * lax.rem(j, 2) + i], O["Dc"].at[2 * j + i], dsem.at[2 * lax.rem(j, 2) + i])
    gat.done(4)
    wl(0, 0).start(); wl(0, 1).start()
    B["oacc"][...] = jnp.zeros_like(B["oacc"])
    B["macc"][...] = jnp.zeros_like(B["macc"])
    def slice_step(j, _):
        b = 2 * lax.rem(j, 2)
        wl(j, 0).wait(); wl(j, 1).wait()
        a[...] = nn(m[...], W(b))
        du[...] = nn(g[...], W(b + 1))
        def body(rs):
            av = a[rs, :]
            sq = av * av
            t = jnp.tanh(G1 * av * (1.0 + G3 * sq))
            u[rs, :] = (0.5 * av * (1.0 + t)).astype(BF16)
            dg = 0.5 * (1.0 + t) + 0.5 * av * (1.0 - t * t) * (G1 * (1.0 + 3.0 * G3 * sq))
            da[rs, :] = (dg * du[rs, :]).astype(BF16)
        rows_loop(rows, 32, body)
        @pl.when(j == 0)
        def _(): gat.stage_k(6)
        @pl.when(j < 3)
        def _():
            gat.done(5 + j)
            wl(j + 1, 0).start(); wl(j + 1, 1).start()
        B["oacc"][...] += nt(u[...], W(b + 1))
        B["macc"][...] += nt(da[...], W(b))
        @pl.when(j >= 2)
        def _():
            dcopy(j - 2, 0).wait(); dcopy(j - 2, 1).wait()
        WB[4 + b] = tn(m[...], da[...]).astype(BF16).reshape(WB.shape[1:])
        dcopy(j, 0).start()
        WB[5 + b] = tn(g[...], u[...]).astype(BF16).reshape(WB.shape[1:])
        dcopy(j, 1).start()
        return 0
    lax.fori_loop(0, 4, slice_step, 0)
    B["gg"][...] = jnp.zeros_like(B["gg"])
    def last(rs):
        yv = B["y1"][rs, :]
        u[rs, :] = (yv + B["oacc"][rs, :]).astype(BF16)
        dv, dgain = norm_back_rows(yv, gm[...], B["macc"][rs, :])
        a[rs, :] = g[rs, :].astype(F32) + dv
        B["gg"][...] += fold8(dgain)
    rows_loop(rows, 32, last)
    put("out", u); put("gy1", a); put("gg")
    for j in (2, 3):
        for i in range(2): dcopy(j, i).wait()
    @pl.when(r < nctx - 1)
    def _():
        for cp in kcopy: cp.wait_send()
        for cp in scopy: cp.wait_send()
    def drains(g_, _):
        gat.drain(g_)
        return 0
    lax.fori_loop(0, 7, drains, 0)
    gat.drain_wide(7)
    for sw in swaps: sw.wait_send()
    for cp in puts: cp.wait()

def forward_call(F, nctx, args):
    rows = args["tokens"].shape[1]
    blk = D // (4 * F)
    sh = lambda *s: jax.ShapeDtypeStruct(s, BF16)
    fl = lambda *s: jax.ShapeDtypeStruct(s, F32)
    R = sh(rows, D)
    R2 = sh(2, rows, D)
    L = fl(HEADS, 1, rows)
    mats = lambda n: sh(n, F, 2, 2, blk, D)
    shapes = dict(G=mats(16), Dc=mats(8), out=R, gg=fl(8, D), h=R, q=R, kv=R2, kvp=R2, skv=R2, n=R, s=R, sq=R, zatt=R, z=R, lse=L, lses=L, att=R, x=R, gy1=fl(rows, D), gains=fl(8, D))
    bufs = dict(x=R, g=R, h=R, q=R, kv=R2, kvp=R2, skv=R2, n=R, s=R, ssend=R, sq=R, zatt=R, z=R, att=R, m=R, u=R, da=R,
        y1=fl(rows, D), a=fl(rows, D), du=fl(rows, D), oacc=fl(rows, D), macc=fl(rows, D), lse=L, lses=L, gains=fl(8, D), gs=fl(1, D), gg=fl(8, D), keep=fl(1, D),
        tin=sh(6, D // 2, D // F), tout=sh(6, 2, 2, blk, D // 2), WB=mats(8))
    S = pltpu.SemaphoreType.DMA
    n = 8
    outs = pl.pallas_call(functools.partial(forward_kernel, F, nctx),
        out_shape=[shapes[k] for k in A_OUT],
        in_specs=[ANY] * len(A_IN), out_specs=[ANY] * len(A_OUT),
        scratch_shapes=[pltpu.VMEM(bufs[k].shape, bufs[k].dtype) for k in A_BUF]
            + [S((n, F - 1)), S((n, F - 1)), S((n, F)), S((n, F)), S((n, F - 1)), S((n, F - 1)), S((n, F)), S((n, F))]
            + [S((16,)), S((12,)), S((len(A_OUT),)), S((8,)), S((2,)), S((2,)), S((2,)), S((2,)), S((3,)), S((3,)), S((4,))],
        compiler_params=pltpu.CompilerParams(collective_id=1, has_side_effects=True, vmem_limit_bytes=62 << 20), name="forward")(*[args[k] for k in A_IN])
    return dict(zip(A_OUT, outs))


B_IN = ("G", "Dc", "out", "gg", "gains", "gs", "keep", "h", "q", "kv", "kvp", "skv", "n", "s", "sq", "zatt", "z", "lse", "lses", "att", "x", "gy1")
B_OUT = ("R", "RX", "OUTF", "GXF", "S0", "SUMS", "DD", "KBH", "B1X", "B1Y", "B2H", "ZB0", "ZB1", "XBH")
B_BUF = ("h", "q", "kv", "kvp", "skv", "n", "s", "sq", "zatt", "z", "lse", "lses", "att", "gy1", "gg", "gains", "gs", "keep",
         "WB", "do", "datt", "dqb", "dkv", "dsend", "dret", "dskv", "dntok", "dsin", "dsout", "ggv",
         "A", "TK", "T1X", "T1Y", "T2", "TZ0", "TZ1", "TX", "lo", "hi", "hi2", "DS1", "dsp", "gin", "g1", "g2")
B_SEM = ("isem", "wsem", "dsem", "psem", "prem", "csem", "crem", "osem", "orem",
         "ks", "kr", "s1", "r1", "s2", "r2", "zs", "zr", "ws", "wr", "vs", "vr", "us", "ur", "bs", "br", "fs", "fr", "xs", "xr", "lsem", "dss", "dsr", "d2s", "d2r", "d3s", "d3r", "g1s", "g1r", "g2s", "g2r", "rsem")

def back_kernel(F, nctx, *refs):
    I = dict(zip(B_IN, refs)); at = len(B_IN)
    O = dict(zip(B_OUT, refs[at:])); at += len(B_OUT)
    B = dict(zip(B_BUF, refs[at:])); at += len(B_BUF)
    S = dict(zip(B_SEM, refs[at:]))
    z, x, k, y = where_am_i()
    c = x * 2 + k
    r = c
    rows = B["do"].shape[0]
    blk = D // (4 * F)
    half = D // 2
    mine, other = cols_of(y), cols_of(1 - y)
    xdev, ydev, kdev = (z, (1 - x) * 2 + k, y), (z, c, 1 - y), (z, x * 2 + 1 - k, y)
    dev = lambda cc: (z, cc, y)
    def local(src, dst, sem): return pltpu.make_async_copy(src, dst, sem)
    def remote(src, dst, s, rr, d):
        return pltpu.make_async_remote_copy(src_ref=src, dst_ref=dst, send_sem=s, recv_sem=rr, device_id=d, device_id_type=MESH)
    def to_z(d): return lax.rem(z - (d + 1) + F, F)
    def from_z(d): return lax.rem(z + d + 1, F)
    W4 = (0, 1, 2, 3)
    slots = {7: (0, 0), 5: (1, 1), 6: (2, 2), 3: (3, 3), 2: (4, 0), 4: (5, 1), 0: (6, 2), 1: (7, 3)}
    wload = {w: local(I["G"].at[w], B["WB"].at[sl], S["wsem"].at[i]) for w, (i, sl) in slots.items()}
    W = lambda w: B["WB"][slots[w][1]].reshape(D, D)
    order = ("gy1", "att", "q", "kv", "kvp", "skv", "lse", "gs", "n", "s", "h", "keep", "sq", "zatt", "z", "lses", "gains", "gg")
    loads = {}
    for i, name in enumerate(order):
        loads[name] = local(I[name], B[name], S["isem"].at[i])
    loads["gy1"].start()
    wload[7].start()
    for name in order[1:]: loads[name].start()
    for w in (5, 6, 3): wload[w].start()
    barrier_with(F, 7, True)
    def ksend_from(ref, p, first_row): return remote(ref.at[pl.ds(first_row, 2), :, :, 1 - k], O["KBH"].at[pl.ds(2 * p, 2)], S["ks"].at[p], S["kr"].at[p], kdev)
    for p in range(4): ksend_from(I["Dc"], p, 2 * p).start()
    oswap = remote(I["out"].at[:, other], O["OUTF"].at[y], S["osem"].at[0], S["orem"].at[0], ydev)
    oown = local(I["out"].at[:, mine], O["OUTF"].at[y], S["rsem"].at[0])
    oswap.start(); oown.start()
    A = B["A"]
    def sl(p): return lax.rem(p, 4)
    def two(p): return lax.rem(p, 2)
    def first(p, e):
        a = A.at[sl(p), e]
        if e == 0: return remote(a.at[:, 1 - x], O["B1X"].at[p], S["s1"].at[p, 0], S["r1"].at[p, 0], xdev)
        return remote(a.at[:, :, :, other], O["B1Y"].at[p], S["s1"].at[p, 1], S["r1"].at[p, 1], ydev)
    def second(p): return remote(A.at[sl(p), 0, :, x, :, other], O["B2H"].at[p], S["s2"].at[p], S["r2"].at[p], ydev)
    def zsend(p, d): return remote(A.at[sl(p), 0, to_z(d), x, :, mine], O["ZB0"].at[p, d], S["zs"].at[p, d], S["zr"].at[p, d], (to_z(d), c, y))
    def zwide(p, d): return remote(A.at[sl(p), 1, to_z(d), :, :, mine], O["ZB1"].at[p, d], S["ws"].at[p, d], S["wr"].at[p, d], (to_z(d), c, y))
    def xswap(p): return remote(B["hi"].at[sl(p)], O["XBH"].at[p], S["vs"].at[p], S["vr"].at[p], xdev)
    def bcast(p, i): return remote(B["lo"].at[two(p)], O["R"].at[2 * p, x, k], S["bs"].at[p, i], S["br"].at[p, i], (kdev, xdev)[i])
    def wide(p): return remote(B["hi2"].at[two(p)], O["R"].at[2 * p + 1, :, k], S["us"].at[p], S["ur"].at[p], kdev)
    def fwd(p):
        rr = O["R"].at[2 * p, 1 - x, k]
        return remote(rr, rr, S["fs"].at[p], S["fr"].at[p], kdev)
    def extra(e, i):
        src = B["lo"].at[0] if e == 0 else B["hi2"].at[0, x]
        return remote(src, O["RX"].at[e, c], S["xs"].at[e, i], S["xr"].at[e, i], (z, lax.rem(c + i, 4), 1 - y))
    def landed(ref, sem): local(ref, ref, sem).wait()
    def plus(a, b): return a + b
    def own_load(p, do):
        @pl.when(p < 4)
        def _(): do(local(I["Dc"].at[pl.ds(2 * p, 2), :, :, k], A.at[sl(p)], S["lsem"].at[0]))
        @pl.when(p >= 4)
        def _(): do(local(O["DD"].at[pl.ds(jnp.maximum(2 * p - 8, 0), 2), :, :, k], A.at[sl(p)], S["lsem"].at[0]))
    def guard(p, body, least=0):
        if isinstance(p, int):
            if least <= p < 8: body()
        else:
            pl.when((p >= least) & (p < 8))(body)
    def sent(p):
        first(p, 0).wait_send()
        first(p, 1).wait_send()
        second(p).wait_send()
        xswap(p).wait_send()
        for d in range(F - 1):
            zsend(p, d).wait_send()
            zwide(p, d).wait_send()
    def sent_last(p):
        bcast(p, 0).wait_send()
        bcast(p, 1).wait_send()
        wide(p).wait_send()
    def lk(p): return local(O["KBH"].at[pl.ds(2 * p, 2)], B["TK"], S["lsem"].at[1])
    def l1x(p): return local(O["B1X"].at[p], B["T1X"], S["lsem"].at[2])
    def l1y(p): return local(O["B1Y"].at[p], B["T1Y"], S["lsem"].at[3])
    def l2(p): return local(O["B2H"].at[p], B["T2"], S["lsem"].at[4])
    def lz0(p): return local(O["ZB0"].at[p], B["TZ0"], S["lsem"].at[5])
    def lz1(p): return local(O["ZB1"].at[p], B["TZ1"], S["lsem"].at[6])
    def lx(p): return local(O["XBH"].at[p], B["TX"], S["lsem"].at[7])
    def rown0(p): return local(B["lo"].at[two(p)], O["R"].at[2 * p, x, k], S["lsem"].at[8])
    def rown1(p): return local(B["hi2"].at[two(p)], O["R"].at[2 * p + 1, :, k], S["lsem"].at[9])
    def pair_step(s):
        def k_in():
            guard(s - 4, lambda: sent(s - 4))
            landed(O["KBH"].at[pl.ds(2 * s, 2)], S["kr"].at[s])
            own_load(s, lambda cp: cp.start())
            lk(s).start()
        def s1_in():
            p = s - 1
            first(p, 0).wait_recv()
            l1x(p).start()
            first(p, 1).wait_recv()
            l1y(p).start()
        def s2_in():
            p = s - 2
            second(p).wait_recv()
            l2(p).start()
            for d in range(F - 1): zwide(p, d).wait_recv()
            lz1(p).start()
        def z_in():
            p = s - 3
            for d in range(F - 1): zsend(p, d).wait_recv()
            lz0(p).start()
            xswap(p).wait_recv()
            lx(p).start()
        def k_do():
            own_load(s, lambda cp: cp.wait())
            lk(s).wait()
            a, t = A.at[sl(s)], B["TK"]
            for e in range(2):
                def add(i, _):
                    zz, xx = lax.div(i, 2), lax.rem(i, 2)
                    a[e, zz, xx] = plus(a[e, zz, xx], t[e, zz, xx])
                    return 0
                lax.fori_loop(0, 2 * F, add, 0)
                first(s, e).start()
        def s1_do():
            p = s - 1
            a = A.at[sl(p)]
            l1x(p).wait()
            def add0(i, _):
                a[0, i, x] = plus(a[0, i, x], B["T1X"][i])
                return 0
            lax.fori_loop(0, F, add0, 0)
            second(p).start()
            l1y(p).wait()
            def add1(i, _):
                for xx in range(2): a[1, i, xx, :, mine] = plus(a[1, i, xx, :, mine], B["T1Y"][i, xx])
                return 0
            lax.fori_loop(0, F, add1, 0)
            for d in range(F - 1): zwide(p, d).start()
        def s2_do():
            p = s - 2
            a = A.at[sl(p)]
            l2(p).wait()
            def add(i, _):
                a[0, i, x, :, mine] = plus(a[0, i, x, :, mine], B["T2"][i])
                return 0
            lax.fori_loop(0, F, add, 0)
            for d in range(F - 1): zsend(p, d).start()
            lz1(p).wait()
            for xx in range(2):
                total = a[1, z, xx, :, mine].astype(F32)
                for d in range(F - 1): total = total + B["TZ1"][d, xx].astype(F32)
                B["hi"][sl(p), xx] = total.astype(BF16)
            xswap(p).start()
        def z_do():
            p = s - 3
            guard(p - 2, lambda: sent_last(p - 2))
            lz0(p).wait()
            total = A[sl(p), 0, z, x, :, mine].astype(F32)
            for d in range(F - 1): total = total + B["TZ0"][d].astype(F32)
            B["lo"][two(p)] = total.astype(BF16)
            for i in range(2): bcast(p, i).start()
            rown0(p).start()
            lx(p).wait()
            for xx in range(2): B["hi2"][two(p), xx] = plus(B["hi"][sl(p), xx], B["TX"][xx])
            wide(p).start()
            rown1(p).start()
            rown0(p).wait()
            rown1(p).wait()
            def special():
                for e in range(2):
                    for i in range(4): extra(e, i).start()
                for e in range(2):
                    for i in range(4): extra(e, i).wait_send()
            if isinstance(p, int):
                if p == 6: special()
            else: pl.when(p == 6)(special)
        def f_do():
            p = s - 4
            landed(O["R"].at[2 * p, 1 - x, k], S["br"].at[p, 1])
            fwd(p).start()
        guard(s, k_in)
        guard(s - 1, s1_in)
        guard(s - 2, s2_in)
        guard(s - 3, z_in)
        guard(s, k_do)
        guard(s - 1, s1_do)
        guard(s - 2, s2_do)
        guard(s - 3, z_do)
        guard(s - 4, f_do)
    ggv = B["ggv"]
    ggv[...] = jnp.zeros_like(ggv)
    loads["gy1"].wait()
    do, datt, dqb, dkv, dskv, dntok, dsin, dsout = (B[i] for i in ("do", "datt", "dqb", "dkv", "dskv", "dntok", "dsin", "dsout"))
    def cast(rs): do[rs, :] = B["gy1"][rs, :].astype(BF16)
    rows_loop(rows, 64, cast)
    wload[7].wait()
    datt[...] = nn(do[...], W(7)).astype(BF16)
    wload[2].start()
    for name in order[1:7]: loads[name].wait()
    hz = F // 2
    def pair_view(ref):
        return lambda i, cs: ref[i * hz:(i + 1) * hz, :, :, :, cs].reshape(rows, HEAD)
    kvp_at, skv_at = pair_view(B["kvp"]), pair_view(B["skv"])
    def parts_of(cs, qc):
        upto = (qc + 1) * (rows // 2)
        return [(lambda: kvp_at(0, cs), lambda: kvp_at(1, cs), lambda s: jnp.where(r == 0, NEG, s)),
                (lambda: B["kv"][0, pl.ds(0, upto), cs], lambda: B["kv"][1, pl.ds(0, upto), cs], lambda s: causal_scores(s, 0, qc * (rows // 2))),
                (lambda: skv_at(0, cs), lambda: skv_at(1, cs), lambda s: s)]
    def sink(i, cs, dk, dv):
        dst = (B["dsend"], dkv, dskv)[i]
        dst[0, :, cs] = dk.astype(dst.dtype)
        dst[1, :, cs] = dv.astype(dst.dtype)
    def halves(i, _):
        pair_step(i)
        attend_heads_back(parts_of, B["q"], datt, B["lse"], dqb, sink, rows, 2, 1, i * (HEADS // 2), HEADS // 2)
        return 0
    lax.fori_loop(0, 2, halves, 0)
    pcopy = remote(B["dsend"], B["dret"], S["psem"].at[0], S["prem"].at[0], dev(r - 1))
    @pl.when(r > 0)
    def _(): pcopy.start()
    wload[5].wait(); wload[6].wait()
    dntok[...] = nt(dskv[0], W(5)) + nt(dskv[1], W(6))
    wload[4].start(); wload[0].start()
    for name in order[7:11]: loads[name].wait()
    hr = rows // 2
    ccopy = [remote(dsout.at[pl.ds(i * hr, hr)], dsin.at[pl.ds(i * hr, hr)], S["csem"].at[i], S["crem"].at[i], dev(r - 1)) for i in range(2)]
    def finish_state(more):
        for i in range(2):
            def body(j, _):
                rs = pl.ds(pl.multiple_of(i * hr + j * 32, 32), 32)
                dv, dgain = norm_back_rows(B["s"][rs, :].astype(F32), B["gs"][...], dntok[rs, :])
                if more: dv = dv + B["keep"][...] * dsin[rs, :].astype(F32)
                dsout[rs, :] = dv.astype(BF16)
                ggv[pl.ds(8, 8), :] += fold8(dgain)
                return 0
            lax.fori_loop(0, hr // 32, body, 0)
            @pl.when(r > 0)
            def _(): ccopy[i].start()
    @pl.when(r == nctx - 1)
    def _(): finish_state(False)
    stages = (B["kvp"], B["skv"])
    def grad_out(i, left, right):
        if i >= 2: pass
        st = stages[i % 2]
        st[...] = tn(left[...], right[...]).astype(BF16).reshape(st.shape)
        local(st, O["DD"].at[i], S["dsem"].at[i]).start()
        if i % 2 == 1:
            for q in (i - 1, i): local(stages[q % 2], O["DD"].at[q], S["dsem"].at[q]).wait()
            ksend_from(O["DD"], 4 + i // 2, i - 1).start()
    grad_out(0, do, B["att"])
    xload = local(I["x"], B["att"], S["rsem"].at[2])
    xload.start()
    grad_out(1, B["n"], dskv.at[0])
    pair_step(2)
    grad_out(2, B["n"], dskv.at[1])
    grad_out(3, B["h"], dqb)
    for name in order[11:]: loads[name].wait()
    wload[3].wait(); wload[2].wait()
    dzb = datt
    def turn(t, _):
        @pl.when(r == nctx - 2 - t)
        def _():
            for cp in ccopy: cp.wait_recv()
            def body(rs):
                d = dsin[rs, :].astype(F32)
                kr = B["keep"][...]
                dzb[rs, :] = ((1.0 - kr) * d).astype(BF16)
                ggv[pl.ds(16, 8), :] += fold8(d * (B["s"][rs, :].astype(F32) - B["z"][rs, :].astype(F32)) * kr * (1.0 - kr))
            rows_loop(rows, 32, body)
            do[...] = nn(dzb[...], W(3)).astype(BF16)
            def sink2(i, cs, dk, dv):
                dkv[0, :, cs] += dk
                dkv[1, :, cs] += dv
            attend_heads_back(state_parts(B["kv"]), B["sq"], do, B["lses"], B["q"], sink2, rows, 1, 4, 0, HEADS)
            dntok[...] += nt(B["q"][...], W(2))
            finish_state(True)
        @pl.when(t < nctx - 2)
        def _(): pair_step(3 + t)
        return 0
    lax.fori_loop(0, nctx - 1, turn, 0)
    n2 = 2 * F
    prow = rows // n2
    me = z * 2 + y
    def zy(i):
        q = lax.rem(me + i + 1, n2)
        return q, (lax.div(q, 2), 0, lax.rem(q, 2))
    def back_of(i): return lax.rem(me - (i + 1) + n2, n2)
    def d1(i):
        q, d = zy(i)
        return remote(dsout.at[pl.ds(pl.multiple_of(q * prow, prow), prow)], B["DS1"].at[me], S["dss"].at[i], S["dsr"].at[i], d)
    def d2(i):
        q, d = zy(i)
        return remote(B["dsp"], O["S0"].at[me], S["d2s"].at[i], S["d2r"].at[i], d)
    def d3(i, d): return remote(O["S0"], O["S0"], S["d3s"].at[i], S["d3r"].at[0], d)
    dsown = local(B["dsp"], O["S0"].at[me], S["rsem"].at[3])
    @pl.when(r == 0)
    def _():
        for i in range(n2 - 1): d1(i).start()
    @pl.when(r == nctx - 1)
    def _():
        B["q"][...] = jnp.zeros_like(B["q"])
        dzb[...] = jnp.zeros_like(dzb)
        B["zatt"][...] = jnp.zeros_like(B["zatt"])
    grad_out(4, B["n"], B["q"])
    grad_out(5, dzb, B["zatt"])
    @pl.when(r < nctx - 1)
    def _(): pcopy.wait_recv()
    @pl.when(r == nctx - 1)
    def _(): B["dret"][...] = jnp.zeros_like(B["dret"])
    wload[1].start()
    for i in range(2):
        def add(rs): dskv[i, rs, :] = (dkv[i, rs, :] + B["dret"][i, rs, :].astype(F32)).astype(BF16)
        rows_loop(rows, 32, add)
    grad_out(6, B["h"], dskv.at[0])
    grad_out(7, B["h"], dskv.at[1])
    pair_step(5)
    wload[4].wait(); wload[0].wait(); wload[1].wait()
    xload.wait()
    dntok[...] = nt(dqb[...], W(4)) + nt(dskv[0], W(0)) + nt(dskv[1], W(1))
    gxb = B["att"]
    def last(rs):
        dv, dgain = norm_back_rows(gxb[rs, :].astype(F32), B["gains"][pl.ds(0, 1), :], dntok[rs, :])
        ggv[pl.ds(0, 8), :] += fold8(dgain)
        gxb[rs, :] = (B["gy1"][rs, :] + dv).astype(BF16)
    rows_loop(rows, 32, last)
    gswap = remote(gxb.at[:, other], O["GXF"].at[y], S["osem"].at[1], S["orem"].at[1], ydev)
    gown = local(gxb.at[:, mine], O["GXF"].at[y], S["rsem"].at[1])
    gswap.start(); gown.start()
    gin = B["gin"]
    gin[...] = jnp.zeros_like(gin)
    for i in range(3): gin[pl.ds(i, 1), :] = jnp.sum(ggv[pl.ds(8 * i, 8), :], axis=0, keepdims=True)
    gin[pl.ds(3, 1), :] = jnp.sum(B["gg"][...], axis=0, keepdims=True)
    around = ((0, 0, 1), (0, 1, 0), (0, 1, 1), (1, 0, 0), (1, 0, 1), (1, 1, 0), (1, 1, 1))
    def plane(i):
        dx, dk, dy = around[i]
        return lax.rem(x + dx, 2), lax.rem(k + dk, 2), lax.rem(y + dy, 2)
    spot = c * 2 + y
    def g1copy(i):
        px, pk, py = plane(i)
        return remote(gin, B["g1"].at[spot], S["g1s"].at[i], S["g1r"].at[i], (z, px * 2 + pk, py))
    def g2copy(d): return remote(gin, B["g2"].at[z], S["g2s"].at[d], S["g2r"].at[d], (to_z(d), c, y))
    B["g1"][spot] = gin[...]
    for i in range(7): g1copy(i).start()
    def tail(i, _):
        s = 6 + i
        @pl.when(i == 1)
        def _():
            for j in range(7):
                g1copy(j).wait_send()
                px, pk, py = plane(j)
                landed(B["g1"].at[(px * 2 + pk) * 2 + py], S["g1r"].at[j])
            total = B["g1"][0]
            for j in range(1, 8): total = total + B["g1"][j]
            gin[...] = total
            B["g2"][z] = total
            for d in range(F - 1): g2copy(d).start()
        @pl.when((i == 1) & (r == 0))
        def _():
            B["DS1"][me] = dsout[pl.ds(pl.multiple_of(me * prow, prow), prow), :]
            for j in range(n2 - 1): landed(B["DS1"].at[back_of(j)], S["dsr"].at[j])
            total = B["DS1"][0].astype(F32)
            for j in range(1, n2): total = total + B["DS1"][j].astype(F32)
            B["dsp"][...] = total.astype(BF16)
            dsown.start()
            for j in range(n2 - 1): d2(j).start()
        @pl.when((i == 2) & (r == 0))
        def _():
            for j in range(n2 - 1): landed(O["S0"].at[back_of(j)], S["d2r"].at[j])
            dsown.wait()
            d3(0, dev(1)).start()
            d3(1, dev(2)).start()
        @pl.when((i == 3) & (r == 2))
        def _():
            landed(O["S0"], S["d3r"].at[0])
            d3(0, dev(3)).start()
        @pl.when(i == 3)
        def _():
            for d in range(F - 1):
                g2copy(d).wait_send()
                landed(B["g2"].at[from_z(d)], S["g2r"].at[d])
            total = B["g2"][0]
            for d in range(1, F): total = total + B["g2"][d]
            gin[...] = total
            local(gin, O["SUMS"], S["rsem"].at[4]).start()
        pair_step(s)
        return 0
    lax.fori_loop(0, 6, tail, 0)
    local(gin, O["SUMS"], S["rsem"].at[4]).wait()
    for p in range(4, 8): sent(p)
    for p in (6, 7): sent_last(p)
    def ends(p, _):
        ksend_from(O["DD"], p, 0).wait_send()
        fwd(p).wait_send()
        landed(O["R"].at[2 * p, x, 1 - k], S["br"].at[p, 0])
        landed(O["R"].at[2 * p, 1 - x, 1 - k], S["fr"].at[p])
        landed(O["R"].at[2 * p + 1, :, 1 - k], S["ur"].at[p])
        return 0
    lax.fori_loop(0, 8, ends, 0)
    for e in range(2):
        for i in range(4): landed(O["RX"].at[e, lax.rem(c - i + 4, 4)], S["xr"].at[e, i])
    @pl.when(r == 0)
    def _():
        for j in range(n2 - 1):
            d1(j).wait_send()
            d2(j).wait_send()
        d3(0, dev(1)).wait_send()
        d3(1, dev(2)).wait_send()
    @pl.when(r == 2)
    def _(): d3(0, dev(3)).wait_send()
    @pl.when((r == 1) | (r == 3))
    def _(): landed(O["S0"], S["d3r"].at[0])
    @pl.when(r > 0)
    def _():
        pcopy.wait_send()
        for cp in ccopy: cp.wait_send()
    oswap.wait(); oown.wait(); gswap.wait(); gown.wait()

def back_call(F, nctx, vals, gs, keep):
    rows = vals["h"].shape[0]
    blk = D // (4 * F)
    half = D // 2
    sh = lambda *s: jax.ShapeDtypeStruct(s, BF16)
    fl = lambda *s: jax.ShapeDtypeStruct(s, F32)
    mats = lambda n: sh(n, F, 2, 2, blk, D)
    R, R2, L = sh(rows, D), sh(2, rows, D), fl(HEADS, 1, rows)
    prow = rows // (2 * F)
    shapes = dict(R=sh(16, 2, 2, blk, half), RX=sh(2, 4, blk, half), OUTF=sh(2, rows, half), GXF=sh(2, rows, half), S0=sh(2 * F, prow, D), SUMS=fl(8, D),
        DD=mats(8), KBH=sh(16, F, 2, blk, D), B1X=sh(8, F, blk, D), B1Y=sh(8, F, 2, blk, half), B2H=sh(8, F, blk, half),
        ZB0=sh(8, F - 1, blk, half), ZB1=sh(8, F - 1, 2, blk, half), XBH=sh(8, 2, blk, half))
    one = sh(F, 2, 2, blk, D)
    bufs = dict(h=R, q=R, kv=R2, kvp=one, skv=one, n=R, s=R, sq=R, zatt=R, z=R, lse=L, lses=L, att=R, gy1=fl(rows, D), gg=fl(8, D), gains=fl(8, D), gs=fl(1, D), keep=fl(1, D),
        WB=mats(4), do=R, datt=R, dqb=R, dkv=fl(2, rows, D), dsend=R2, dret=R2, dskv=R2, dntok=fl(rows, D), dsin=R, dsout=R, ggv=fl(24, D),
        A=sh(4, 2, F, 2, blk, D), TK=sh(2, F, 2, blk, D), T1X=sh(F, blk, D), T1Y=sh(F, 2, blk, half), T2=sh(F, blk, half), TZ0=sh(F - 1, blk, half), TZ1=sh(F - 1, 2, blk, half), TX=sh(2, blk, half),
        lo=sh(2, blk, half), hi=sh(4, 2, blk, half), hi2=sh(2, 2, blk, half), DS1=sh(2 * F, prow, D), dsp=sh(prow, D), gin=fl(8, D), g1=fl(8, 8, D), g2=fl(F, 8, D))
    X = pltpu.SemaphoreType.DMA
    sems = dict(isem=(18,), wsem=(8,), dsem=(8,), psem=(1,), prem=(1,), csem=(2,), crem=(2,), osem=(2,), orem=(2,),
        ks=(8,), kr=(8,), s1=(8, 2), r1=(8, 2), s2=(8,), r2=(8,), zs=(8, F - 1), zr=(8, F - 1), ws=(8, F - 1), wr=(8, F - 1), vs=(8,), vr=(8,), us=(8,), ur=(8,), bs=(8, 2), br=(8, 2), fs=(8,), fr=(8,), xs=(2, 4), xr=(2, 4), lsem=(10,),
        dss=(2 * F,), dsr=(2 * F,), d2s=(2 * F,), d2r=(2 * F,), d3s=(2,), d3r=(1,), g1s=(7,), g1r=(7,), g2s=(F - 1,), g2r=(F - 1,), rsem=(5,))
    args = dict(vals)
    args["gs"], args["keep"] = gs, keep
    args["kvp"], args["skv"] = (args[i].reshape(one.shape) for i in ("kvp", "skv"))
    outs = pl.pallas_call(functools.partial(back_kernel, F, nctx),
        out_shape=[shapes[i] for i in B_OUT], in_specs=[ANY] * len(B_IN), out_specs=[ANY] * len(B_OUT),
        scratch_shapes=[pltpu.VMEM(bufs[i].shape, bufs[i].dtype) for i in B_BUF] + [X(sems[i]) for i in B_SEM],
        compiler_params=pltpu.CompilerParams(collective_id=2, has_side_effects=True, vmem_limit_bytes=63 << 20), name="backward")(*[args[i] for i in B_IN])
    return dict(zip(B_OUT, outs))


def local(
    tokens,
    cotangent,
    w_query,
    w_key,
    w_value,
    w_out,
    w_state_key,
    w_state_value,
    w_state_query,
    w_state_out,
    w_up,
    w_down,
    gain_attn,
    gain_state,
    gain_mlp,
    forget_logit,
    state_init,
):
    fsdp = lax.axis_size("fsdp")
    tp_rank = lax.axis_index("tp")
    ctx_count = lax.axis_size("ctx")
    half = D // 2
    rows = D // fsdp
    blk = rows // 4
    tiles = lambda w: w.reshape(2, 2, blk, w.shape[1])
    args = dict(
        tokens=tokens, cotangent=cotangent, gtp=jnp.pad(jnp.stack([gain_attn, gain_mlp]), ((0, 6), (0, 0))),
        gstate=gain_state[None], keep=jax.nn.sigmoid(forget_logit)[None], s0=state_init,
        key=tiles(w_key), value=tiles(w_value), squery=tiles(w_state_query), sout=w_state_out, query=tiles(w_query),
        skey=tiles(w_state_key), svalue=tiles(w_state_value), out=w_out, up=tiles(w_up), down=w_down)
    vals = forward_call(fsdp, ctx_count, args)
    got = back_call(fsdp, ctx_count, vals, args["gstate"], args["keep"])
    full = got["R"].reshape(16, rows, half).astype(F32)
    r = {w: full[8 + i] for i, w in enumerate((7, 5, 6, 4, 2, 3, 0, 1))}
    rx = got["RX"].reshape(2, rows, half).astype(F32)
    small = got["SUMS"]

    def both(mine, other):
        first = jnp.where(tp_rank == 0, mine, other)
        second = jnp.where(tp_rank == 0, other, mine)
        return jnp.concatenate([first, second], axis=1)

    at = lambda i: lax.dynamic_slice_in_dim(small[i], tp_rank * half, half, 0)
    return (
        got["OUTF"],
        got["GXF"],
        r[4],
        r[0],
        r[1],
        r[7].T,
        r[5],
        r[6],
        both(r[2], rx[0]),
        both(r[3], rx[1]).T,
        full[0:8:2].swapaxes(0, 1).reshape(rows, -1),
        full[1:8:2].swapaxes(1, 2).reshape(-1, rows),
        at(0),
        small[1],
        at(3),
        small[2],
        got["S0"].reshape(state_init.shape).astype(F32),
    )


def solution(mesh):
    placed = (
        P("fsdp", "ctx", "tp"),
        P("fsdp", "ctx", "tp"),
        P("fsdp", "tp"),
        P("fsdp", "tp"),
        P("fsdp", "tp"),
        P("tp", "fsdp"),
        P("fsdp", "tp"),
        P("fsdp", "tp"),
        P("fsdp", None),
        P(None, "fsdp"),
        P("fsdp", "tp"),
        P("tp", "fsdp"),
        P("tp"),
        P(),
        P("tp"),
        P(),
        P(),
    )
    return jax.shard_map(
        local,
        mesh=mesh,
        in_specs=placed,
        out_specs=(
            P("fsdp", "ctx", "tp"),
            P("fsdp", "ctx", "tp"),
            P("fsdp", "tp"),
            P("fsdp", "tp"),
            P("fsdp", "tp"),
            P("tp", "fsdp"),
            P("fsdp", "tp"),
            P("fsdp", "tp"),
            P("fsdp", None),
            P(None, "fsdp"),
            P("fsdp", "tp"),
            P("tp", "fsdp"),
            P("tp"),
            P(),
            P("tp"),
            P(),
            P(),
        ),
        check_vma=False,
    )
```

```python
import functools

import jax
import jax.numpy as jnp
from jax import lax
from jax.experimental import pallas as pl
from jax.experimental.pallas import tpu as pltpu
from jax.sharding import PartitionSpec as P

MESH = pl.DeviceIdType.MESH
ANY = pl.BlockSpec(memory_space=pl.ANY)
D = 1024
HEADS = 8
HEAD = 128
EPS = 1e-06
NEG = -1e30
LOG2E = 1.4426950408889634
F32 = jnp.float32
BF16 = jnp.bfloat16
SCALE = HEAD ** -0.5
CE = SCALE * LOG2E

def nn(a, b): return lax.dot_general(a, b, (((1,), (0,)), ((), ())), preferred_element_type=F32)
def nt(a, b): return lax.dot_general(a, b, (((1,), (1,)), ((), ())), preferred_element_type=F32)
def tn(a, b): return lax.dot_general(a, b, (((0,), (0,)), ((), ())), preferred_element_type=F32)

def rows_loop(total, step, body):
    def run(i, _):
        body(pl.ds(pl.multiple_of(i * step, step), step))
        return 0
    lax.fori_loop(0, total // step, run, 0)

def inverse_of(v):
    return lax.rsqrt(jnp.mean(v * v, axis=-1, keepdims=True) + EPS)

def norm_into(dst, src, gain):
    def body(rs):
        v = src[rs, :].astype(F32)
        dst[rs, :] = (v * inverse_of(v) * gain[...]).astype(dst.dtype)
    rows_loop(src.shape[0], 32, body)

def head_cols(h): return pl.ds(pl.multiple_of(h * HEAD, HEAD), HEAD)

def causal_scores(s, first_key, first_query):
    keys = lax.broadcasted_iota(jnp.int32, s.shape, 0) + first_key
    qs = lax.broadcasted_iota(jnp.int32, s.shape, 1) + first_query
    return jnp.where(keys <= qs, s, NEG)

def over_heads(one, unroll, h0, count):
    def body(i, _):
        for u in range(unroll):
            one(h0 + i * unroll + u)
        return 0
    lax.fori_loop(0, count // unroll, body, 0)

def attend_heads(parts_of, q, out, lse, rows, chunks, unroll, h0=0, count=HEADS):
    step = rows // chunks
    def one(h):
        cs = head_cols(h)
        for qc in range(chunks):
            rs = pl.ds(qc * step, step)
            qh = q[rs, cs]
            parts = parts_of(cs, qc)
            scores = [mask(nt(keys(), qh)) for keys, values, mask in parts]
            big = functools.reduce(jnp.maximum, [jnp.max(s, axis=0, keepdims=True) for s in scores])
            es = [jnp.exp2((s - big) * CE) for s in scores]
            total = functools.reduce(jnp.add, [jnp.sum(e, axis=0, keepdims=True) for e in es])
            inv = 1.0 / total
            acc = functools.reduce(jnp.add, [tn((e * inv).astype(BF16), p[1]()) for e, p in zip(es, parts)])
            out[rs, cs] = acc.astype(BF16)
            lse[h, :, pl.ds(qc * step, step)] = big * CE + jnp.log2(total)
    over_heads(one, unroll, h0, count)

def token_parts(kvp, kv, skv, first, rows, chunks):
    def parts_of(cs, qc):
        step = rows // chunks
        upto = (qc + 1) * step
        same = lambda s: s
        earlier = lambda s: jnp.where(first, NEG, s)
        causal = lambda s: causal_scores(s, 0, qc * step)
        return [(lambda: kvp[0, :, cs], lambda: kvp[1, :, cs], earlier),
                (lambda: kv[0, pl.ds(0, upto), cs], lambda: kv[1, pl.ds(0, upto), cs], causal),
                (lambda: skv[0, :, cs], lambda: skv[1, :, cs], same)]
    return parts_of

def state_parts(kv):
    def parts_of(cs, qc):
        return [(lambda: kv[0, :, cs], lambda: kv[1, :, cs], lambda s: s)]
    return parts_of

def chain_barrier(r, n, dev):
    bar = pltpu.get_barrier_semaphore()
    @pl.when(r > 0)
    def _(): pl.semaphore_signal(bar, inc=1, device_id=dev(r - 1), device_id_type=MESH)
    @pl.when(r < n - 1)
    def _(): pl.semaphore_signal(bar, inc=1, device_id=dev(r + 1), device_id_type=MESH)
    pl.semaphore_wait(bar, jnp.where(r > 0, 1, 0) + jnp.where(r < n - 1, 1, 0))

def where_am_i():
    f = lax.axis_index("fsdp")
    c = lax.axis_index("ctx")
    return f, lax.div(c, 2), lax.rem(c, 2), lax.axis_index("tp")

def cols_of(t):
    return pl.ds(pl.multiple_of(t * (D // 2), D // 2), D // 2)

G1 = 0.7978845608028654
G3 = 0.044715

def norm_back_rows(v, gain, e):
    inv = inverse_of(v)
    w = e * gain
    proj = jnp.sum(w * v, axis=-1, keepdims=True) * (1.0 / D)
    return inv * w - v * (inv * inv * inv) * proj, e * v * inv

def fold8(v):
    return functools.reduce(jnp.add, [v[i * 8:(i + 1) * 8] for i in range(v.shape[0] // 8)])

def attend_heads_back(parts_of, q, datt, lse, dq, sink, rows, chunks, unroll, h0, count):
    step = rows // chunks
    def one(h):
        cs = head_cols(h)
        sums = None
        for qc in range(chunks):
            rs = pl.ds(qc * step, step)
            qh = q[rs, cs]
            gh = datt[rs, cs]
            ls = lse[h, :, pl.ds(qc * step, step)]
            parts = parts_of(cs, qc)
            ps = [jnp.exp2(p[2](nt(p[0](), qh)) * CE - ls) for p in parts]
            dps = [nt(p[1](), gh) for p in parts]
            delta = functools.reduce(jnp.add, [jnp.sum(a * b, axis=0, keepdims=True) for a, b in zip(ps, dps)])
            dss = [(a * (b - delta)).astype(BF16) for a, b in zip(ps, dps)]
            dq[rs, cs] = (functools.reduce(jnp.add, [tn(d, p[0]()) for d, p in zip(dss, parts)]) * SCALE).astype(dq.dtype)
            new = [(nn(d, qh), nn(a.astype(BF16), gh)) for a, d in zip(ps, dss)]
            if sums is None: sums = new
            else:
                merged = []
                for (k0, v0), (k1, v1) in zip(sums, new):
                    n0 = k0.shape[0]
                    if n0 < k1.shape[0]:
                        k1 = jnp.concatenate([k0 + k1[:n0], k1[n0:]], axis=0)
                        v1 = jnp.concatenate([v0 + v1[:n0], v1[n0:]], axis=0)
                    else:
                        k1, v1 = k0 + k1, v0 + v1
                    merged.append((k1, v1))
                sums = merged
        for i, (dk, dv) in enumerate(sums): sink(i, cs, dk * SCALE, dv)
    over_heads(one, unroll, h0, count)


class Gather:
    def __init__(self, G, own, F, sems):
        self.G, self.own, self.F, self.sems = G, own, F, sems
        self.z, self.x, self.k, self.y = where_am_i()

    def src_z(self, d):
        return lax.rem(self.z + d + 1, self.F)

    def region(self, g, z, x, k, cols=None):
        w = pl.ds(2 * g, 2)
        if cols is None:
            return self.G.at[w, z, x, k]
        return self.G.at[w, z, x, k, :, cols]

    def both_x(self, g, z, k, cols=None):
        w = pl.ds(2 * g, 2)
        if cols is None:
            return self.G.at[w, z, :, k]
        return self.G.at[w, z, :, k, :, cols]

    def remote(self, ref, i, g, d, dev, src=None):
        return pltpu.make_async_remote_copy(
            src_ref=ref if src is None else src, dst_ref=ref, send_sem=self.sems[i].at[g, d], recv_sem=self.sems[i + 1].at[g, d],
            device_id=dev, device_id_type=MESH)

    def landed(self, ref, i, g, d):
        pltpu.make_async_copy(ref, ref, self.sems[i + 1].at[g, d]).wait()

    def zcopy(self, g, d):
        to = lax.rem(self.z - (d + 1) + self.F, self.F)
        return self.remote(self.region(g, self.z, self.x, self.k, cols_of(self.y)), 0, g, d, (to, self.x * 2 + self.k, self.y), self.own.at[pl.ds(2 * g, 2), self.x, self.k])

    def ycopy(self, g, d):
        dev = (self.z, self.x * 2 + self.k, 1 - self.y)
        if d == self.F - 1:
            return self.remote(self.both_x(g, self.z, self.k, cols_of(self.y)), 2, g, d, dev, self.own.at[pl.ds(2 * g, 2), :, self.k])
        return self.remote(self.region(g, self.src_z(d), self.x, self.k, cols_of(self.y)), 2, g, d, dev)

    def xcopy(self, g, d):
        return self.remote(self.region(g, self.src_z(d), self.x, self.k), 4, g, d, (self.z, (1 - self.x) * 2 + self.k, self.y))

    def kcopy(self, g, d):
        dev = (self.z, self.x * 2 + 1 - self.k, self.y)
        if d == self.F - 1:
            return self.remote(self.both_x(g, self.z, self.k, cols_of(1 - self.y)), 6, g, d, dev)
        return self.remote(self.both_x(g, self.src_z(d), self.k), 6, g, d, dev)

    def send_z(self, g):
        for d in range(self.F - 1):
            self.zcopy(g, d).start()
        self.ycopy(g, self.F - 1).start()

    def stage_y(self, g):
        for d in range(self.F - 1):
            self.landed(self.region(g, self.src_z(d), self.x, self.k, cols_of(self.y)), 0, g, d)
            self.ycopy(g, d).start()

    def stage_x(self, g):
        o = cols_of(1 - self.y)
        for d in range(self.F - 1):
            self.landed(self.region(g, self.src_z(d), self.x, self.k, o), 2, g, d)
            self.xcopy(g, d).start()
        self.landed(self.both_x(g, self.z, self.k, o), 2, g, self.F - 1)
        self.kcopy(g, self.F - 1).start()

    def stage_k(self, g):
        for d in range(self.F - 1):
            self.landed(self.region(g, self.src_z(d), 1 - self.x, self.k), 4, g, d)
            self.kcopy(g, d).start()

    def done(self, g):
        for d in range(self.F - 1):
            self.landed(self.both_x(g, self.src_z(d), 1 - self.k), 6, g, d)
        self.landed(self.both_x(g, self.z, 1 - self.k, cols_of(1 - self.y)), 6, g, self.F - 1)

    def zwide(self, g, d):
        to = lax.rem(self.z - (d + 1) + self.F, self.F)
        return self.remote(self.both_x(g, self.z, self.k, cols_of(self.y)), 0, g, d, (to, self.x * 2 + self.k, self.y), self.own.at[pl.ds(2 * g, 2), :, self.k])

    def ywide(self, g, d):
        return self.remote(self.both_x(g, self.src_z(d), self.k, cols_of(self.y)), 2, g, d, (self.z, self.x * 2 + self.k, 1 - self.y))

    def send_z_wide(self, g):
        for d in range(self.F - 1):
            self.zwide(g, d).start()
        self.ycopy(g, self.F - 1).start()

    def stage_y_wide(self, g):
        for d in range(self.F - 1):
            self.landed(self.both_x(g, self.src_z(d), self.k, cols_of(self.y)), 0, g, d)
            self.ywide(g, d).start()

    def stage_x_wide(self, g):
        for d in range(self.F - 1):
            self.landed(self.both_x(g, self.src_z(d), self.k, cols_of(1 - self.y)), 2, g, d)
            self.kcopy(g, d).start()
        self.landed(self.both_x(g, self.z, self.k, cols_of(1 - self.y)), 2, g, self.F - 1)
        self.kcopy(g, self.F - 1).start()

    def drain_wide(self, g):
        for d in range(self.F):
            if d < self.F - 1:
                self.zwide(g, d).wait_send()
                self.ywide(g, d).wait_send()
            self.kcopy(g, d).wait_send()
        self.ycopy(g, self.F - 1).wait_send()

    def drain(self, g):
        for d in range(self.F):
            if d < self.F - 1:
                self.zcopy(g, d).wait_send()
                self.xcopy(g, d).wait_send()
            self.ycopy(g, d).wait_send()
            self.kcopy(g, d).wait_send()

def barrier_with(F, count, across=False):
    z, x, k, y = where_am_i()
    bar = pltpu.get_barrier_semaphore()
    peers = [(lax.rem(z + d + 1, F), x * 2 + k, y) for d in range(F - 1)]
    for dx, dk, dy in ((0, 0, 1), (1, 0, 0), (0, 1, 0), (1, 1, 0), (1, 0, 1), (0, 1, 1), (1, 1, 1))[:count]:
        peers.append((z, lax.rem(x + dx, 2) * 2 + lax.rem(k + dk, 2), lax.rem(y + dy, 2)))
    if across:
        peers += [(lax.rem(z + d + 1, F), x * 2 + k, 1 - y) for d in range(F - 1)]
    for p in peers:
        pl.semaphore_signal(bar, inc=1, device_id=p, device_id_type=MESH)
    pl.semaphore_wait(bar, len(peers))

A_IN = ("tokens", "cotangent", "gtp", "gstate", "keep", "s0", "key", "value", "squery", "sout", "query", "skey", "svalue", "out", "up", "down")
A_OUT = ("G", "Dc", "out", "gg", "h", "q", "kv", "kvp", "skv", "n", "s", "sq", "zatt", "z", "lse", "lses", "att", "x", "gy1", "gains")
A_BUF = ("x", "g", "h", "q", "kv", "kvp", "skv", "n", "s", "ssend", "sq", "zatt", "z", "att", "m", "u", "da", "y1", "a", "du", "oacc", "macc", "lse", "lses", "gains", "gs", "gg", "keep", "tin", "own", "WB")

def forward_kernel(F, nctx, *refs):
    I = dict(zip(A_IN, refs)); at = len(A_IN)
    O = dict(zip(A_OUT, refs[at:])); at += len(A_OUT)
    B = dict(zip(A_BUF, refs[at:])); at += len(A_BUF)
    gsems = refs[at:at + 8]
    osems, ins, osem, wsem, ksem, krem, ssem, srem, ysem, yrem, dsem = refs[at + 8:]
    z_, x_, k_, y_ = where_am_i()
    r = x_ * 2 + k_
    rows = B["x"].shape[0]
    half = D // 2
    dev = lambda c: (z_, c, y_)
    gat = Gather(O["G"], B["own"], F, gsems)
    G = O["G"]
    mine = cols_of(y_)
    WB = B["WB"]
    W = lambda i: WB[i].reshape(D, D)
    own = B["own"]
    def take(w, ref): return pltpu.make_async_copy(ref, own.at[w], osems.at[w])
    def place(w): return pltpu.make_async_copy(own.at[w], G.at[w, z_, :, :, :, mine], osems.at[w])
    takes = {0: take(0, I["key"]), 1: take(1, I["value"]), 2: take(2, I["squery"].at[:, :, :, mine]), 4: take(4, I["query"]),
             5: take(5, I["skey"]), 6: take(6, I["svalue"])}
    for j in range(4):
        takes[8 + 2 * j] = take(8 + 2 * j, I["up"].at[:, :, :, pl.ds(j * half, half)])
    tsrc = [(3, I["sout"].at[mine]), (7, I["out"])] + [(9 + 2 * j, I["down"].at[pl.ds(j * half, half)]) for j in range(4)]
    tcopies = {w: pltpu.make_async_copy(ref, B["tin"].at[i], ins.at[i]) for i, (w, ref) in enumerate(tsrc)}
    def ready(w):
        if w in tcopies:
            tcopies[w].wait()
            own[w] = B["tin"][[v for v, _ in tsrc].index(w)].T.reshape(own.shape[1:])
        else:
            takes[w].wait()
        place(w).start()
    for w in (0, 1, 2): takes[w].start()
    tcopies[3].start()
    loc = [pltpu.make_async_copy(I["tokens"].at[y_], B["x"].at[:, mine], ins.at[6]),
           pltpu.make_async_copy(I["gtp"], B["gains"].at[:, mine], ins.at[7]),
           pltpu.make_async_copy(I["keep"], B["keep"], ins.at[8]),
           pltpu.make_async_copy(I["gstate"], B["gs"], ins.at[9]),
           pltpu.make_async_copy(I["cotangent"].at[y_], B["g"].at[:, mine], ins.at[10])]
    s0copy = pltpu.make_async_copy(I["s0"], B["s"], ins.at[11])
    for c in loc: c.start()
    for w in (4, 5, 6): takes[w].start()
    tcopies[7].start()
    for j in range(4):
        takes[8 + 2 * j].start()
        tcopies[9 + 2 * j].start()
    barrier_with(F, 4)
    pdev = (z_, r, 1 - y_)
    swap = lambda i, s, d: pltpu.make_async_remote_copy(src_ref=s, dst_ref=d, send_sem=ysem.at[i], recv_sem=yrem.at[i], device_id=pdev, device_id_type=MESH)
    swaps = [swap(0, I["tokens"].at[1 - y_], B["x"].at[:, mine]), swap(1, I["gtp"], B["gains"].at[:, mine]), swap(2, I["cotangent"].at[1 - y_], B["g"].at[:, mine])]
    swaps[0].start(); swaps[1].start()
    ready(0); ready(1)
    gat.send_z(0)
    ready(2); ready(3)
    gat.send_z(1)
    ready(4); ready(5)
    gat.send_z(2)
    for i in range(5): loc[i].wait()
    swaps[0].wait_recv(); swaps[1].wait_recv()
    ga, gm, gs = B["gains"].at[pl.ds(0, 1)], B["gains"].at[pl.ds(1, 1)], B["gs"]
    norm_into(B["h"], B["x"], ga)
    puts = []
    def put(name, src=None):
        cp = pltpu.make_async_copy(B[name] if src is None else src, O[name], osem.at[len(puts)])
        cp.start(); puts.append(cp)
    kv, kvp, s = B["kv"], B["kvp"], B["s"]
    xcopy = pltpu.make_async_remote_copy(src_ref=B["x"], dst_ref=B["att"], send_sem=ksem.at[0], recv_sem=krem.at[0], device_id=dev(r + 1), device_id_type=MESH)
    @pl.when(r < nctx - 1)
    def _(): xcopy.start()
    put("x"); put("h"); put("gains")
    ready(6); ready(7)
    gat.send_z(3)
    gat.stage_y(0)
    ready(8); ready(9)
    gat.send_z(4)
    gat.stage_y(1); gat.stage_x(0)
    ready(10); ready(11)
    gat.send_z(5)
    @pl.when(r == 0)
    def _():
        s0copy.start()
        kvp[...] = jnp.zeros_like(kvp)
        s0copy.wait()
    @pl.when(r > 0)
    def _():
        xcopy.wait_recv()
        norm_into(B["zatt"], B["att"], ga)
    gat.stage_y(2); gat.stage_x(1)
    ready(12); ready(13)
    gat.send_z(6)
    gat.stage_k(0)
    gat.stage_y(3)
    ready(14); ready(15)
    gat.send_z_wide(7)
    loads = [pltpu.make_async_copy(G.at[w], WB.at[w], wsem.at[w]) for w in range(8)]
    gat.done(0)
    for w in (0, 1):
        place(w).wait()
        loads[w].start()
    for i in range(2):
        loads[i].wait()
        kv[i] = nn(B["h"][...], W(i)).astype(BF16)
    put("kv")
    gat.stage_x(2)
    @pl.when(r > 0)
    def _():
        for i in range(2): kvp[i] = nn(B["zatt"][...], W(i)).astype(BF16)
    put("kvp")
    gat.stage_y(4)
    gat.stage_k(1)
    swaps[2].start()
    gat.done(1)
    for w in (2, 3):
        place(w).wait()
        loads[w].start()
    scopy = [pltpu.make_async_remote_copy(src_ref=B["ssend"].at[:, pl.ds(i * half, half)], dst_ref=s.at[:, pl.ds(i * half, half)],
             send_sem=ssem.at[i], recv_sem=srem.at[i], device_id=dev(r + 1), device_id_type=MESH) for i in range(2)]
    def state_in():
        @pl.when(r > 0)
        def _():
            for cp in scopy: cp.wait_recv()
        norm_into(B["n"], s, gs)
    loads[2].wait(); loads[3].wait()
    def chain_step():
        state_in()
        B["sq"][...] = nn(B["n"][...], W(2)).astype(BF16)
        attend_heads(state_parts(kv), B["sq"], B["zatt"], B["lses"], rows, 1, 8)
        for i in range(2):
            cs = pl.ds(i * half, half)
            zz = nt(B["zatt"][...], WB[3].reshape(D, D)[i * half:(i + 1) * half])
            B["z"][:, cs] = zz.astype(BF16)
            kr = B["keep"][:, cs]
            B["ssend"][:, cs] = (kr * s[:, cs].astype(F32) + (1.0 - kr) * zz).astype(BF16)
            scopy[i].start()
    def slot(i, _):
        def when(k, body): pl.when(i == k)(body)
        def s1a(): gat.stage_y(6)
        when(1, s1a)
        def s2a():
            gat.stage_x(5)
            gat.stage_y_wide(7)
            gat.done(3)
            for w in (6, 7):
                place(w).wait()
                loads[w].start()
        when(2, s2a)
        def s3a():
            gat.stage_k(4)
            gat.stage_x(6)
        when(3, s3a)
        @pl.when((i == r) & (r < nctx - 1))
        def _(): chain_step()
        def s0b():
            gat.stage_y(5)
            gat.stage_x(3)
            gat.stage_k(2)
        when(0, s0b)
        def s1b():
            gat.stage_x(4)
            gat.done(2)
            for w in (4, 5):
                place(w).wait()
                loads[w].start()
            gat.stage_k(3)
            loads[4].wait()
            B["q"][...] = nn(B["h"][...], W(4)).astype(BF16)
        when(1, s1b)
        def s3b():
            @pl.when(r == nctx - 1)
            def _(): state_in()
            for j in range(2):
                loads[5 + j].wait()
                B["skv"][j] = nn(B["n"][...], W(5 + j)).astype(BF16)
        when(3, s3b)
        def s6():
            gat.stage_k(5)
        when(6, s6)
        @pl.when(i >= 4)
        def _(): attend_heads(token_parts(kvp, kv, B["skv"], r == 0, rows, 2), B["q"], B["att"], B["lse"], rows, 2, 2, 2 * (i - 4), 2)
        return 0
    lax.fori_loop(0, 8, slot, 0)
    for name in ("s", "n", "sq", "zatt", "z", "lses", "q", "skv", "att", "lse"): put(name)
    loads[7].wait()
    B["y1"][...] = B["x"][...].astype(F32) + nt(B["att"][...], W(7))
    norm_into(B["m"], B["y1"], gm)
    swaps[2].wait_recv()
    m, g, a, du, u, da = B["m"], B["g"], B["a"], B["du"], B["u"], B["da"]
    def wl(j, i): return pltpu.make_async_copy(G.at[8 + 2 * j + i], WB.at[2 * lax.rem(j, 2) + i], wsem.at[2 * lax.rem(j, 2) + i])
    def dcopy(j, i): return pltpu.make_async_copy(WB.at[4 + 2 * lax.rem(j, 2) + i], O["Dc"].at[2 * j + i], dsem.at[2 * lax.rem(j, 2) + i])
    for w in range(8, 16): place(w).wait()
    gat.done(4)
    wl(0, 0).start(); wl(0, 1).start()
    B["oacc"][...] = jnp.zeros_like(B["oacc"])
    B["macc"][...] = jnp.zeros_like(B["macc"])
    def slice_step(j, _):
        b = 2 * lax.rem(j, 2)
        wl(j, 0).wait(); wl(j, 1).wait()
        a[...] = nn(m[...], W(b))
        du[...] = nn(g[...], W(b + 1))
        def body(rs):
            av = a[rs, :]
            sq = av * av
            t = jnp.tanh(G1 * av * (1.0 + G3 * sq))
            u[rs, :] = (0.5 * av * (1.0 + t)).astype(BF16)
            dg = 0.5 * (1.0 + t) + 0.5 * av * (1.0 - t * t) * (G1 * (1.0 + 3.0 * G3 * sq))
            da[rs, :] = (dg * du[rs, :]).astype(BF16)
        rows_loop(rows, 32, body)
        B["oacc"][...] += nt(u[...], W(b + 1))
        @pl.when(j == 0)
        def _(): gat.stage_x_wide(7)
        B["macc"][...] += nt(da[...], W(b))
        @pl.when(j >= 2)
        def _():
            dcopy(j - 2, 0).wait(); dcopy(j - 2, 1).wait()
        WB[4 + b] = tn(m[...], da[...]).astype(BF16).reshape(WB.shape[1:])
        dcopy(j, 0).start()
        @pl.when(j == 0)
        def _(): gat.stage_k(6)
        @pl.when(j < 3)
        def _():
            gat.done(5 + j)
            wl(j + 1, 0).start(); wl(j + 1, 1).start()
        WB[5 + b] = tn(g[...], u[...]).astype(BF16).reshape(WB.shape[1:])
        dcopy(j, 1).start()
        return 0
    lax.fori_loop(0, 4, slice_step, 0)
    B["gg"][...] = jnp.zeros_like(B["gg"])
    def last(rs):
        yv = B["y1"][rs, :]
        u[rs, :] = (yv + B["oacc"][rs, :]).astype(BF16)
        dv, dgain = norm_back_rows(yv, gm[...], B["macc"][rs, :])
        a[rs, :] = g[rs, :].astype(F32) + dv
        B["gg"][...] += fold8(dgain)
    rows_loop(rows, 32, last)
    put("out", u); put("gy1", a); put("gg")
    for j in (2, 3):
        for i in range(2): dcopy(j, i).wait()
    @pl.when(r < nctx - 1)
    def _():
        xcopy.wait_send()
        for cp in scopy: cp.wait_send()
    def drains(g_, _):
        gat.drain(g_)
        return 0
    lax.fori_loop(0, 7, drains, 0)
    gat.drain_wide(7)
    for sw in swaps: sw.wait_send()
    for cp in puts: cp.wait()

def forward_call(F, nctx, args):
    rows = args["tokens"].shape[1]
    blk = D // (4 * F)
    sh = lambda *s: jax.ShapeDtypeStruct(s, BF16)
    fl = lambda *s: jax.ShapeDtypeStruct(s, F32)
    R = sh(rows, D)
    R2 = sh(2, rows, D)
    L = fl(HEADS, 1, rows)
    mats = lambda n: sh(n, F, 2, 2, blk, D)
    shapes = dict(G=mats(16), Dc=mats(8), out=R, gg=fl(8, D), h=R, q=R, kv=R2, kvp=R2, skv=R2, n=R, s=R, sq=R, zatt=R, z=R, lse=L, lses=L, att=R, x=R, gy1=fl(rows, D), gains=fl(8, D))
    bufs = dict(x=R, g=R, h=R, q=R, kv=R2, kvp=R2, skv=R2, n=R, s=R, ssend=R, sq=R, zatt=R, z=R, att=R, m=R, u=R, da=R,
        y1=fl(rows, D), a=fl(rows, D), du=fl(rows, D), oacc=fl(rows, D), macc=fl(rows, D), lse=L, lses=L, gains=fl(8, D), gs=fl(1, D), gg=fl(8, D), keep=fl(1, D),
        tin=sh(6, D // 2, D // F), own=sh(16, 2, 2, blk, D // 2), WB=mats(8))
    S = pltpu.SemaphoreType.DMA
    n = 8
    outs = pl.pallas_call(functools.partial(forward_kernel, F, nctx),
        out_shape=[shapes[k] for k in A_OUT],
        in_specs=[ANY] * len(A_IN), out_specs=[ANY] * len(A_OUT),
        scratch_shapes=[pltpu.VMEM(bufs[k].shape, bufs[k].dtype) for k in A_BUF]
            + [S((n, F - 1)), S((n, F - 1)), S((n, F)), S((n, F)), S((n, F - 1)), S((n, F - 1)), S((n, F)), S((n, F))]
            + [S((16,)), S((12,)), S((len(A_OUT),)), S((8,)), S((2,)), S((2,)), S((2,)), S((2,)), S((3,)), S((3,)), S((4,))],
        compiler_params=pltpu.CompilerParams(collective_id=1, has_side_effects=True, vmem_limit_bytes=62 << 20), name="forward")(*[args[k] for k in A_IN])
    return dict(zip(A_OUT, outs))


B_IN = ("G", "Dc", "out", "gg", "gains", "gs", "keep", "h", "q", "kv", "kvp", "skv", "n", "s", "sq", "zatt", "z", "lse", "lses", "att", "x", "gy1")
B_OUT = ("R", "RX", "OUTF", "GXF", "S0", "SUMS", "DD", "KBH", "B1X", "B1Y", "B2H", "ZB0", "ZB1", "XBH")
B_BUF = ("h", "q", "kv", "kvp", "skv", "n", "s", "sq", "zatt", "z", "lse", "lses", "att", "gy1", "gg", "gains", "gs", "keep",
         "WB", "do", "datt", "dqb", "dkv", "dsend", "dret", "dskv", "dntok", "dsin", "dsout", "ggv",
         "A", "TK", "T1X", "T1Y", "T2", "TZ0", "TZ1", "TX", "lo", "hi", "hi2", "DS1", "dsp", "gin", "g1", "g2")
B_SEM = ("isem", "wsem", "dsem", "psem", "prem", "csem", "crem", "osem", "orem",
         "ks", "kr", "s1", "r1", "s2", "r2", "zs", "zr", "ws", "wr", "vs", "vr", "us", "ur", "bs", "br", "fs", "fr", "xs", "xr", "lsem", "dss", "dsr", "d2s", "d2r", "d3s", "d3r", "g1s", "g1r", "g2s", "g2r", "rsem")

def back_kernel(F, nctx, *refs):
    I = dict(zip(B_IN, refs)); at = len(B_IN)
    O = dict(zip(B_OUT, refs[at:])); at += len(B_OUT)
    B = dict(zip(B_BUF, refs[at:])); at += len(B_BUF)
    S = dict(zip(B_SEM, refs[at:]))
    z, x, k, y = where_am_i()
    c = x * 2 + k
    r = c
    rows = B["do"].shape[0]
    blk = D // (4 * F)
    half = D // 2
    mine, other = cols_of(y), cols_of(1 - y)
    xdev, ydev, kdev = (z, (1 - x) * 2 + k, y), (z, c, 1 - y), (z, x * 2 + 1 - k, y)
    dev = lambda cc: (z, cc, y)
    def local(src, dst, sem): return pltpu.make_async_copy(src, dst, sem)
    def remote(src, dst, s, rr, d):
        return pltpu.make_async_remote_copy(src_ref=src, dst_ref=dst, send_sem=s, recv_sem=rr, device_id=d, device_id_type=MESH)
    def to_z(d): return lax.rem(z - (d + 1) + F, F)
    def from_z(d): return lax.rem(z + d + 1, F)
    W4 = (0, 1, 2, 3)
    slots = {7: (0, 0), 5: (1, 1), 6: (2, 2), 3: (3, 3), 2: (4, 0), 4: (5, 1), 0: (6, 2), 1: (7, 3)}
    wload = {w: local(I["G"].at[w], B["WB"].at[sl], S["wsem"].at[i]) for w, (i, sl) in slots.items()}
    W = lambda w: B["WB"][slots[w][1]].reshape(D, D)
    order = ("gy1", "att", "q", "kv", "kvp", "skv", "lse", "gs", "n", "s", "h", "keep", "sq", "zatt", "z", "lses", "gains", "gg")
    loads = {}
    for i, name in enumerate(order):
        loads[name] = local(I[name], B[name], S["isem"].at[i])
    loads["gy1"].start()
    wload[7].start()
    for name in order[1:]: loads[name].start()
    for w in (5, 6, 3): wload[w].start()
    barrier_with(F, 7, True)
    def ksend_from(ref, p, first_row): return remote(ref.at[pl.ds(first_row, 2), :, :, 1 - k], O["KBH"].at[pl.ds(2 * p, 2)], S["ks"].at[p], S["kr"].at[p], kdev)
    for p in range(4): ksend_from(I["Dc"], p, 2 * p).start()
    oload = local(I["out"], B["dsout"], S["rsem"].at[0])
    oload.start()
    oswap = remote(B["dsout"].at[:, other], O["OUTF"].at[y], S["osem"].at[0], S["orem"].at[0], ydev)
    oown = local(B["dsout"].at[:, mine], O["OUTF"].at[y], S["rsem"].at[0])
    A = B["A"]
    def sl(p): return lax.rem(p, 4)
    def two(p): return lax.rem(p, 2)
    def first(p, e):
        a = A.at[sl(p), e]
        if e == 0: return remote(a.at[:, 1 - x], O["B1X"].at[p], S["s1"].at[p, 0], S["r1"].at[p, 0], xdev)
        return remote(a.at[:, :, :, other], O["B1Y"].at[p], S["s1"].at[p, 1], S["r1"].at[p, 1], ydev)
    def second(p): return remote(A.at[sl(p), 0, :, x, :, other], O["B2H"].at[p], S["s2"].at[p], S["r2"].at[p], ydev)
    def zsend(p, d): return remote(A.at[sl(p), 0, to_z(d), x, :, mine], O["ZB0"].at[p, d], S["zs"].at[p, d], S["zr"].at[p, d], (to_z(d), c, y))
    def zwide(p, d): return remote(A.at[sl(p), 1, to_z(d), :, :, mine], O["ZB1"].at[p, d], S["ws"].at[p, d], S["wr"].at[p, d], (to_z(d), c, y))
    def xswap(p): return remote(B["hi"].at[sl(p)], O["XBH"].at[p], S["vs"].at[p], S["vr"].at[p], xdev)
    def bcast(p, i): return remote(B["lo"].at[two(p)], O["R"].at[2 * p, x, k], S["bs"].at[p, i], S["br"].at[p, i], (kdev, xdev)[i])
    def wide(p): return remote(B["hi2"].at[two(p)], O["R"].at[2 * p + 1, :, k], S["us"].at[p], S["ur"].at[p], kdev)
    def fwd(p):
        rr = O["R"].at[2 * p, 1 - x, k]
        return remote(rr, rr, S["fs"].at[p], S["fr"].at[p], kdev)
    def extra(e, i):
        src = B["lo"].at[0] if e == 0 else B["hi2"].at[0, x]
        return remote(src, O["RX"].at[e, c], S["xs"].at[e, i], S["xr"].at[e, i], (z, lax.rem(c + i, 4), 1 - y))
    def landed(ref, sem): local(ref, ref, sem).wait()
    def plus(a, b): return a + b
    def own_load(p, do):
        @pl.when(p < 4)
        def _(): do(local(I["Dc"].at[pl.ds(2 * p, 2), :, :, k], A.at[sl(p)], S["lsem"].at[0]))
        @pl.when(p >= 4)
        def _(): do(local(O["DD"].at[pl.ds(jnp.maximum(2 * p - 8, 0), 2), :, :, k], A.at[sl(p)], S["lsem"].at[0]))
    def guard(p, body, least=0):
        if isinstance(p, int):
            if least <= p < 8: body()
        else:
            pl.when((p >= least) & (p < 8))(body)
    def sent(p):
        first(p, 0).wait_send()
        first(p, 1).wait_send()
        second(p).wait_send()
        xswap(p).wait_send()
        for d in range(F - 1):
            zsend(p, d).wait_send()
            zwide(p, d).wait_send()
    def sent_last(p):
        bcast(p, 0).wait_send()
        bcast(p, 1).wait_send()
        wide(p).wait_send()
    def lk(p): return local(O["KBH"].at[pl.ds(2 * p, 2)], B["TK"], S["lsem"].at[1])
    def l1x(p): return local(O["B1X"].at[p], B["T1X"], S["lsem"].at[2])
    def l1y(p): return local(O["B1Y"].at[p], B["T1Y"], S["lsem"].at[3])
    def l2(p): return local(O["B2H"].at[p], B["T2"], S["lsem"].at[4])
    def lz0(p): return local(O["ZB0"].at[p], B["TZ0"], S["lsem"].at[5])
    def lz1(p): return local(O["ZB1"].at[p], B["TZ1"], S["lsem"].at[6])
    def lx(p): return local(O["XBH"].at[p], B["TX"], S["lsem"].at[7])
    def rown0(p): return local(B["lo"].at[two(p)], O["R"].at[2 * p, x, k], S["lsem"].at[8])
    def rown1(p): return local(B["hi2"].at[two(p)], O["R"].at[2 * p + 1, :, k], S["lsem"].at[9])
    def pair_step(s):
        def k_in():
            guard(s - 4, lambda: sent(s - 4))
            landed(O["KBH"].at[pl.ds(2 * s, 2)], S["kr"].at[s])
            own_load(s, lambda cp: cp.start())
            lk(s).start()
        def s1_in():
            p = s - 1
            first(p, 0).wait_recv()
            l1x(p).start()
            first(p, 1).wait_recv()
            l1y(p).start()
        def s2_in():
            p = s - 2
            second(p).wait_recv()
            l2(p).start()
            for d in range(F - 1): zwide(p, d).wait_recv()
            lz1(p).start()
        def z_in():
            p = s - 3
            for d in range(F - 1): zsend(p, d).wait_recv()
            lz0(p).start()
            xswap(p).wait_recv()
            lx(p).start()
        def k_do():
            own_load(s, lambda cp: cp.wait())
            lk(s).wait()
            a, t = A.at[sl(s)], B["TK"]
            for e in range(2):
                def add(i, _):
                    zz, xx = lax.div(i, 2), lax.rem(i, 2)
                    a[e, zz, xx] = plus(a[e, zz, xx], t[e, zz, xx])
                    return 0
                lax.fori_loop(0, 2 * F, add, 0)
                first(s, e).start()
        def s1_do():
            p = s - 1
            a = A.at[sl(p)]
            l1x(p).wait()
            def add0(i, _):
                a[0, i, x] = plus(a[0, i, x], B["T1X"][i])
                return 0
            lax.fori_loop(0, F, add0, 0)
            second(p).start()
            l1y(p).wait()
            def add1(i, _):
                for xx in range(2): a[1, i, xx, :, mine] = plus(a[1, i, xx, :, mine], B["T1Y"][i, xx])
                return 0
            lax.fori_loop(0, F, add1, 0)
            for d in range(F - 1): zwide(p, d).start()
        def s2_do():
            p = s - 2
            a = A.at[sl(p)]
            l2(p).wait()
            def add(i, _):
                a[0, i, x, :, mine] = plus(a[0, i, x, :, mine], B["T2"][i])
                return 0
            lax.fori_loop(0, F, add, 0)
            for d in range(F - 1): zsend(p, d).start()
            lz1(p).wait()
            for xx in range(2):
                total = a[1, z, xx, :, mine].astype(F32)
                for d in range(F - 1): total = total + B["TZ1"][d, xx].astype(F32)
                B["hi"][sl(p), xx] = total.astype(BF16)
            xswap(p).start()
        def z_do():
            p = s - 3
            guard(p - 2, lambda: sent_last(p - 2))
            lz0(p).wait()
            total = A[sl(p), 0, z, x, :, mine].astype(F32)
            for d in range(F - 1): total = total + B["TZ0"][d].astype(F32)
            B["lo"][two(p)] = total.astype(BF16)
            for i in range(2): bcast(p, i).start()
            rown0(p).start()
            lx(p).wait()
            for xx in range(2): B["hi2"][two(p), xx] = plus(B["hi"][sl(p), xx], B["TX"][xx])
            wide(p).start()
            rown1(p).start()
            rown0(p).wait()
            rown1(p).wait()
            def special():
                for e in range(2):
                    for i in range(4): extra(e, i).start()
                for e in range(2):
                    for i in range(4): extra(e, i).wait_send()
            if isinstance(p, int):
                if p == 6: special()
            else: pl.when(p == 6)(special)
        def f_do():
            p = s - 4
            landed(O["R"].at[2 * p, 1 - x, k], S["br"].at[p, 1])
            fwd(p).start()
        guard(s, k_in)
        guard(s, k_do)
        guard(s - 1, s1_in)
        guard(s - 1, s1_do)
        guard(s - 2, s2_in)
        guard(s - 2, s2_do)
        guard(s - 3, z_in)
        guard(s - 3, z_do)
        guard(s - 4, f_do)
    ggv = B["ggv"]
    ggv[...] = jnp.zeros_like(ggv)
    loads["gy1"].wait()
    do, datt, dqb, dkv, dskv, dntok, dsin, dsout = (B[i] for i in ("do", "datt", "dqb", "dkv", "dskv", "dntok", "dsin", "dsout"))
    def cast(rs): do[rs, :] = B["gy1"][rs, :].astype(BF16)
    rows_loop(rows, 64, cast)
    wload[7].wait()
    datt[...] = nn(do[...], W(7)).astype(BF16)
    wload[2].start()
    oload.wait()
    oswap.start(); oown.start()
    for name in order[1:7]: loads[name].wait()
    hz = F // 2
    def pair_view(ref):
        return lambda i, cs: ref[i * hz:(i + 1) * hz, :, :, :, cs].reshape(rows, HEAD)
    kvp_at, skv_at = pair_view(B["kvp"]), pair_view(B["skv"])
    def parts_of(cs, qc):
        upto = (qc + 1) * (rows // 2)
        return [(lambda: kvp_at(0, cs), lambda: kvp_at(1, cs), lambda s: jnp.where(r == 0, NEG, s)),
                (lambda: B["kv"][0, pl.ds(0, upto), cs], lambda: B["kv"][1, pl.ds(0, upto), cs], lambda s: causal_scores(s, 0, qc * (rows // 2))),
                (lambda: skv_at(0, cs), lambda: skv_at(1, cs), lambda s: s)]
    def sink(i, cs, dk, dv):
        dst = (B["dsend"], dkv, dskv)[i]
        dst[0, :, cs] = dk.astype(dst.dtype)
        dst[1, :, cs] = dv.astype(dst.dtype)
    def halves(i, _):
        pair_step(i)
        attend_heads_back(parts_of, B["q"], datt, B["lse"], dqb, sink, rows, 2, 1, i * (HEADS // 2), HEADS // 2)
        return 0
    lax.fori_loop(0, 2, halves, 0)
    pcopy = remote(B["dsend"], B["dret"], S["psem"].at[0], S["prem"].at[0], dev(r - 1))
    @pl.when(r > 0)
    def _(): pcopy.start()
    wload[5].wait(); wload[6].wait()
    dntok[...] = nt(dskv[0], W(5)) + nt(dskv[1], W(6))
    wload[4].start(); wload[0].start()
    for name in order[7:11]: loads[name].wait()
    oswap.wait_send(); oown.wait()
    hr = rows // 2
    ccopy = [remote(dsout.at[pl.ds(i * hr, hr)], dsin.at[pl.ds(i * hr, hr)], S["csem"].at[i], S["crem"].at[i], dev(r - 1)) for i in range(2)]
    def finish_state(more):
        for i in range(2):
            def body(j, _):
                rs = pl.ds(pl.multiple_of(i * hr + j * 32, 32), 32)
                dv, dgain = norm_back_rows(B["s"][rs, :].astype(F32), B["gs"][...], dntok[rs, :])
                if more: dv = dv + B["keep"][...] * dsin[rs, :].astype(F32)
                dsout[rs, :] = dv.astype(BF16)
                ggv[pl.ds(8, 8), :] += fold8(dgain)
                return 0
            lax.fori_loop(0, hr // 32, body, 0)
            @pl.when(r > 0)
            def _(): ccopy[i].start()
    @pl.when(r == nctx - 1)
    def _(): finish_state(False)
    stages = (B["kvp"], B["skv"])
    def grad_out(i, left, right):
        if i >= 2: pass
        st = stages[i % 2]
        st[...] = tn(left[...], right[...]).astype(BF16).reshape(st.shape)
        local(st, O["DD"].at[i], S["dsem"].at[i]).start()
        if i % 2 == 1:
            for q in (i - 1, i): local(stages[q % 2], O["DD"].at[q], S["dsem"].at[q]).wait()
            ksend_from(O["DD"], 4 + i // 2, i - 1).start()
    grad_out(0, do, B["att"])
    xload = local(I["x"], B["att"], S["rsem"].at[2])
    xload.start()
    grad_out(1, B["n"], dskv.at[0])
    pair_step(2)
    grad_out(2, B["n"], dskv.at[1])
    grad_out(3, B["h"], dqb)
    for name in order[11:]: loads[name].wait()
    wload[3].wait(); wload[2].wait()
    dzb = datt
    def turn(t, _):
        @pl.when(r == nctx - 2 - t)
        def _():
            for cp in ccopy: cp.wait_recv()
            def body(rs):
                d = dsin[rs, :].astype(F32)
                kr = B["keep"][...]
                dzb[rs, :] = ((1.0 - kr) * d).astype(BF16)
                ggv[pl.ds(16, 8), :] += fold8(d * (B["s"][rs, :].astype(F32) - B["z"][rs, :].astype(F32)) * kr * (1.0 - kr))
            rows_loop(rows, 32, body)
            do[...] = nn(dzb[...], W(3)).astype(BF16)
            def sink2(i, cs, dk, dv):
                dkv[0, :, cs] += dk
                dkv[1, :, cs] += dv
            attend_heads_back(state_parts(B["kv"]), B["sq"], do, B["lses"], B["q"], sink2, rows, 1, 4, 0, HEADS)
            dntok[...] += nt(B["q"][...], W(2))
            finish_state(True)
        @pl.when(t < nctx - 2)
        def _(): pair_step(3 + t)
        return 0
    lax.fori_loop(0, nctx - 1, turn, 0)
    n2 = 2 * F
    prow = rows // n2
    me = z * 2 + y
    def zy(i):
        q = lax.rem(me + i + 1, n2)
        return q, (lax.div(q, 2), 0, lax.rem(q, 2))
    def back_of(i): return lax.rem(me - (i + 1) + n2, n2)
    def d1(i):
        q, d = zy(i)
        return remote(dsout.at[pl.ds(pl.multiple_of(q * prow, prow), prow)], B["DS1"].at[me], S["dss"].at[i], S["dsr"].at[i], d)
    def d2(i):
        q, d = zy(i)
        return remote(B["dsp"], O["S0"].at[me], S["d2s"].at[i], S["d2r"].at[i], d)
    def d3(i, d): return remote(O["S0"], O["S0"], S["d3s"].at[i], S["d3r"].at[0], d)
    dsown = local(B["dsp"], O["S0"].at[me], S["rsem"].at[3])
    @pl.when(r == 0)
    def _():
        for i in range(n2 - 1): d1(i).start()
    @pl.when(r == nctx - 1)
    def _():
        B["q"][...] = jnp.zeros_like(B["q"])
        dzb[...] = jnp.zeros_like(dzb)
        B["zatt"][...] = jnp.zeros_like(B["zatt"])
    grad_out(4, B["n"], B["q"])
    grad_out(5, dzb, B["zatt"])
    @pl.when(r < nctx - 1)
    def _(): pcopy.wait_recv()
    @pl.when(r == nctx - 1)
    def _(): B["dret"][...] = jnp.zeros_like(B["dret"])
    wload[1].start()
    for i in range(2):
        def add(rs): dskv[i, rs, :] = (dkv[i, rs, :] + B["dret"][i, rs, :].astype(F32)).astype(BF16)
        rows_loop(rows, 32, add)
    grad_out(6, B["h"], dskv.at[0])
    grad_out(7, B["h"], dskv.at[1])
    pair_step(5)
    wload[4].wait(); wload[0].wait(); wload[1].wait()
    xload.wait()
    dntok[...] = nt(dqb[...], W(4)) + nt(dskv[0], W(0)) + nt(dskv[1], W(1))
    gxb = B["att"]
    def last(rs):
        dv, dgain = norm_back_rows(gxb[rs, :].astype(F32), B["gains"][pl.ds(0, 1), :], dntok[rs, :])
        ggv[pl.ds(0, 8), :] += fold8(dgain)
        gxb[rs, :] = (B["gy1"][rs, :] + dv).astype(BF16)
    rows_loop(rows, 32, last)
    gswap = remote(gxb.at[:, other], O["GXF"].at[y], S["osem"].at[1], S["orem"].at[1], ydev)
    gown = local(gxb.at[:, mine], O["GXF"].at[y], S["rsem"].at[1])
    gswap.start(); gown.start()
    gin = B["gin"]
    gin[...] = jnp.zeros_like(gin)
    for i in range(3): gin[pl.ds(i, 1), :] = jnp.sum(ggv[pl.ds(8 * i, 8), :], axis=0, keepdims=True)
    gin[pl.ds(3, 1), :] = jnp.sum(B["gg"][...], axis=0, keepdims=True)
    around = ((0, 0, 1), (0, 1, 0), (0, 1, 1), (1, 0, 0), (1, 0, 1), (1, 1, 0), (1, 1, 1))
    def plane(i):
        dx, dk, dy = around[i]
        return lax.rem(x + dx, 2), lax.rem(k + dk, 2), lax.rem(y + dy, 2)
    spot = c * 2 + y
    def g1copy(i):
        px, pk, py = plane(i)
        return remote(gin, B["g1"].at[spot], S["g1s"].at[i], S["g1r"].at[i], (z, px * 2 + pk, py))
    def g2copy(d): return remote(gin, B["g2"].at[z], S["g2s"].at[d], S["g2r"].at[d], (to_z(d), c, y))
    B["g1"][spot] = gin[...]
    for i in range(7): g1copy(i).start()
    def tail(i, _):
        s = 6 + i
        @pl.when(i == 1)
        def _():
            for j in range(7):
                g1copy(j).wait_send()
                px, pk, py = plane(j)
                landed(B["g1"].at[(px * 2 + pk) * 2 + py], S["g1r"].at[j])
            total = B["g1"][0]
            for j in range(1, 8): total = total + B["g1"][j]
            gin[...] = total
            B["g2"][z] = total
            for d in range(F - 1): g2copy(d).start()
        @pl.when((i == 1) & (r == 0))
        def _():
            B["DS1"][me] = dsout[pl.ds(pl.multiple_of(me * prow, prow), prow), :]
            for j in range(n2 - 1): landed(B["DS1"].at[back_of(j)], S["dsr"].at[j])
            total = B["DS1"][0].astype(F32)
            for j in range(1, n2): total = total + B["DS1"][j].astype(F32)
            B["dsp"][...] = total.astype(BF16)
            dsown.start()
            for j in range(n2 - 1): d2(j).start()
        @pl.when((i == 2) & (r == 0))
        def _():
            for j in range(n2 - 1): landed(O["S0"].at[back_of(j)], S["d2r"].at[j])
            dsown.wait()
            d3(0, dev(1)).start()
            d3(1, dev(2)).start()
        @pl.when((i == 3) & (r == 2))
        def _():
            landed(O["S0"], S["d3r"].at[0])
            d3(0, dev(3)).start()
        @pl.when(i == 3)
        def _():
            for d in range(F - 1):
                g2copy(d).wait_send()
                landed(B["g2"].at[from_z(d)], S["g2r"].at[d])
            total = B["g2"][0]
            for d in range(1, F): total = total + B["g2"][d]
            gin[...] = total
            local(gin, O["SUMS"], S["rsem"].at[4]).start()
        pair_step(s)
        return 0
    lax.fori_loop(0, 6, tail, 0)
    local(gin, O["SUMS"], S["rsem"].at[4]).wait()
    for p in range(4, 8): sent(p)
    for p in (6, 7): sent_last(p)
    def ends(p, _):
        ksend_from(O["DD"], p, 0).wait_send()
        fwd(p).wait_send()
        landed(O["R"].at[2 * p, x, 1 - k], S["br"].at[p, 0])
        landed(O["R"].at[2 * p, 1 - x, 1 - k], S["fr"].at[p])
        landed(O["R"].at[2 * p + 1, :, 1 - k], S["ur"].at[p])
        return 0
    lax.fori_loop(0, 8, ends, 0)
    for e in range(2):
        for i in range(4): landed(O["RX"].at[e, lax.rem(c - i + 4, 4)], S["xr"].at[e, i])
    @pl.when(r == 0)
    def _():
        for j in range(n2 - 1):
            d1(j).wait_send()
            d2(j).wait_send()
        d3(0, dev(1)).wait_send()
        d3(1, dev(2)).wait_send()
    @pl.when(r == 2)
    def _(): d3(0, dev(3)).wait_send()
    @pl.when((r == 1) | (r == 3))
    def _(): landed(O["S0"], S["d3r"].at[0])
    @pl.when(r > 0)
    def _():
        pcopy.wait_send()
        for cp in ccopy: cp.wait_send()
    oswap.wait_recv(); gswap.wait(); gown.wait()

def back_call(F, nctx, vals, gs, keep):
    rows = vals["h"].shape[0]
    blk = D // (4 * F)
    half = D // 2
    sh = lambda *s: jax.ShapeDtypeStruct(s, BF16)
    fl = lambda *s: jax.ShapeDtypeStruct(s, F32)
    mats = lambda n: sh(n, F, 2, 2, blk, D)
    R, R2, L = sh(rows, D), sh(2, rows, D), fl(HEADS, 1, rows)
    prow = rows // (2 * F)
    shapes = dict(R=sh(16, 2, 2, blk, half), RX=sh(2, 4, blk, half), OUTF=sh(2, rows, half), GXF=sh(2, rows, half), S0=sh(2 * F, prow, D), SUMS=fl(8, D),
        DD=mats(8), KBH=sh(16, F, 2, blk, D), B1X=sh(8, F, blk, D), B1Y=sh(8, F, 2, blk, half), B2H=sh(8, F, blk, half),
        ZB0=sh(8, F - 1, blk, half), ZB1=sh(8, F - 1, 2, blk, half), XBH=sh(8, 2, blk, half))
    one = sh(F, 2, 2, blk, D)
    bufs = dict(h=R, q=R, kv=R2, kvp=one, skv=one, n=R, s=R, sq=R, zatt=R, z=R, lse=L, lses=L, att=R, gy1=fl(rows, D), gg=fl(8, D), gains=fl(8, D), gs=fl(1, D), keep=fl(1, D),
        WB=mats(4), do=R, datt=R, dqb=R, dkv=fl(2, rows, D), dsend=R2, dret=R2, dskv=R2, dntok=fl(rows, D), dsin=R, dsout=R, ggv=fl(24, D),
        A=sh(4, 2, F, 2, blk, D), TK=sh(2, F, 2, blk, D), T1X=sh(F, blk, D), T1Y=sh(F, 2, blk, half), T2=sh(F, blk, half), TZ0=sh(F - 1, blk, half), TZ1=sh(F - 1, 2, blk, half), TX=sh(2, blk, half),
        lo=sh(2, blk, half), hi=sh(4, 2, blk, half), hi2=sh(2, 2, blk, half), DS1=sh(2 * F, prow, D), dsp=sh(prow, D), gin=fl(8, D), g1=fl(8, 8, D), g2=fl(F, 8, D))
    X = pltpu.SemaphoreType.DMA
    sems = dict(isem=(18,), wsem=(8,), dsem=(8,), psem=(1,), prem=(1,), csem=(2,), crem=(2,), osem=(2,), orem=(2,),
        ks=(8,), kr=(8,), s1=(8, 2), r1=(8, 2), s2=(8,), r2=(8,), zs=(8, F - 1), zr=(8, F - 1), ws=(8, F - 1), wr=(8, F - 1), vs=(8,), vr=(8,), us=(8,), ur=(8,), bs=(8, 2), br=(8, 2), fs=(8,), fr=(8,), xs=(2, 4), xr=(2, 4), lsem=(10,),
        dss=(2 * F,), dsr=(2 * F,), d2s=(2 * F,), d2r=(2 * F,), d3s=(2,), d3r=(1,), g1s=(7,), g1r=(7,), g2s=(F - 1,), g2r=(F - 1,), rsem=(5,))
    args = dict(vals)
    args["gs"], args["keep"] = gs, keep
    args["kvp"], args["skv"] = (args[i].reshape(one.shape) for i in ("kvp", "skv"))
    outs = pl.pallas_call(functools.partial(back_kernel, F, nctx),
        out_shape=[shapes[i] for i in B_OUT], in_specs=[ANY] * len(B_IN), out_specs=[ANY] * len(B_OUT),
        scratch_shapes=[pltpu.VMEM(bufs[i].shape, bufs[i].dtype) for i in B_BUF] + [X(sems[i]) for i in B_SEM],
        compiler_params=pltpu.CompilerParams(collective_id=2, has_side_effects=True, vmem_limit_bytes=63 << 20), name="backward")(*[args[i] for i in B_IN])
    return dict(zip(B_OUT, outs))


def local(
    tokens,
    cotangent,
    w_query,
    w_key,
    w_value,
    w_out,
    w_state_key,
    w_state_value,
    w_state_query,
    w_state_out,
    w_up,
    w_down,
    gain_attn,
    gain_state,
    gain_mlp,
    forget_logit,
    state_init,
):
    fsdp = lax.axis_size("fsdp")
    tp_rank = lax.axis_index("tp")
    ctx_count = lax.axis_size("ctx")
    half = D // 2
    rows = D // fsdp
    blk = rows // 4
    tiles = lambda w: w.reshape(2, 2, blk, w.shape[1])
    args = dict(
        tokens=tokens, cotangent=cotangent, gtp=jnp.pad(jnp.stack([gain_attn, gain_mlp]), ((0, 6), (0, 0))),
        gstate=gain_state[None], keep=jax.nn.sigmoid(forget_logit)[None], s0=state_init,
        key=tiles(w_key), value=tiles(w_value), squery=tiles(w_state_query), sout=w_state_out, query=tiles(w_query),
        skey=tiles(w_state_key), svalue=tiles(w_state_value), out=w_out, up=tiles(w_up), down=w_down)
    vals = forward_call(fsdp, ctx_count, args)
    got = back_call(fsdp, ctx_count, vals, args["gstate"], args["keep"])
    full = got["R"].reshape(16, rows, half).astype(F32)
    r = {w: full[8 + i] for i, w in enumerate((7, 5, 6, 4, 2, 3, 0, 1))}
    rx = got["RX"].reshape(2, rows, half).astype(F32)
    small = got["SUMS"]

    def both(mine, other):
        first = jnp.where(tp_rank == 0, mine, other)
        second = jnp.where(tp_rank == 0, other, mine)
        return jnp.concatenate([first, second], axis=1)

    at = lambda i: lax.dynamic_slice_in_dim(small[i], tp_rank * half, half, 0)
    return (
        got["OUTF"],
        got["GXF"],
        r[4],
        r[0],
        r[1],
        r[7].T,
        r[5],
        r[6],
        both(r[2], rx[0]),
        both(r[3], rx[1]).T,
        full[0:8:2].swapaxes(0, 1).reshape(rows, -1),
        full[1:8:2].swapaxes(1, 2).reshape(-1, rows),
        at(0),
        small[1],
        at(3),
        small[2],
        got["S0"].reshape(state_init.shape).astype(F32),
    )


def solution(mesh):
    placed = (
        P("fsdp", "ctx", "tp"),
        P("fsdp", "ctx", "tp"),
        P("fsdp", "tp"),
        P("fsdp", "tp"),
        P("fsdp", "tp"),
        P("tp", "fsdp"),
        P("fsdp", "tp"),
        P("fsdp", "tp"),
        P("fsdp", None),
        P(None, "fsdp"),
        P("fsdp", "tp"),
        P("tp", "fsdp"),
        P("tp"),
        P(),
        P("tp"),
        P(),
        P(),
    )
    return jax.shard_map(
        local,
        mesh=mesh,
        in_specs=placed,
        out_specs=(
            P("fsdp", "ctx", "tp"),
            P("fsdp", "ctx", "tp"),
            P("fsdp", "tp"),
            P("fsdp", "tp"),
            P("fsdp", "tp"),
            P("tp", "fsdp"),
            P("fsdp", "tp"),
            P("fsdp", "tp"),
            P("fsdp", None),
            P(None, "fsdp"),
            P("fsdp", "tp"),
            P("tp", "fsdp"),
            P("tp"),
            P(),
            P("tp"),
            P(),
            P(),
        ),
        check_vma=False,
    )
```

```python
import functools

import jax
import jax.numpy as jnp
from jax import lax
from jax.experimental import pallas as pl
from jax.experimental.pallas import tpu as pltpu
from jax.sharding import PartitionSpec as P

MESH = pl.DeviceIdType.MESH
ANY = pl.BlockSpec(memory_space=pl.ANY)
D = 1024
HEADS = 8
HEAD = 128
EPS = 1e-06
NEG = -1e30
LOG2E = 1.4426950408889634
F32 = jnp.float32
BF16 = jnp.bfloat16
SCALE = HEAD ** -0.5
CE = SCALE * LOG2E

def nn(a, b): return lax.dot_general(a, b, (((1,), (0,)), ((), ())), preferred_element_type=F32)
def nt(a, b): return lax.dot_general(a, b, (((1,), (1,)), ((), ())), preferred_element_type=F32)
def tn(a, b): return lax.dot_general(a, b, (((0,), (0,)), ((), ())), preferred_element_type=F32)

def rows_loop(total, step, body):
    def run(i, _):
        body(pl.ds(pl.multiple_of(i * step, step), step))
        return 0
    lax.fori_loop(0, total // step, run, 0)

def inverse_of(v):
    return lax.rsqrt(jnp.mean(v * v, axis=-1, keepdims=True) + EPS)

def norm_into(dst, src, gain):
    def body(rs):
        v = src[rs, :].astype(F32)
        dst[rs, :] = (v * inverse_of(v) * gain[...]).astype(dst.dtype)
    rows_loop(src.shape[0], 32, body)

def head_cols(h): return pl.ds(pl.multiple_of(h * HEAD, HEAD), HEAD)

def causal_scores(s, first_key, first_query):
    keys = lax.broadcasted_iota(jnp.int32, s.shape, 0) + first_key
    qs = lax.broadcasted_iota(jnp.int32, s.shape, 1) + first_query
    return jnp.where(keys <= qs, s, NEG)

def over_heads(one, unroll, h0, count):
    def body(i, _):
        for u in range(unroll):
            one(h0 + i * unroll + u)
        return 0
    lax.fori_loop(0, count // unroll, body, 0)

def attend_heads(parts_of, q, out, lse, rows, chunks, unroll, h0=0, count=HEADS):
    step = rows // chunks
    def one(h):
        cs = head_cols(h)
        for qc in range(chunks):
            rs = pl.ds(qc * step, step)
            qh = q[rs, cs]
            parts = parts_of(cs, qc)
            scores = [mask(nt(keys(), qh)) for keys, values, mask in parts]
            big = functools.reduce(jnp.maximum, [jnp.max(s, axis=0, keepdims=True) for s in scores])
            es = [jnp.exp2((s - big) * CE) for s in scores]
            total = functools.reduce(jnp.add, [jnp.sum(e, axis=0, keepdims=True) for e in es])
            inv = 1.0 / total
            acc = functools.reduce(jnp.add, [tn((e * inv).astype(BF16), p[1]()) for e, p in zip(es, parts)])
            out[rs, cs] = acc.astype(BF16)
            lse[h, :, pl.ds(qc * step, step)] = big * CE + jnp.log2(total)
    over_heads(one, unroll, h0, count)

def token_parts(kvp, kv, skv, first, rows, chunks):
    def parts_of(cs, qc):
        step = rows // chunks
        upto = (qc + 1) * step
        same = lambda s: s
        earlier = lambda s: jnp.where(first, NEG, s)
        causal = lambda s: causal_scores(s, 0, qc * step)
        return [(lambda: kvp[0, :, cs], lambda: kvp[1, :, cs], earlier),
                (lambda: kv[0, pl.ds(0, upto), cs], lambda: kv[1, pl.ds(0, upto), cs], causal),
                (lambda: skv[0, :, cs], lambda: skv[1, :, cs], same)]
    return parts_of

def state_parts(kv):
    def parts_of(cs, qc):
        return [(lambda: kv[0, :, cs], lambda: kv[1, :, cs], lambda s: s)]
    return parts_of

def chain_barrier(r, n, dev):
    bar = pltpu.get_barrier_semaphore()
    @pl.when(r > 0)
    def _(): pl.semaphore_signal(bar, inc=1, device_id=dev(r - 1), device_id_type=MESH)
    @pl.when(r < n - 1)
    def _(): pl.semaphore_signal(bar, inc=1, device_id=dev(r + 1), device_id_type=MESH)
    pl.semaphore_wait(bar, jnp.where(r > 0, 1, 0) + jnp.where(r < n - 1, 1, 0))

def where_am_i():
    f = lax.axis_index("fsdp")
    c = lax.axis_index("ctx")
    return f, lax.div(c, 2), lax.rem(c, 2), lax.axis_index("tp")

def cols_of(t):
    return pl.ds(pl.multiple_of(t * (D // 2), D // 2), D // 2)

G1 = 0.7978845608028654
G3 = 0.044715

def norm_back_rows(v, gain, e):
    inv = inverse_of(v)
    w = e * gain
    proj = jnp.sum(w * v, axis=-1, keepdims=True) * (1.0 / D)
    return inv * w - v * (inv * inv * inv) * proj, e * v * inv

def fold8(v):
    return functools.reduce(jnp.add, [v[i * 8:(i + 1) * 8] for i in range(v.shape[0] // 8)])

def attend_heads_back(parts_of, q, datt, lse, dq, sink, rows, chunks, unroll, h0, count):
    step = rows // chunks
    def one(h):
        cs = head_cols(h)
        sums = None
        for qc in range(chunks):
            rs = pl.ds(qc * step, step)
            qh = q[rs, cs]
            gh = datt[rs, cs]
            ls = lse[h, :, pl.ds(qc * step, step)]
            parts = parts_of(cs, qc)
            ps = [jnp.exp2(p[2](nt(p[0](), qh)) * CE - ls) for p in parts]
            dps = [nt(p[1](), gh) for p in parts]
            delta = functools.reduce(jnp.add, [jnp.sum(a * b, axis=0, keepdims=True) for a, b in zip(ps, dps)])
            dss = [(a * (b - delta)).astype(BF16) for a, b in zip(ps, dps)]
            dq[rs, cs] = (functools.reduce(jnp.add, [tn(d, p[0]()) for d, p in zip(dss, parts)]) * SCALE).astype(dq.dtype)
            new = [(nn(d, qh), nn(a.astype(BF16), gh)) for a, d in zip(ps, dss)]
            if sums is None: sums = new
            else:
                merged = []
                for (k0, v0), (k1, v1) in zip(sums, new):
                    n0 = k0.shape[0]
                    if n0 < k1.shape[0]:
                        k1 = jnp.concatenate([k0 + k1[:n0], k1[n0:]], axis=0)
                        v1 = jnp.concatenate([v0 + v1[:n0], v1[n0:]], axis=0)
                    else:
                        k1, v1 = k0 + k1, v0 + v1
                    merged.append((k1, v1))
                sums = merged
        for i, (dk, dv) in enumerate(sums): sink(i, cs, dk * SCALE, dv)
    over_heads(one, unroll, h0, count)


class Gather:
    def __init__(self, G, own, F, sems):
        self.G, self.own, self.F, self.sems = G, own, F, sems
        self.z, self.x, self.k, self.y = where_am_i()

    def src_z(self, d):
        return lax.rem(self.z + d + 1, self.F)

    def region(self, g, z, x, k, cols=None):
        w = pl.ds(2 * g, 2)
        if cols is None:
            return self.G.at[w, z, x, k]
        return self.G.at[w, z, x, k, :, cols]

    def both_x(self, g, z, k, cols=None):
        w = pl.ds(2 * g, 2)
        if cols is None:
            return self.G.at[w, z, :, k]
        return self.G.at[w, z, :, k, :, cols]

    def remote(self, ref, i, g, d, dev, src=None):
        return pltpu.make_async_remote_copy(
            src_ref=ref if src is None else src, dst_ref=ref, send_sem=self.sems[i].at[g, d], recv_sem=self.sems[i + 1].at[g, d],
            device_id=dev, device_id_type=MESH)

    def landed(self, ref, i, g, d):
        pltpu.make_async_copy(ref, ref, self.sems[i + 1].at[g, d]).wait()

    def zcopy(self, g, d):
        to = lax.rem(self.z - (d + 1) + self.F, self.F)
        return self.remote(self.region(g, self.z, self.x, self.k, cols_of(self.y)), 0, g, d, (to, self.x * 2 + self.k, self.y), self.own.at[pl.ds(2 * g, 2), self.x, self.k])

    def ycopy(self, g, d):
        dev = (self.z, self.x * 2 + self.k, 1 - self.y)
        if d == self.F - 1:
            return self.remote(self.both_x(g, self.z, self.k, cols_of(self.y)), 2, g, d, dev, self.own.at[pl.ds(2 * g, 2), :, self.k])
        return self.remote(self.region(g, self.src_z(d), self.x, self.k, cols_of(self.y)), 2, g, d, dev)

    def xcopy(self, g, d):
        return self.remote(self.region(g, self.src_z(d), self.x, self.k), 4, g, d, (self.z, (1 - self.x) * 2 + self.k, self.y))

    def kcopy(self, g, d):
        dev = (self.z, self.x * 2 + 1 - self.k, self.y)
        if d == self.F - 1:
            return self.remote(self.both_x(g, self.z, self.k, cols_of(1 - self.y)), 6, g, d, dev)
        return self.remote(self.both_x(g, self.src_z(d), self.k), 6, g, d, dev)

    def send_z(self, g):
        for d in range(self.F - 1):
            self.zcopy(g, d).start()
        self.ycopy(g, self.F - 1).start()

    def stage_y(self, g):
        for d in range(self.F - 1):
            self.landed(self.region(g, self.src_z(d), self.x, self.k, cols_of(self.y)), 0, g, d)
            self.ycopy(g, d).start()

    def stage_x(self, g):
        o = cols_of(1 - self.y)
        for d in range(self.F - 1):
            self.landed(self.region(g, self.src_z(d), self.x, self.k, o), 2, g, d)
            self.xcopy(g, d).start()
        self.landed(self.both_x(g, self.z, self.k, o), 2, g, self.F - 1)
        self.kcopy(g, self.F - 1).start()

    def stage_k(self, g):
        for d in range(self.F - 1):
            self.landed(self.region(g, self.src_z(d), 1 - self.x, self.k), 4, g, d)
            self.kcopy(g, d).start()

    def done(self, g):
        for d in range(self.F - 1):
            self.landed(self.both_x(g, self.src_z(d), 1 - self.k), 6, g, d)
        self.landed(self.both_x(g, self.z, 1 - self.k, cols_of(1 - self.y)), 6, g, self.F - 1)

    def zwide(self, g, d):
        to = lax.rem(self.z - (d + 1) + self.F, self.F)
        return self.remote(self.both_x(g, self.z, self.k, cols_of(self.y)), 0, g, d, (to, self.x * 2 + self.k, self.y), self.own.at[pl.ds(2 * g, 2), :, self.k])

    def ywide(self, g, d):
        return self.remote(self.both_x(g, self.src_z(d), self.k, cols_of(self.y)), 2, g, d, (self.z, self.x * 2 + self.k, 1 - self.y))

    def send_z_wide(self, g):
        for d in range(self.F - 1):
            self.zwide(g, d).start()
        self.ycopy(g, self.F - 1).start()

    def stage_y_wide(self, g):
        for d in range(self.F - 1):
            self.landed(self.both_x(g, self.src_z(d), self.k, cols_of(self.y)), 0, g, d)
            self.ywide(g, d).start()

    def stage_x_wide(self, g):
        for d in range(self.F - 1):
            self.landed(self.both_x(g, self.src_z(d), self.k, cols_of(1 - self.y)), 2, g, d)
            self.kcopy(g, d).start()
        self.landed(self.both_x(g, self.z, self.k, cols_of(1 - self.y)), 2, g, self.F - 1)
        self.kcopy(g, self.F - 1).start()

    def drain_wide(self, g):
        for d in range(self.F):
            if d < self.F - 1:
                self.zwide(g, d).wait_send()
                self.ywide(g, d).wait_send()
            self.kcopy(g, d).wait_send()
        self.ycopy(g, self.F - 1).wait_send()

    def drain(self, g):
        for d in range(self.F):
            if d < self.F - 1:
                self.zcopy(g, d).wait_send()
                self.xcopy(g, d).wait_send()
            self.ycopy(g, d).wait_send()
            self.kcopy(g, d).wait_send()

def barrier_with(F, count, across=False):
    z, x, k, y = where_am_i()
    bar = pltpu.get_barrier_semaphore()
    peers = [(lax.rem(z + d + 1, F), x * 2 + k, y) for d in range(F - 1)]
    for dx, dk, dy in ((0, 0, 1), (1, 0, 0), (0, 1, 0), (1, 1, 0), (1, 0, 1), (0, 1, 1), (1, 1, 1))[:count]:
        peers.append((z, lax.rem(x + dx, 2) * 2 + lax.rem(k + dk, 2), lax.rem(y + dy, 2)))
    if across:
        peers += [(lax.rem(z + d + 1, F), x * 2 + k, 1 - y) for d in range(F - 1)]
    for p in peers:
        pl.semaphore_signal(bar, inc=1, device_id=p, device_id_type=MESH)
    pl.semaphore_wait(bar, len(peers))

A_IN = ("tokens", "cotangent", "gattn", "gmlp", "gstate", "keep", "s0", "key", "value", "squery", "sout", "query", "skey", "svalue", "out", "up", "down")
A_OUT = ("G", "Dc", "out", "gg", "h", "q", "kv", "kvp", "skv", "n", "s", "sq", "zatt", "z", "lse", "lses", "att", "x", "gy1", "gains", "keep")
A_BUF = ("x", "g", "h", "q", "kv", "kvp", "skv", "n", "s", "ssend", "sq", "zatt", "z", "att", "m", "u", "da", "y1", "a", "du", "oacc", "macc", "lse", "lses", "gains", "gs", "gg", "keep", "tin", "own", "WB")

def forward_kernel(F, nctx, *refs):
    I = dict(zip(A_IN, refs)); at = len(A_IN)
    O = dict(zip(A_OUT, refs[at:])); at += len(A_OUT)
    B = dict(zip(A_BUF, refs[at:])); at += len(A_BUF)
    gsems = refs[at:at + 8]
    osems, ins, osem, wsem, ksem, krem, ssem, srem, ysem, yrem, dsem = refs[at + 8:]
    z_, x_, k_, y_ = where_am_i()
    r = x_ * 2 + k_
    rows = B["x"].shape[0]
    half = D // 2
    dev = lambda c: (z_, c, y_)
    gat = Gather(O["G"], B["own"], F, gsems)
    G = O["G"]
    mine = cols_of(y_)
    WB = B["WB"]
    W = lambda i: WB[i].reshape(D, D)
    own = B["own"]
    def take(w, ref): return pltpu.make_async_copy(ref, own.at[w], osems.at[w])
    def place(w): return pltpu.make_async_copy(own.at[w], G.at[w, z_, :, :, :, mine], osems.at[w])
    takes = {0: take(0, I["key"]), 1: take(1, I["value"]), 2: take(2, I["squery"].at[:, :, :, mine]), 4: take(4, I["query"]),
             5: take(5, I["skey"]), 6: take(6, I["svalue"])}
    for j in range(4):
        takes[8 + 2 * j] = take(8 + 2 * j, I["up"].at[:, :, :, pl.ds(j * half, half)])
    tsrc = [(3, I["sout"].at[mine]), (7, I["out"])] + [(9 + 2 * j, I["down"].at[pl.ds(j * half, half)]) for j in range(4)]
    tcopies = {w: pltpu.make_async_copy(ref, B["tin"].at[i], ins.at[i]) for i, (w, ref) in enumerate(tsrc)}
    def ready(w):
        if w in tcopies:
            tcopies[w].wait()
            own[w] = B["tin"][[v for v, _ in tsrc].index(w)].T.reshape(own.shape[1:])
        else:
            takes[w].wait()
        place(w).start()
    for w in (0, 1, 2): takes[w].start()
    tcopies[3].start()
    loc = [pltpu.make_async_copy(I["tokens"].at[y_], B["x"].at[:, mine], ins.at[6]),
           pltpu.make_async_copy(I["gattn"], B["gains"].at[0, :, mine], ins.at[7]),
           pltpu.make_async_copy(I["keep"], B["keep"], ins.at[8]),
           pltpu.make_async_copy(I["gstate"], B["gs"], ins.at[9]),
           pltpu.make_async_copy(I["gmlp"], B["gains"].at[1, :, mine], ins.at[12]),
           pltpu.make_async_copy(I["cotangent"].at[y_], B["g"].at[:, mine], ins.at[10])]
    s0copy = pltpu.make_async_copy(I["s0"], B["s"], ins.at[11])
    for c in loc: c.start()
    for w in (4, 5, 6): takes[w].start()
    tcopies[7].start()
    for j in range(4):
        takes[8 + 2 * j].start()
        tcopies[9 + 2 * j].start()
    barrier_with(F, 4)
    pdev = (z_, r, 1 - y_)
    swap = lambda i, s, d: pltpu.make_async_remote_copy(src_ref=s, dst_ref=d, send_sem=ysem.at[i], recv_sem=yrem.at[i], device_id=pdev, device_id_type=MESH)
    swaps = [swap(0, I["tokens"].at[1 - y_], B["x"].at[:, mine]), swap(1, I["gattn"], B["gains"].at[0, :, mine]), swap(2, I["cotangent"].at[1 - y_], B["g"].at[:, mine]), swap(3, I["gmlp"], B["gains"].at[1, :, mine])]
    swaps[0].start(); swaps[1].start(); swaps[3].start()
    ready(0); ready(1)
    gat.send_z(0)
    ready(2); ready(3)
    gat.send_z(1)
    ready(4); ready(5)
    gat.send_z(2)
    for c in loc: c.wait()
    swaps[0].wait_recv(); swaps[1].wait_recv(); swaps[3].wait_recv()
    B["keep"][...] = jax.nn.sigmoid(B["keep"][...])
    ga, gm, gs = B["gains"].at[0], B["gains"].at[1], B["gs"]
    norm_into(B["h"], B["x"], ga)
    puts = []
    def put(name, src=None):
        cp = pltpu.make_async_copy(B[name] if src is None else src, O[name], osem.at[len(puts)])
        cp.start(); puts.append(cp)
    kv, kvp, s = B["kv"], B["kvp"], B["s"]
    xcopy = pltpu.make_async_remote_copy(src_ref=B["x"], dst_ref=B["att"], send_sem=ksem.at[0], recv_sem=krem.at[0], device_id=dev(r + 1), device_id_type=MESH)
    @pl.when(r < nctx - 1)
    def _(): xcopy.start()
    put("x"); put("h"); put("gains"); put("keep")
    ready(6); ready(7)
    gat.send_z(3)
    gat.stage_y(0)
    ready(8); ready(9)
    gat.send_z(4)
    gat.stage_y(1); gat.stage_x(0)
    ready(10); ready(11)
    gat.send_z(5)
    @pl.when(r == 0)
    def _():
        s0copy.start()
        kvp[...] = jnp.zeros_like(kvp)
        s0copy.wait()
    @pl.when(r > 0)
    def _():
        xcopy.wait_recv()
        norm_into(B["zatt"], B["att"], ga)
    gat.stage_y(2); gat.stage_x(1)
    ready(12); ready(13)
    gat.send_z(6)
    gat.stage_k(0)
    gat.stage_y(3)
    ready(14); ready(15)
    gat.send_z_wide(7)
    loads = [pltpu.make_async_copy(G.at[w], WB.at[w], wsem.at[w]) for w in range(8)]
    gat.done(0)
    for w in (0, 1):
        place(w).wait()
        loads[w].start()
    for i in range(2):
        loads[i].wait()
        kv[i] = nn(B["h"][...], W(i)).astype(BF16)
    put("kv")
    gat.stage_x(2)
    @pl.when(r > 0)
    def _():
        for i in range(2): kvp[i] = nn(B["zatt"][...], W(i)).astype(BF16)
    put("kvp")
    gat.stage_y(4)
    gat.stage_k(1)
    swaps[2].start()
    gat.done(1)
    for w in (2, 3):
        place(w).wait()
        loads[w].start()
    scopy = [pltpu.make_async_remote_copy(src_ref=B["ssend"].at[:, pl.ds(i * half, half)], dst_ref=s.at[:, pl.ds(i * half, half)],
             send_sem=ssem.at[i], recv_sem=srem.at[i], device_id=dev(r + 1), device_id_type=MESH) for i in range(2)]
    def state_in():
        @pl.when(r > 0)
        def _():
            for cp in scopy: cp.wait_recv()
        norm_into(B["n"], s, gs)
    loads[2].wait(); loads[3].wait()
    def chain_step():
        state_in()
        B["sq"][...] = nn(B["n"][...], W(2)).astype(BF16)
        attend_heads(state_parts(kv), B["sq"], B["zatt"], B["lses"], rows, 1, 8)
        for i in range(2):
            cs = pl.ds(i * half, half)
            zz = nt(B["zatt"][...], WB[3].reshape(D, D)[i * half:(i + 1) * half])
            B["z"][:, cs] = zz.astype(BF16)
            kr = B["keep"][:, cs]
            B["ssend"][:, cs] = (kr * s[:, cs].astype(F32) + (1.0 - kr) * zz).astype(BF16)
            scopy[i].start()
    def slot(i, _):
        def when(k, body): pl.when(i == k)(body)
        def s1a(): gat.stage_y(6)
        when(1, s1a)
        def s2a():
            gat.stage_x(5)
            gat.done(3)
            for w in (6, 7):
                place(w).wait()
                loads[w].start()
        when(2, s2a)
        def s3a():
            gat.stage_y_wide(7)
            pass
        when(3, s3a)
        @pl.when((i == r) & (r < nctx - 1))
        def _(): chain_step()
        def s0b():
            gat.stage_y(5)
            gat.stage_x(3)
            gat.stage_k(2)
        when(0, s0b)
        def s1b():
            gat.done(2)
            for w in (4, 5):
                place(w).wait()
                loads[w].start()
            gat.stage_k(3)
            gat.stage_x(4)
            loads[4].wait()
            B["q"][...] = nn(B["h"][...], W(4)).astype(BF16)
        when(1, s1b)
        def s3b():
            @pl.when(r == nctx - 1)
            def _(): state_in()
            for j in range(2):
                loads[5 + j].wait()
                B["skv"][j] = nn(B["n"][...], W(5 + j)).astype(BF16)
        when(3, s3b)
        def s4():
            gat.stage_k(4)
            gat.stage_x(6)
        when(4, s4)
        def s6():
            gat.stage_k(5)
        when(6, s6)
        @pl.when(i >= 4)
        def _(): attend_heads(token_parts(kvp, kv, B["skv"], r == 0, rows, 2), B["q"], B["att"], B["lse"], rows, 2, 2, 2 * (i - 4), 2)
        return 0
    lax.fori_loop(0, 8, slot, 0)
    for name in ("s", "n", "sq", "zatt", "z", "lses", "q", "skv", "att", "lse"): put(name)
    loads[7].wait()
    B["y1"][...] = B["x"][...].astype(F32) + nt(B["att"][...], W(7))
    norm_into(B["m"], B["y1"], gm)
    swaps[2].wait_recv()
    m, g, a, du, u, da = B["m"], B["g"], B["a"], B["du"], B["u"], B["da"]
    def wl(j, i): return pltpu.make_async_copy(G.at[8 + 2 * j + i], WB.at[2 * lax.rem(j, 2) + i], wsem.at[2 * lax.rem(j, 2) + i])
    def dcopy(j, i): return pltpu.make_async_copy(WB.at[4 + 2 * lax.rem(j, 2) + i], O["Dc"].at[2 * j + i], dsem.at[2 * lax.rem(j, 2) + i])
    for w in range(8, 16): place(w).wait()
    gat.done(4)
    wl(0, 0).start(); wl(0, 1).start()
    B["oacc"][...] = jnp.zeros_like(B["oacc"])
    B["macc"][...] = jnp.zeros_like(B["macc"])
    def slice_step(j, _):
        b = 2 * lax.rem(j, 2)
        wl(j, 0).wait(); wl(j, 1).wait()
        a[...] = nn(m[...], W(b))
        du[...] = nn(g[...], W(b + 1))
        def body(rs):
            av = a[rs, :]
            sq = av * av
            t = jnp.tanh(G1 * av * (1.0 + G3 * sq))
            u[rs, :] = (0.5 * av * (1.0 + t)).astype(BF16)
            dg = 0.5 * (1.0 + t) + 0.5 * av * (1.0 - t * t) * (G1 * (1.0 + 3.0 * G3 * sq))
            da[rs, :] = (dg * du[rs, :]).astype(BF16)
        rows_loop(rows, 32, body)
        B["oacc"][...] += nt(u[...], W(b + 1))
        @pl.when(j == 0)
        def _(): gat.stage_x_wide(7)
        B["macc"][...] += nt(da[...], W(b))
        @pl.when(j >= 2)
        def _():
            dcopy(j - 2, 0).wait(); dcopy(j - 2, 1).wait()
        WB[4 + b] = tn(m[...], da[...]).astype(BF16).reshape(WB.shape[1:])
        dcopy(j, 0).start()
        @pl.when(j == 0)
        def _(): gat.stage_k(6)
        @pl.when(j < 3)
        def _():
            gat.done(5 + j)
            wl(j + 1, 0).start(); wl(j + 1, 1).start()
        WB[5 + b] = tn(g[...], u[...]).astype(BF16).reshape(WB.shape[1:])
        dcopy(j, 1).start()
        return 0
    lax.fori_loop(0, 4, slice_step, 0)
    B["gg"][...] = jnp.zeros_like(B["gg"])
    def last(rs):
        yv = B["y1"][rs, :]
        u[rs, :] = (yv + B["oacc"][rs, :]).astype(BF16)
        dv, dgain = norm_back_rows(yv, gm[...], B["macc"][rs, :])
        a[rs, :] = g[rs, :].astype(F32) + dv
        B["gg"][...] += fold8(dgain)
    rows_loop(rows, 32, last)
    put("out", u); put("gy1", a); put("gg")
    for j in (2, 3):
        for i in range(2): dcopy(j, i).wait()
    @pl.when(r < nctx - 1)
    def _():
        xcopy.wait_send()
        for cp in scopy: cp.wait_send()
    def drains(g_, _):
        gat.drain(g_)
        return 0
    lax.fori_loop(0, 7, drains, 0)
    gat.drain_wide(7)
    for sw in swaps: sw.wait_send()
    for cp in puts: cp.wait()

def forward_call(F, nctx, args):
    rows = args["tokens"].shape[1]
    blk = D // (4 * F)
    sh = lambda *s: jax.ShapeDtypeStruct(s, BF16)
    fl = lambda *s: jax.ShapeDtypeStruct(s, F32)
    R = sh(rows, D)
    R2 = sh(2, rows, D)
    L = fl(HEADS, 1, rows)
    mats = lambda n: sh(n, F, 2, 2, blk, D)
    shapes = dict(G=mats(16), Dc=mats(8), out=R, gg=fl(8, D), h=R, q=R, kv=R2, kvp=R2, skv=R2, n=R, s=R, sq=R, zatt=R, z=R, lse=L, lses=L, att=R, x=R, gy1=fl(rows, D), gains=fl(2, 1, D), keep=fl(1, D))
    bufs = dict(x=R, g=R, h=R, q=R, kv=R2, kvp=R2, skv=R2, n=R, s=R, ssend=R, sq=R, zatt=R, z=R, att=R, m=R, u=R, da=R,
        y1=fl(rows, D), a=fl(rows, D), du=fl(rows, D), oacc=fl(rows, D), macc=fl(rows, D), lse=L, lses=L, gains=fl(2, 1, D), gs=fl(1, D), gg=fl(8, D), keep=fl(1, D),
        tin=sh(6, D // 2, D // F), own=sh(16, 2, 2, blk, D // 2), WB=mats(8))
    S = pltpu.SemaphoreType.DMA
    n = 8
    outs = pl.pallas_call(functools.partial(forward_kernel, F, nctx),
        out_shape=[shapes[k] for k in A_OUT],
        in_specs=[ANY] * len(A_IN), out_specs=[ANY] * len(A_OUT),
        scratch_shapes=[pltpu.VMEM(bufs[k].shape, bufs[k].dtype) for k in A_BUF]
            + [S((n, F - 1)), S((n, F - 1)), S((n, F)), S((n, F)), S((n, F - 1)), S((n, F - 1)), S((n, F)), S((n, F))]
            + [S((16,)), S((13,)), S((len(A_OUT),)), S((8,)), S((2,)), S((2,)), S((2,)), S((2,)), S((4,)), S((4,)), S((4,))],
        compiler_params=pltpu.CompilerParams(collective_id=1, has_side_effects=True, vmem_limit_bytes=62 << 20), name="forward")(*[args[k] for k in A_IN])
    return dict(zip(A_OUT, outs))


B_IN = ("G", "Dc", "out", "gg", "gains", "gs", "keep", "h", "q", "kv", "kvp", "skv", "n", "s", "sq", "zatt", "z", "lse", "lses", "att", "x", "gy1")
B_OUT = ("R", "RX", "OUTF", "GXF", "S0", "SUMS", "DD", "KBH", "B1X", "B1Y", "B2H", "ZB0", "ZB1", "XBH")
B_BUF = ("h", "q", "kv", "kvp", "skv", "n", "s", "sq", "zatt", "z", "lse", "lses", "att", "gy1", "gg", "gains", "gs", "keep",
         "WB", "do", "datt", "dqb", "dkv", "dsend", "dret", "dskv", "dntok", "dsin", "dsout", "ggv",
         "A", "TK", "T1X", "T1Y", "T2", "TZ0", "TZ1", "TX", "lo", "hi", "hi2", "DS1", "dsp", "gin", "g1", "g2")
B_SEM = ("isem", "wsem", "dsem", "psem", "prem", "csem", "crem", "osem", "orem",
         "ks", "kr", "s1", "r1", "s2", "r2", "zs", "zr", "ws", "wr", "vs", "vr", "us", "ur", "bs", "br", "fs", "fr", "xs", "xr", "lsem", "dss", "dsr", "d2s", "d2r", "d3s", "d3r", "g1s", "g1r", "g2s", "g2r", "rsem")

def back_kernel(F, nctx, *refs):
    I = dict(zip(B_IN, refs)); at = len(B_IN)
    O = dict(zip(B_OUT, refs[at:])); at += len(B_OUT)
    B = dict(zip(B_BUF, refs[at:])); at += len(B_BUF)
    S = dict(zip(B_SEM, refs[at:]))
    z, x, k, y = where_am_i()
    c = x * 2 + k
    r = c
    rows = B["do"].shape[0]
    blk = D // (4 * F)
    half = D // 2
    mine, other = cols_of(y), cols_of(1 - y)
    xdev, ydev, kdev = (z, (1 - x) * 2 + k, y), (z, c, 1 - y), (z, x * 2 + 1 - k, y)
    dev = lambda cc: (z, cc, y)
    def local(src, dst, sem): return pltpu.make_async_copy(src, dst, sem)
    def remote(src, dst, s, rr, d):
        return pltpu.make_async_remote_copy(src_ref=src, dst_ref=dst, send_sem=s, recv_sem=rr, device_id=d, device_id_type=MESH)
    def to_z(d): return lax.rem(z - (d + 1) + F, F)
    def from_z(d): return lax.rem(z + d + 1, F)
    W4 = (0, 1, 2, 3)
    slots = {7: (0, 0), 5: (1, 1), 6: (2, 2), 3: (3, 3), 2: (4, 0), 4: (5, 1), 0: (6, 2), 1: (7, 3)}
    wload = {w: local(I["G"].at[w], B["WB"].at[sl], S["wsem"].at[i]) for w, (i, sl) in slots.items()}
    W = lambda w: B["WB"][slots[w][1]].reshape(D, D)
    order = ("gy1", "att", "q", "kv", "kvp", "skv", "lse", "gs", "n", "s", "h", "keep", "sq", "zatt", "z", "lses", "gains", "gg")
    loads = {}
    for i, name in enumerate(order):
        loads[name] = local(I[name], B[name], S["isem"].at[i])
    loads["gy1"].start()
    wload[7].start()
    for name in order[1:]: loads[name].start()
    for w in (5, 6, 3): wload[w].start()
    barrier_with(F, 7, True)
    def ksend_from(ref, p, first_row): return remote(ref.at[pl.ds(first_row, 2), :, :, 1 - k], O["KBH"].at[pl.ds(2 * p, 2)], S["ks"].at[p], S["kr"].at[p], kdev)
    for p in range(4): ksend_from(I["Dc"], p, 2 * p).start()
    oload = local(I["out"], B["dsout"], S["rsem"].at[0])
    oload.start()
    oswap = remote(B["dsout"].at[:, other], O["OUTF"].at[y], S["osem"].at[0], S["orem"].at[0], ydev)
    oown = local(B["dsout"].at[:, mine], O["OUTF"].at[y], S["rsem"].at[0])
    A = B["A"]
    def sl(p): return lax.rem(p, 4)
    def two(p): return lax.rem(p, 2)
    def first(p, e):
        a = A.at[sl(p), e]
        if e == 0: return remote(a.at[:, 1 - x], O["B1X"].at[p], S["s1"].at[p, 0], S["r1"].at[p, 0], xdev)
        return remote(a.at[:, :, :, other], O["B1Y"].at[p], S["s1"].at[p, 1], S["r1"].at[p, 1], ydev)
    def second(p): return remote(A.at[sl(p), 0, :, x, :, other], O["B2H"].at[p], S["s2"].at[p], S["r2"].at[p], ydev)
    def zsend(p, d): return remote(A.at[sl(p), 0, to_z(d), x, :, mine], O["ZB0"].at[p, d], S["zs"].at[p, d], S["zr"].at[p, d], (to_z(d), c, y))
    def zwide(p, d): return remote(A.at[sl(p), 1, to_z(d), :, :, mine], O["ZB1"].at[p, d], S["ws"].at[p, d], S["wr"].at[p, d], (to_z(d), c, y))
    def xswap(p): return remote(B["hi"].at[sl(p)], O["XBH"].at[p], S["vs"].at[p], S["vr"].at[p], xdev)
    def bcast(p, i): return remote(B["lo"].at[two(p)], O["R"].at[2 * p, x, k], S["bs"].at[p, i], S["br"].at[p, i], (kdev, xdev)[i])
    def wide(p): return remote(B["hi2"].at[two(p)], O["R"].at[2 * p + 1, :, k], S["us"].at[p], S["ur"].at[p], kdev)
    def fwd(p):
        rr = O["R"].at[2 * p, 1 - x, k]
        return remote(rr, rr, S["fs"].at[p], S["fr"].at[p], kdev)
    def extra(e, i):
        src = B["lo"].at[0] if e == 0 else B["hi2"].at[0, x]
        return remote(src, O["RX"].at[e, c], S["xs"].at[e, i], S["xr"].at[e, i], (z, lax.rem(c + i, 4), 1 - y))
    def landed(ref, sem): local(ref, ref, sem).wait()
    def plus(a, b): return a + b
    def own_load(p, do):
        @pl.when(p < 4)
        def _(): do(local(I["Dc"].at[pl.ds(2 * p, 2), :, :, k], A.at[sl(p)], S["lsem"].at[0]))
        @pl.when(p >= 4)
        def _(): do(local(O["DD"].at[pl.ds(jnp.maximum(2 * p - 8, 0), 2), :, :, k], A.at[sl(p)], S["lsem"].at[0]))
    def guard(p, body, least=0):
        if isinstance(p, int):
            if least <= p < 8: body()
        else:
            pl.when((p >= least) & (p < 8))(body)
    def sent(p):
        first(p, 0).wait_send()
        first(p, 1).wait_send()
        second(p).wait_send()
        xswap(p).wait_send()
        for d in range(F - 1):
            zsend(p, d).wait_send()
            zwide(p, d).wait_send()
    def sent_last(p):
        bcast(p, 0).wait_send()
        bcast(p, 1).wait_send()
        wide(p).wait_send()
    def lk(p): return local(O["KBH"].at[pl.ds(2 * p, 2)], B["TK"], S["lsem"].at[1])
    def l1x(p): return local(O["B1X"].at[p], B["T1X"], S["lsem"].at[2])
    def l1y(p): return local(O["B1Y"].at[p], B["T1Y"], S["lsem"].at[3])
    def l2(p): return local(O["B2H"].at[p], B["T2"], S["lsem"].at[4])
    def lz0(p): return local(O["ZB0"].at[p], B["TZ0"], S["lsem"].at[5])
    def lz1(p): return local(O["ZB1"].at[p], B["TZ1"], S["lsem"].at[6])
    def lx(p): return local(O["XBH"].at[p], B["TX"], S["lsem"].at[7])
    def rown0(p): return local(B["lo"].at[two(p)], O["R"].at[2 * p, x, k], S["lsem"].at[8])
    def rown1(p): return local(B["hi2"].at[two(p)], O["R"].at[2 * p + 1, :, k], S["lsem"].at[9])
    def pair_step(s):
        def k_in():
            guard(s - 4, lambda: sent(s - 4))
            landed(O["KBH"].at[pl.ds(2 * s, 2)], S["kr"].at[s])
            own_load(s, lambda cp: cp.start())
            lk(s).start()
        def s1_in():
            p = s - 1
            first(p, 0).wait_recv()
            l1x(p).start()
            first(p, 1).wait_recv()
            l1y(p).start()
        def s2_in():
            p = s - 2
            second(p).wait_recv()
            l2(p).start()
            for d in range(F - 1): zwide(p, d).wait_recv()
            lz1(p).start()
        def z_in():
            p = s - 3
            for d in range(F - 1): zsend(p, d).wait_recv()
            lz0(p).start()
            xswap(p).wait_recv()
            lx(p).start()
        def k_do():
            own_load(s, lambda cp: cp.wait())
            lk(s).wait()
            a, t = A.at[sl(s)], B["TK"]
            for e in range(2):
                def add(i, _):
                    zz, xx = lax.div(i, 2), lax.rem(i, 2)
                    a[e, zz, xx] = plus(a[e, zz, xx], t[e, zz, xx])
                    return 0
                lax.fori_loop(0, 2 * F, add, 0)
                first(s, e).start()
        def s1_do():
            p = s - 1
            a = A.at[sl(p)]
            l1x(p).wait()
            def add0(i, _):
                a[0, i, x] = plus(a[0, i, x], B["T1X"][i])
                return 0
            lax.fori_loop(0, F, add0, 0)
            second(p).start()
            l1y(p).wait()
            def add1(i, _):
                for xx in range(2): a[1, i, xx, :, mine] = plus(a[1, i, xx, :, mine], B["T1Y"][i, xx])
                return 0
            lax.fori_loop(0, F, add1, 0)
            for d in range(F - 1): zwide(p, d).start()
        def s2_do():
            p = s - 2
            a = A.at[sl(p)]
            l2(p).wait()
            def add(i, _):
                a[0, i, x, :, mine] = plus(a[0, i, x, :, mine], B["T2"][i])
                return 0
            lax.fori_loop(0, F, add, 0)
            for d in range(F - 1): zsend(p, d).start()
            lz1(p).wait()
            for xx in range(2):
                total = a[1, z, xx, :, mine].astype(F32)
                for d in range(F - 1): total = total + B["TZ1"][d, xx].astype(F32)
                B["hi"][sl(p), xx] = total.astype(BF16)
            xswap(p).start()
        def z_do():
            p = s - 3
            guard(p - 2, lambda: sent_last(p - 2))
            lz0(p).wait()
            total = A[sl(p), 0, z, x, :, mine].astype(F32)
            for d in range(F - 1): total = total + B["TZ0"][d].astype(F32)
            B["lo"][two(p)] = total.astype(BF16)
            for i in range(2): bcast(p, i).start()
            rown0(p).start()
            lx(p).wait()
            for xx in range(2): B["hi2"][two(p), xx] = plus(B["hi"][sl(p), xx], B["TX"][xx])
            wide(p).start()
            rown1(p).start()
            rown0(p).wait()
            rown1(p).wait()
            def special():
                for e in range(2):
                    for i in range(4): extra(e, i).start()
                for e in range(2):
                    for i in range(4): extra(e, i).wait_send()
            if isinstance(p, int):
                if p == 6: special()
            else: pl.when(p == 6)(special)
        def f_do():
            p = s - 4
            landed(O["R"].at[2 * p, 1 - x, k], S["br"].at[p, 1])
            fwd(p).start()
        guard(s, k_in)
        guard(s, k_do)
        guard(s - 1, s1_in)
        guard(s - 1, s1_do)
        guard(s - 2, s2_in)
        guard(s - 2, s2_do)
        guard(s - 3, z_in)
        guard(s - 3, z_do)
        guard(s - 4, f_do)
    ggv = B["ggv"]
    ggv[...] = jnp.zeros_like(ggv)
    loads["gy1"].wait()
    do, datt, dqb, dkv, dskv, dntok, dsin, dsout = (B[i] for i in ("do", "datt", "dqb", "dkv", "dskv", "dntok", "dsin", "dsout"))
    def cast(rs): do[rs, :] = B["gy1"][rs, :].astype(BF16)
    rows_loop(rows, 64, cast)
    wload[7].wait()
    datt[...] = nn(do[...], W(7)).astype(BF16)
    wload[2].start()
    oload.wait()
    oswap.start(); oown.start()
    for name in order[1:7]: loads[name].wait()
    hz = F // 2
    def pair_view(ref):
        return lambda i, cs: ref[i * hz:(i + 1) * hz, :, :, :, cs].reshape(rows, HEAD)
    kvp_at, skv_at = pair_view(B["kvp"]), pair_view(B["skv"])
    def parts_of(cs, qc):
        upto = (qc + 1) * (rows // 2)
        return [(lambda: kvp_at(0, cs), lambda: kvp_at(1, cs), lambda s: jnp.where(r == 0, NEG, s)),
                (lambda: B["kv"][0, pl.ds(0, upto), cs], lambda: B["kv"][1, pl.ds(0, upto), cs], lambda s: causal_scores(s, 0, qc * (rows // 2))),
                (lambda: skv_at(0, cs), lambda: skv_at(1, cs), lambda s: s)]
    def sink(i, cs, dk, dv):
        dst = (B["dsend"], dkv, dskv)[i]
        dst[0, :, cs] = dk.astype(dst.dtype)
        dst[1, :, cs] = dv.astype(dst.dtype)
    def halves(i, _):
        pair_step(i)
        attend_heads_back(parts_of, B["q"], datt, B["lse"], dqb, sink, rows, 2, 1, i * (HEADS // 2), HEADS // 2)
        return 0
    lax.fori_loop(0, 2, halves, 0)
    pcopy = remote(B["dsend"], B["dret"], S["psem"].at[0], S["prem"].at[0], dev(r - 1))
    @pl.when(r > 0)
    def _(): pcopy.start()
    wload[5].wait(); wload[6].wait()
    dntok[...] = nt(dskv[0], W(5)) + nt(dskv[1], W(6))
    wload[4].start(); wload[0].start()
    for name in order[7:11]: loads[name].wait()
    oswap.wait_send(); oown.wait()
    hr = rows // 2
    ccopy = [remote(dsout.at[pl.ds(i * hr, hr)], dsin.at[pl.ds(i * hr, hr)], S["csem"].at[i], S["crem"].at[i], dev(r - 1)) for i in range(2)]
    def finish_state(more):
        for i in range(2):
            def body(j, _):
                rs = pl.ds(pl.multiple_of(i * hr + j * 32, 32), 32)
                dv, dgain = norm_back_rows(B["s"][rs, :].astype(F32), B["gs"][...], dntok[rs, :])
                if more: dv = dv + B["keep"][...] * dsin[rs, :].astype(F32)
                dsout[rs, :] = dv.astype(BF16)
                ggv[pl.ds(8, 8), :] += fold8(dgain)
                return 0
            lax.fori_loop(0, hr // 32, body, 0)
            @pl.when(r > 0)
            def _(): ccopy[i].start()
    @pl.when(r == nctx - 1)
    def _(): finish_state(False)
    stages = (B["kvp"], B["skv"])
    def grad_out(i, left, right):
        if i >= 2: pass
        st = stages[i % 2]
        st[...] = tn(left[...], right[...]).astype(BF16).reshape(st.shape)
        local(st, O["DD"].at[i], S["dsem"].at[i]).start()
        if i % 2 == 1:
            for q in (i - 1, i): local(stages[q % 2], O["DD"].at[q], S["dsem"].at[q]).wait()
            ksend_from(O["DD"], 4 + i // 2, i - 1).start()
    grad_out(0, do, B["att"])
    xload = local(I["x"], B["att"], S["rsem"].at[2])
    xload.start()
    grad_out(1, B["n"], dskv.at[0])
    pair_step(2)
    grad_out(2, B["n"], dskv.at[1])
    grad_out(3, B["h"], dqb)
    for name in order[11:]: loads[name].wait()
    wload[3].wait(); wload[2].wait()
    dzb = datt
    def turn(t, _):
        @pl.when(r == nctx - 2 - t)
        def _():
            for cp in ccopy: cp.wait_recv()
            def body(rs):
                d = dsin[rs, :].astype(F32)
                kr = B["keep"][...]
                dzb[rs, :] = ((1.0 - kr) * d).astype(BF16)
                ggv[pl.ds(16, 8), :] += fold8(d * (B["s"][rs, :].astype(F32) - B["z"][rs, :].astype(F32)) * kr * (1.0 - kr))
            rows_loop(rows, 32, body)
            do[...] = nn(dzb[...], W(3)).astype(BF16)
            def sink2(i, cs, dk, dv):
                dkv[0, :, cs] += dk
                dkv[1, :, cs] += dv
            attend_heads_back(state_parts(B["kv"]), B["sq"], do, B["lses"], B["q"], sink2, rows, 1, 4, 0, HEADS)
            dntok[...] += nt(B["q"][...], W(2))
            finish_state(True)
        @pl.when(t < nctx - 2)
        def _(): pair_step(3 + t)
        return 0
    lax.fori_loop(0, nctx - 1, turn, 0)
    n2 = 2 * F
    prow = rows // n2
    me = z * 2 + y
    def zy(i):
        q = lax.rem(me + i + 1, n2)
        return q, (lax.div(q, 2), 0, lax.rem(q, 2))
    def back_of(i): return lax.rem(me - (i + 1) + n2, n2)
    def d1(i):
        q, d = zy(i)
        return remote(dsout.at[pl.ds(pl.multiple_of(q * prow, prow), prow)], B["DS1"].at[me], S["dss"].at[i], S["dsr"].at[i], d)
    def d2(i):
        q, d = zy(i)
        return remote(B["dsp"], O["S0"].at[me], S["d2s"].at[i], S["d2r"].at[i], d)
    def d3(i, d): return remote(O["S0"], O["S0"], S["d3s"].at[i], S["d3r"].at[0], d)
    dsown = local(B["dsp"], O["S0"].at[me], S["rsem"].at[3])
    @pl.when(r == 0)
    def _():
        for i in range(n2 - 1): d1(i).start()
    @pl.when(r == nctx - 1)
    def _():
        B["q"][...] = jnp.zeros_like(B["q"])
        dzb[...] = jnp.zeros_like(dzb)
        B["zatt"][...] = jnp.zeros_like(B["zatt"])
    grad_out(4, B["n"], B["q"])
    grad_out(5, dzb, B["zatt"])
    @pl.when(r < nctx - 1)
    def _(): pcopy.wait_recv()
    @pl.when(r == nctx - 1)
    def _(): B["dret"][...] = jnp.zeros_like(B["dret"])
    wload[1].start()
    for i in range(2):
        def add(rs): dskv[i, rs, :] = (dkv[i, rs, :] + B["dret"][i, rs, :].astype(F32)).astype(BF16)
        rows_loop(rows, 32, add)
    grad_out(6, B["h"], dskv.at[0])
    grad_out(7, B["h"], dskv.at[1])
    pair_step(5)
    wload[4].wait(); wload[0].wait(); wload[1].wait()
    xload.wait()
    dntok[...] = nt(dqb[...], W(4)) + nt(dskv[0], W(0)) + nt(dskv[1], W(1))
    gxb = B["att"]
    def last(rs):
        dv, dgain = norm_back_rows(gxb[rs, :].astype(F32), B["gains"][0], dntok[rs, :])
        ggv[pl.ds(0, 8), :] += fold8(dgain)
        gxb[rs, :] = (B["gy1"][rs, :] + dv).astype(BF16)
    rows_loop(rows, 32, last)
    gswap = remote(gxb.at[:, other], O["GXF"].at[y], S["osem"].at[1], S["orem"].at[1], ydev)
    gown = local(gxb.at[:, mine], O["GXF"].at[y], S["rsem"].at[1])
    gswap.start(); gown.start()
    gin = B["gin"]
    gin[...] = jnp.zeros_like(gin)
    for i in range(3): gin[pl.ds(i, 1), :] = jnp.sum(ggv[pl.ds(8 * i, 8), :], axis=0, keepdims=True)
    gin[pl.ds(3, 1), :] = jnp.sum(B["gg"][...], axis=0, keepdims=True)
    around = ((0, 0, 1), (0, 1, 0), (0, 1, 1), (1, 0, 0), (1, 0, 1), (1, 1, 0), (1, 1, 1))
    def plane(i):
        dx, dk, dy = around[i]
        return lax.rem(x + dx, 2), lax.rem(k + dk, 2), lax.rem(y + dy, 2)
    spot = c * 2 + y
    def g1copy(i):
        px, pk, py = plane(i)
        return remote(gin, B["g1"].at[spot], S["g1s"].at[i], S["g1r"].at[i], (z, px * 2 + pk, py))
    def g2copy(d): return remote(gin, B["g2"].at[z], S["g2s"].at[d], S["g2r"].at[d], (to_z(d), c, y))
    B["g1"][spot] = gin[...]
    for i in range(7): g1copy(i).start()
    def tail(i, _):
        s = 6 + i
        @pl.when(i == 1)
        def _():
            for j in range(7):
                g1copy(j).wait_send()
                px, pk, py = plane(j)
                landed(B["g1"].at[(px * 2 + pk) * 2 + py], S["g1r"].at[j])
            total = B["g1"][0]
            for j in range(1, 8): total = total + B["g1"][j]
            gin[...] = total
            B["g2"][z] = total
            for d in range(F - 1): g2copy(d).start()
        @pl.when((i == 1) & (r == 0))
        def _():
            B["DS1"][me] = dsout[pl.ds(pl.multiple_of(me * prow, prow), prow), :]
            for j in range(n2 - 1): landed(B["DS1"].at[back_of(j)], S["dsr"].at[j])
            total = B["DS1"][0].astype(F32)
            for j in range(1, n2): total = total + B["DS1"][j].astype(F32)
            B["dsp"][...] = total.astype(BF16)
            dsown.start()
            for j in range(n2 - 1): d2(j).start()
        @pl.when((i == 2) & (r == 0))
        def _():
            for j in range(n2 - 1): landed(O["S0"].at[back_of(j)], S["d2r"].at[j])
            dsown.wait()
            d3(0, dev(1)).start()
            d3(1, dev(2)).start()
        @pl.when((i == 3) & (r == 2))
        def _():
            landed(O["S0"], S["d3r"].at[0])
            d3(0, dev(3)).start()
        @pl.when(i == 3)
        def _():
            for d in range(F - 1):
                g2copy(d).wait_send()
                landed(B["g2"].at[from_z(d)], S["g2r"].at[d])
            total = B["g2"][0]
            for d in range(1, F): total = total + B["g2"][d]
            gin[...] = total
            local(gin, O["SUMS"], S["rsem"].at[4]).start()
        pair_step(s)
        return 0
    lax.fori_loop(0, 6, tail, 0)
    local(gin, O["SUMS"], S["rsem"].at[4]).wait()
    for p in range(4, 8): sent(p)
    for p in (6, 7): sent_last(p)
    def ends(p, _):
        ksend_from(O["DD"], p, 0).wait_send()
        fwd(p).wait_send()
        landed(O["R"].at[2 * p, x, 1 - k], S["br"].at[p, 0])
        landed(O["R"].at[2 * p, 1 - x, 1 - k], S["fr"].at[p])
        landed(O["R"].at[2 * p + 1, :, 1 - k], S["ur"].at[p])
        return 0
    lax.fori_loop(0, 8, ends, 0)
    for e in range(2):
        for i in range(4): landed(O["RX"].at[e, lax.rem(c - i + 4, 4)], S["xr"].at[e, i])
    @pl.when(r == 0)
    def _():
        for j in range(n2 - 1):
            d1(j).wait_send()
            d2(j).wait_send()
        d3(0, dev(1)).wait_send()
        d3(1, dev(2)).wait_send()
    @pl.when(r == 2)
    def _(): d3(0, dev(3)).wait_send()
    @pl.when((r == 1) | (r == 3))
    def _(): landed(O["S0"], S["d3r"].at[0])
    @pl.when(r > 0)
    def _():
        pcopy.wait_send()
        for cp in ccopy: cp.wait_send()
    oswap.wait_recv(); gswap.wait(); gown.wait()

def back_call(F, nctx, vals, gs):
    rows = vals["h"].shape[0]
    blk = D // (4 * F)
    half = D // 2
    sh = lambda *s: jax.ShapeDtypeStruct(s, BF16)
    fl = lambda *s: jax.ShapeDtypeStruct(s, F32)
    mats = lambda n: sh(n, F, 2, 2, blk, D)
    R, R2, L = sh(rows, D), sh(2, rows, D), fl(HEADS, 1, rows)
    prow = rows // (2 * F)
    shapes = dict(R=sh(16, 2, 2, blk, half), RX=sh(2, 4, blk, half), OUTF=sh(2, rows, half), GXF=sh(2, rows, half), S0=sh(2 * F, prow, D), SUMS=fl(8, D),
        DD=mats(8), KBH=sh(16, F, 2, blk, D), B1X=sh(8, F, blk, D), B1Y=sh(8, F, 2, blk, half), B2H=sh(8, F, blk, half),
        ZB0=sh(8, F - 1, blk, half), ZB1=sh(8, F - 1, 2, blk, half), XBH=sh(8, 2, blk, half))
    one = sh(F, 2, 2, blk, D)
    bufs = dict(h=R, q=R, kv=R2, kvp=one, skv=one, n=R, s=R, sq=R, zatt=R, z=R, lse=L, lses=L, att=R, gy1=fl(rows, D), gg=fl(8, D), gains=fl(2, 1, D), gs=fl(1, D), keep=fl(1, D),
        WB=mats(4), do=R, datt=R, dqb=R, dkv=fl(2, rows, D), dsend=R2, dret=R2, dskv=R2, dntok=fl(rows, D), dsin=R, dsout=R, ggv=fl(24, D),
        A=sh(4, 2, F, 2, blk, D), TK=sh(2, F, 2, blk, D), T1X=sh(F, blk, D), T1Y=sh(F, 2, blk, half), T2=sh(F, blk, half), TZ0=sh(F - 1, blk, half), TZ1=sh(F - 1, 2, blk, half), TX=sh(2, blk, half),
        lo=sh(2, blk, half), hi=sh(4, 2, blk, half), hi2=sh(2, 2, blk, half), DS1=sh(2 * F, prow, D), dsp=sh(prow, D), gin=fl(8, D), g1=fl(8, 8, D), g2=fl(F, 8, D))
    X = pltpu.SemaphoreType.DMA
    sems = dict(isem=(18,), wsem=(8,), dsem=(8,), psem=(1,), prem=(1,), csem=(2,), crem=(2,), osem=(2,), orem=(2,),
        ks=(8,), kr=(8,), s1=(8, 2), r1=(8, 2), s2=(8,), r2=(8,), zs=(8, F - 1), zr=(8, F - 1), ws=(8, F - 1), wr=(8, F - 1), vs=(8,), vr=(8,), us=(8,), ur=(8,), bs=(8, 2), br=(8, 2), fs=(8,), fr=(8,), xs=(2, 4), xr=(2, 4), lsem=(10,),
        dss=(2 * F,), dsr=(2 * F,), d2s=(2 * F,), d2r=(2 * F,), d3s=(2,), d3r=(1,), g1s=(7,), g1r=(7,), g2s=(F - 1,), g2r=(F - 1,), rsem=(5,))
    args = dict(vals)
    args["gs"] = gs
    args["kvp"], args["skv"] = (args[i].reshape(one.shape) for i in ("kvp", "skv"))
    outs = pl.pallas_call(functools.partial(back_kernel, F, nctx),
        out_shape=[shapes[i] for i in B_OUT], in_specs=[ANY] * len(B_IN), out_specs=[ANY] * len(B_OUT),
        scratch_shapes=[pltpu.VMEM(bufs[i].shape, bufs[i].dtype) for i in B_BUF] + [X(sems[i]) for i in B_SEM],
        compiler_params=pltpu.CompilerParams(collective_id=2, has_side_effects=True, vmem_limit_bytes=63 << 20), name="backward")(*[args[i] for i in B_IN])
    return dict(zip(B_OUT, outs))


def local(
    tokens,
    cotangent,
    w_query,
    w_key,
    w_value,
    w_out,
    w_state_key,
    w_state_value,
    w_state_query,
    w_state_out,
    w_up,
    w_down,
    gain_attn,
    gain_state,
    gain_mlp,
    forget_logit,
    state_init,
):
    fsdp = lax.axis_size("fsdp")
    tp_rank = lax.axis_index("tp")
    ctx_count = lax.axis_size("ctx")
    half = D // 2
    rows = D // fsdp
    blk = rows // 4
    tiles = lambda w: w.reshape(2, 2, blk, w.shape[1])
    args = dict(
        tokens=tokens, cotangent=cotangent, gattn=gain_attn[None], gmlp=gain_mlp[None],
        gstate=gain_state[None], keep=forget_logit[None], s0=state_init,
        key=tiles(w_key), value=tiles(w_value), squery=tiles(w_state_query), sout=w_state_out, query=tiles(w_query),
        skey=tiles(w_state_key), svalue=tiles(w_state_value), out=w_out, up=tiles(w_up), down=w_down)
    vals = forward_call(fsdp, ctx_count, args)
    got = back_call(fsdp, ctx_count, vals, args["gstate"])
    full = got["R"].reshape(16, rows, half)
    r = {w: full[8 + i] for i, w in enumerate((7, 5, 6, 4, 2, 3, 0, 1))}
    rx = got["RX"].reshape(2, rows, half)
    small = got["SUMS"]

    def both(mine, other):
        first = jnp.where(tp_rank == 0, mine, other)
        second = jnp.where(tp_rank == 0, other, mine)
        return jnp.concatenate([first, second], axis=1)

    at = lambda i: lax.dynamic_slice_in_dim(small[i], tp_rank * half, half, 0)
    return (
        got["OUTF"],
        got["GXF"],
        r[4].astype(F32),
        r[0].astype(F32),
        r[1].astype(F32),
        r[7].T.astype(F32),
        r[5].astype(F32),
        r[6].astype(F32),
        both(r[2], rx[0]).astype(F32),
        both(r[3], rx[1]).T.astype(F32),
        full[0:8:2].swapaxes(0, 1).reshape(rows, -1).astype(F32),
        full[1:8:2].swapaxes(1, 2).reshape(-1, rows).astype(F32),
        at(0),
        small[1],
        at(3),
        small[2],
        got["S0"].reshape(state_init.shape).astype(F32),
    )


def solution(mesh):
    placed = (
        P("fsdp", "ctx", "tp"),
        P("fsdp", "ctx", "tp"),
        P("fsdp", "tp"),
        P("fsdp", "tp"),
        P("fsdp", "tp"),
        P("tp", "fsdp"),
        P("fsdp", "tp"),
        P("fsdp", "tp"),
        P("fsdp", None),
        P(None, "fsdp"),
        P("fsdp", "tp"),
        P("tp", "fsdp"),
        P("tp"),
        P(),
        P("tp"),
        P(),
        P(),
    )
    return jax.shard_map(
        local,
        mesh=mesh,
        in_specs=placed,
        out_specs=(
            P("fsdp", "ctx", "tp"),
            P("fsdp", "ctx", "tp"),
            P("fsdp", "tp"),
            P("fsdp", "tp"),
            P("fsdp", "tp"),
            P("tp", "fsdp"),
            P("fsdp", "tp"),
            P("fsdp", "tp"),
            P("fsdp", None),
            P(None, "fsdp"),
            P("fsdp", "tp"),
            P("tp", "fsdp"),
            P("tp"),
            P(),
            P("tp"),
            P(),
            P(),
        ),
        check_vma=False,
    )
```
